256 devices in a mesh: ent: 64 (over x, z, core), rel: 4 (over y).
Axes of the slice: x: 4, y: 4, z: 8, core: 2. Of those that a mesh axis runs over, the one named last changes fastest.
Arguments:
- state_zero: bfloat16 [65536, 256], P('ent'), may hold values from -6 to 6
- state_one: bfloat16 [65536, 256], P('ent'), may hold values from -6 to 6
- aggregate_one: bfloat16 [65536, 256], P('ent'), may hold values from -6 to 6
- aggregate_two: bfloat16 [65536, 256], P('ent'), may hold values from -6 to 6
- cotangent: bfloat16 [65536, 256], P('ent'), may hold values from -6 to 6
- relation_table: bfloat16 [1312, 256], P('rel'), may hold values from -6 to 6
- update_in: bfloat16 [2, 64, 256], replicated, may hold values from -0.75 to 0.75
- update_bias: float32 [2, 256], replicated, may hold values from -3 to 3
- update_out: bfloat16 [2, 256, 32], replicated, may hold values from -0.375 to 0.375
- frontier_tiles: int32 [2, 128], P(None, 'ent'), may hold values from 0 to 7, as said below
- frontier_count: int32 [2, 64], P(None, 'ent'), may hold values from 1 to 2, as said below
- edge_source: int32 [262144], P(('ent', 'rel')), may hold values from 0 to 1023
- edge_relation: int32 [262144], P(('ent', 'rel')), may hold values from 0 to 327
- edge_target: int32 [262144], P(('ent', 'rel')), may hold values from 0 to 1023
- edge_owner: int32 [262144, 1], P(('ent', 'rel')), may hold values from 0 to 63; in each aligned block of 1024 rows (0 to 1023, 1024 to 2047, ...) at most 24 rows name the same one
Outputs:
- grad_state_zero: bfloat16 [65536, 256], P(('ent', 'rel'))
- grad_relation: float32 [1312, 256], P('rel')
- grad_update_in: float32 [2, 64, 256], replicated
- grad_update_bias: float32 [2, 256], replicated
- grad_update_out: float32 [2, 256, 32], replicated
The draws below stay inside these ranges and needn't reach their ends.
Inputs may be any that keep to these rules, and one draw needn't show every extreme that they name: `frontier_tiles`: within one owner's 2 slots of a hop the tile numbers are distinct, padded slots included. The first frontier_count entries of an owner's list are its live tiles; in each hop some owner has all 2 live. `edge_owner`: among the 1024 edges of one device at most 24 name the same owner, and in some device some owner is named by exactly 24.
All inputs are finite; a program needn't handle non-finite values.
Results may differ from the reference program's by a relative error of at most 0.009.
Values may be sent and summed in bfloat16 or wider, within the bound.
No kernel may reach another device: no remote copies, remote signals or barrier semaphores. Data moves between devices by JAX's collectives and lax.ppermute only.
A program may use at most 64 MiB of HBM per device.

```python
import math
import jax
import jax.numpy as jnp
import numpy as np
from jax import lax

QUERIES = 8
DIM = 32
FEAT = 256
WIDE = 256
REL_GROUP = 328
RELATIONS = 1312
TILE = 128
ENT_DEV = 1024
TILES = 8
SLOTS = 2
ENTITIES = 65536
EDGES_DEV = 1024
CAP = 24
EDGES = 262144
N_ENT = 64
N_REL = 4


def draw_frontier_tiles(key, part):

    def pick_tiles(sub_key):
        return jax.random.permutation(sub_key, TILES)[:SLOTS]
    key_list = jax.random.split(jax.random.fold_in(key, 11), 2 * N_ENT)
    return jax.vmap(pick_tiles)(key_list).reshape(2, N_ENT * SLOTS).astype(jnp.int32)


def draw_frontier_count(key, part):
    drawn_counts = jax.random.randint(jax.random.fold_in(key, 23), (2, N_ENT), 1, SLOTS + 1)
    chosen = jax.random.randint(jax.random.fold_in(key, 29), (2, 1), 0, N_ENT)
    filled = jnp.arange(N_ENT, dtype=jnp.int32)[None, :] == chosen
    return jnp.where(filled, SLOTS, drawn_counts).astype(jnp.int32)


def set_ends(result, stream_key, smallest, high):
    index_at = [jax.random.randint(jax.random.fold_in(stream_key, axis), (), 0, length) for axis, length in enumerate(result.shape)]
    longest = result.shape.index(max(result.shape))
    next_to = index_at[:longest] + [(index_at[longest] + 1) % result.shape[longest]] + index_at[longest + 1:]
    return result.at[tuple(index_at)].set(smallest).at[tuple(next_to)].set(high)


def block_scale(own_key, dims, cuts, smallest, high):
    loudness = 1.0
    for dim, blocks in cuts:
        heights = jax.random.uniform(jax.random.fold_in(jax.random.fold_in(own_key, 6), dim), (blocks,), jnp.float32, smallest / len(cuts), high / len(cuts))
        loudness = loudness * jnp.repeat(jnp.exp(heights), dims[dim] // blocks).reshape((-1,) + (1,) * (len(dims) - 1 - dim))
    return loudness


def shared_out(own_key, own, number, rows, count, top, most, skew):
    order = jax.random.permutation(own_key, count)
    packed, usual = portions_of(count, rows * top, most, skew, True), portions_of(count, rows * top, most, skew, False)
    places = jnp.arange(count)

    def named(tallies, turn):
        used = int((tallies > 0).sum())
        fixed = max(1, used // 4)
        shifted = fixed + (places - fixed + turn * (used - fixed)) % max(1, count - fixed)
        return jnp.zeros((count,), jnp.int32).at[order[jnp.where(places < fixed, places, shifted)]].set(jnp.asarray(tallies, jnp.int32))

    tallies = jnp.where(number % 4 == 0, named(packed, number // 4), named(usual, number - number // 4 - 1))
    mixed = jax.random.permutation(jax.random.fold_in(own, 3), count)
    donor, sink = mixed[0:count // 2 * 2:2], mixed[1:count // 2 * 2:2]
    margin = jnp.minimum(tallies[donor] - 1, most - tallies[sink]) // 2
    margin = jnp.where((donor == order[0]) | (sink == order[0]) | (tallies[sink] == 0), 0, jnp.maximum(margin, 0))
    shifted = jax.random.randint(jax.random.fold_in(own, 4), (count // 2,), 0, 1 << 20) % (margin + 1)
    tallies = tallies.at[donor].add(-shifted).at[sink].add(shifted)
    members = jnp.searchsorted(jnp.cumsum(tallies), jnp.arange(rows * top), side="right").astype(jnp.int32)
    grid = members.reshape(top, rows).T
    grid = grid[jax.random.permutation(jax.random.fold_in(own, 1), rows)]
    turn = jax.random.randint(jax.random.fold_in(own, 2), (rows, 1), 0, top)
    return jnp.take_along_axis(grid, (jnp.arange(top)[None, :] + turn) % top, axis=1)


def portions_of(count, total, reach, skew, full):
    loads = [(1 << 20) // math.isqrt(grade ** skew) + 1 for grade in range(1, count + 1)]
    largest = reach if full else min(reach, max(-(-total // count), total * loads[0] // sum(loads)))
    least = 1 if total - largest >= count - 1 else 0
    holding, surplus = [largest] + [least] * (count - 1), total - largest - least * (count - 1)
    while surplus > 0:
        free = [i for i in range(1, count) if holding[i] < largest] or [i for i in range(1, count) if holding[i] < reach]
        mass, budget = sum([loads[i] for i in free]), surplus
        for i in free:
            more = min(reach - holding[i], max(1, budget * loads[i] // mass), surplus)
            holding[i] = holding[i] + more
            surplus = surplus - more
    return np.array(holding)


def scatter_about(key, extent, spread, reach, cuts=(), kind=jnp.bfloat16):
    loudness = block_scale(key, extent, cuts, -0.22, 0.18) if cuts else 1.0
    drawn = jax.random.normal(key, extent, jnp.float32) * spread * loudness
    return jnp.minimum(jnp.maximum(drawn, -reach), reach).astype(kind)


def setup_inputs(seed: int = 0) -> dict:
    streams_of = jax.random.split(jax.random.key(seed), 16)
    state_zero = scatter_about(streams_of[0], (ENTITIES, FEAT), 1.0, 6.0, ((0, 64),))
    state_one = scatter_about(streams_of[1], (ENTITIES, FEAT), 1.0, 6.0, ((0, 64),))
    aggregate_one = scatter_about(streams_of[2], (ENTITIES, FEAT), 1.0, 6.0, ((0, 64),))
    aggregate_two = scatter_about(streams_of[3], (ENTITIES, FEAT), 1.0, 6.0, ((0, 64),))
    cotangent = scatter_about(streams_of[4], (ENTITIES, FEAT), 1.0, 6.0, ((0, 64),))
    relation_table = scatter_about(streams_of[5], (RELATIONS, FEAT), 1.0, 6.0, ((0, 4),))
    update_in = scatter_about(streams_of[6], (2, 2 * DIM, WIDE), (2 * DIM) ** -0.5, 0.75)
    update_bias = scatter_about(streams_of[7], (2, WIDE), 0.5, 3.0, (), jnp.float32)
    update_out = scatter_about(streams_of[8], (2, WIDE, DIM), WIDE ** -0.5, 0.375)
    frontier_tiles = draw_frontier_tiles(jax.random.fold_in(streams_of[15], 71), 0)
    frontier_count = draw_frontier_count(jax.random.fold_in(streams_of[15], 71), 0)
    edge_source = set_ends(jax.random.randint(streams_of[11], (EDGES,), 0, ENT_DEV), jax.random.fold_in(streams_of[11], 1), 0, ENT_DEV - 1).astype(jnp.int32)
    edge_relation = set_ends(jax.random.randint(streams_of[12], (EDGES,), 0, REL_GROUP), jax.random.fold_in(streams_of[12], 1), 0, REL_GROUP - 1).astype(jnp.int32)
    edge_target = set_ends(jax.random.randint(streams_of[13], (EDGES,), 0, ENT_DEV), jax.random.fold_in(streams_of[13], 1), 0, ENT_DEV - 1).astype(jnp.int32)
    edge_owner_keys = jax.random.split(jax.random.fold_in(streams_of[14], 1), EDGES // EDGES_DEV)
    edge_owner_turns = jax.random.permutation(jax.random.fold_in(streams_of[14], 3), EDGES // EDGES_DEV)
    edge_owner = jax.vmap(lambda own, number: shared_out(jax.random.fold_in(streams_of[14], 2), own, number, EDGES_DEV, N_ENT, 1, CAP, 2))(edge_owner_keys, edge_owner_turns).reshape((EDGES, 1))
    return {"state_zero": state_zero, "state_one": state_one, "aggregate_one": aggregate_one, "aggregate_two": aggregate_two, "cotangent": cotangent, "relation_table": relation_table, "update_in": update_in, "update_bias": update_bias, "update_out": update_out, "frontier_tiles": frontier_tiles, "frontier_count": frontier_count, "edge_source": edge_source, "edge_relation": edge_relation, "edge_target": edge_target, "edge_owner": edge_owner}


def round_trip(values):
    return lax.optimization_barrier(values.astype(jnp.bfloat16)).astype(jnp.float32)

def frontier_rows(tile_ids, live_count):
    slot_valid = jnp.arange(SLOTS, dtype=jnp.int32) < live_count
    tile_range = jnp.arange(TILES, dtype=jnp.int32)
    matched = (tile_ids[None, :] == tile_range[:, None]) & slot_valid[None, :]
    return jnp.repeat(jnp.any(matched, axis=1).astype(jnp.float32), TILE)

def update_backward(aggregate, state, upstream, update_in, update_bias, update_out):
    row_count = aggregate.shape[0]
    inputs = jnp.concatenate([aggregate.reshape(row_count, QUERIES, DIM), state.reshape(row_count, QUERIES, DIM)], axis=2).astype(jnp.float32)
    weight_first = update_in.astype(jnp.float32)
    weight_second = update_out.astype(jnp.float32)
    pre_act = jnp.einsum('nqd,de->nqe', inputs, weight_first) + update_bias
    gate_value = jax.nn.sigmoid(pre_act)
    activated = round_trip(pre_act * gate_value)
    slope = gate_value * (1.0 + pre_act * (1.0 - gate_value))
    upstream_low = round_trip(upstream).reshape(row_count, QUERIES, DIM)
    grad_act = jnp.einsum('nqd,ed->nqe', upstream_low, weight_second)
    grad_pre = grad_act * slope
    grad_pre_low = round_trip(grad_pre)
    grad_out = jnp.einsum('nqe,nqd->ed', activated, upstream_low)
    grad_bias = lax.optimization_barrier(jnp.sum(grad_pre, axis=(0, 1)))
    grad_in = jnp.einsum('nqd,nqe->de', inputs, grad_pre_low)
    grad_inputs = jnp.einsum('nqe,de->nqd', grad_pre_low, weight_first)
    grad_agg = grad_inputs[:, :, :DIM].reshape(row_count, FEAT).astype(jnp.bfloat16)
    grad_state = grad_inputs[:, :, DIM:].reshape(row_count, FEAT)
    return (grad_agg, grad_state, grad_in, grad_bias, grad_out)

def mlp_pass(aggregate, state, upstream, update_in, update_bias, update_out):

    def step(carry, block_index):
        start_row = block_index * ENT_DEV
        pieces = [lax.dynamic_slice_in_dim(source_array, start_row, ENT_DEV, 0) for source_array in (aggregate, state, upstream)]
        grad_agg, grad_state, grad_in, grad_bias, grad_out = update_backward(pieces[0], pieces[1], pieces[2], update_in, update_bias, update_out)
        return ((carry[0] + grad_in, carry[1] + grad_bias, carry[2] + grad_out), (grad_agg, grad_state))
    initial = (jnp.zeros((2 * DIM, WIDE), jnp.float32), jnp.zeros((WIDE,), jnp.float32), jnp.zeros((WIDE, DIM), jnp.float32))
    sums, (grad_agg, grad_state) = lax.scan(step, initial, jnp.arange(N_ENT, dtype=jnp.int32))
    return (grad_agg.reshape(ENTITIES, FEAT), grad_state.reshape(ENTITIES, FEAT), sums)

def edge_pass(grad_agg, state, relation_table, tile_lists, live_counts, edge_source, edge_relation, edge_target, edge_owner):

    def step(carry, block_index):
        tile_ids = lax.dynamic_slice_in_dim(tile_lists, block_index * SLOTS, SLOTS, 0)
        live_count = lax.dynamic_index_in_dim(live_counts, block_index, 0, keepdims=False)
        row_mask = frontier_rows(tile_ids, live_count)
        state_block = lax.dynamic_slice_in_dim(state, block_index * ENT_DEV, ENT_DEV, 0)
        total = jnp.zeros((ENT_DEV, FEAT), jnp.float32)
        for group in range(N_REL):
            device = block_index * N_REL + group
            first_edge = device * EDGES_DEV
            source = lax.dynamic_slice_in_dim(edge_source, first_edge, EDGES_DEV, 0)
            relation = lax.dynamic_slice_in_dim(edge_relation, first_edge, EDGES_DEV, 0)
            target = lax.dynamic_slice_in_dim(edge_target, first_edge, EDGES_DEV, 0)
            owners = lax.dynamic_slice_in_dim(edge_owner[:, 0], first_edge, EDGES_DEV, 0)
            served = grad_agg[(owners * ENT_DEV + target).astype(jnp.int32)].astype(jnp.float32) * row_mask[source][:, None]
            table = relation_table[group * REL_GROUP:(group + 1) * REL_GROUP].astype(jnp.float32)
            partial_value = jnp.zeros((ENT_DEV, FEAT), jnp.float32).at[source].add(served * table[relation])
            total = total + round_trip(partial_value)
            rel_grad = jax.ops.segment_sum(served * state_block[source].astype(jnp.float32), relation, num_segments=REL_GROUP)
            carry = carry.at[group * REL_GROUP:(group + 1) * REL_GROUP].add(rel_grad)
        return (carry, total)
    initial = jnp.zeros((RELATIONS, FEAT), jnp.float32)
    rel_total, parts = lax.scan(step, initial, jnp.arange(N_ENT, dtype=jnp.int32))
    return (parts.reshape(ENTITIES, FEAT), rel_total)

def reference(state_zero, state_one, aggregate_one, aggregate_two, cotangent, relation_table, update_in, update_bias, update_out, frontier_tiles, frontier_count, edge_source, edge_relation, edge_target, edge_owner):
    upstream = cotangent.astype(jnp.float32)
    relation_grad = jnp.zeros((RELATIONS, FEAT), jnp.float32)
    layer_sums = [None, None]
    for aggregate, state, layer in ((aggregate_two, state_one, 1), (aggregate_one, state_zero, 0)):
        grad_agg, grad_state, sums = mlp_pass(aggregate, state, upstream, update_in[layer], update_bias[layer], update_out[layer])
        source_grad, rel_part = edge_pass(grad_agg, state, relation_table, frontier_tiles[layer], frontier_count[layer], edge_source, edge_relation, edge_target, edge_owner)
        relation_grad = relation_grad + rel_part
        layer_sums[layer] = sums
        upstream = upstream + grad_state + source_grad
    scale_weights = 1.0 / math.sqrt(ENTITIES * QUERIES)
    scale_relations = math.sqrt(RELATIONS / EDGES)
    grad_in_all = jnp.stack([layer_sums[0][0], layer_sums[1][0]]) * scale_weights
    grad_bias_all = jnp.stack([layer_sums[0][1], layer_sums[1][1]]) * scale_weights
    grad_out_all = jnp.stack([layer_sums[0][2], layer_sums[1][2]]) * scale_weights
    return (upstream.astype(jnp.bfloat16), relation_grad * scale_relations, grad_in_all, grad_bias_all, grad_out_all)
```

```python
import functools
import math

import jax
import jax.numpy as jnp
from jax import lax
from jax.experimental import pallas as pl
from jax.experimental.pallas import tpu as pltpu
from jax.sharding import PartitionSpec as P

QUERIES = 8
DIM = 32
TILE = 128
WIDE = 256
HALF_Q = 4
F32 = jnp.float32
BF16 = jnp.bfloat16
VMEM = pl.BlockSpec(memory_space=pltpu.VMEM)
SMEM = pl.BlockSpec(memory_space=pltpu.SMEM)


def iota(shape, dim):
    return lax.broadcasted_iota(jnp.int32, shape, dim)


def dot_nn(a, b):
    return lax.dot_general(a, b, (((1,), (0,)), ((), ())), preferred_element_type=F32)


def dot_nt(a, b):
    return lax.dot_general(a, b, (((1,), (1,)), ((), ())), preferred_element_type=F32)


def dot_tn(a, b):
    return lax.dot_general(a, b, (((0,), (0,)), ((), ())), preferred_element_type=F32)


def params(vmem=60 << 20):
    return pltpu.CompilerParams(vmem_limit_bytes=vmem)


def cost(flops, nbytes, trans=0):
    return pl.CostEstimate(flops=int(flops), bytes_accessed=int(nbytes), transcendentals=int(trans))


def slots_kernel(peers, owner_ref, target_ref, source_ref, relation_ref, request_ref, ids_ref):
    edges = owner_ref.shape[1]
    owner = owner_ref[...]
    hit = (iota((peers, edges), 0) == owner).astype(F32)
    hit_low = hit.astype(BF16)
    below = (iota((TILE, TILE), 0) < iota((TILE, TILE), 1)).astype(BF16)
    offset = jnp.zeros((peers, 1), F32)
    pieces = []
    for b in range(edges // TILE):
        block = hit_low[:, b * TILE:(b + 1) * TILE]
        pieces.append(dot_nn(block, below) + offset)
        offset = offset + jnp.sum(hit[:, b * TILE:(b + 1) * TILE], axis=1, keepdims=True)
    before = jnp.concatenate(pieces, axis=1)
    earlier = jnp.sum(before * hit, axis=0, keepdims=True).astype(jnp.int32)
    place = (iota((32, edges), 0) == earlier).astype(F32)

    def spread(values):
        high = lax.shift_right_logical(values, 5)
        low = values & 31
        return [place * high.astype(F32), place * low.astype(F32)]

    zero = jnp.zeros((64, edges), F32)
    first = jnp.concatenate(spread(target_ref[...]) + [zero], axis=0).astype(BF16)
    request_ref[:, 0, :] = dot_nt(hit_low, first)
    second = jnp.concatenate(
        spread(source_ref[...] + 1) + spread(relation_ref[...] + 1), axis=0
    ).astype(BF16)
    ids_ref[...] = dot_nt(hit_low, second)


def slot_columns(table, capacity, bases):
    peers = table.shape[0]
    slots = peers * capacity
    row = iota((slots, peers), 0)
    start = iota((slots, peers), 1) * capacity
    expand = ((row >= start) & (row < start + capacity)).astype(BF16)
    spread = dot_nn(expand, table.astype(BF16))
    row = iota((slots, 128), 0)
    group = ((row.astype(F32) + 0.5) * (1.0 / capacity)).astype(jnp.int32)
    place = row - group * capacity
    lane = iota((slots, 128), 1)
    columns = []
    for base in bases:
        weight = jnp.where(lane == place + base, 32.0, 0.0) + jnp.where(
            lane == place + (base + 32), 1.0, 0.0
        )
        columns.append(jnp.sum(spread * weight, axis=1, keepdims=True).astype(jnp.int32))
    return columns


def compact_column(column, tiles, count):
    tile = lax.shift_right_arithmetic(column, 7)
    inner = column & 127
    result = jnp.full(column.shape, -1, jnp.int32)
    for k in range(len(tiles)):
        live = (tile == tiles[k]) & (count > k)
        result = jnp.where(live, inner + k * TILE, result)
    return result


def onehot(column, width):
    return (iota((column.shape[0], width), 1) == column).astype(F32).astype(BF16)


def build_weights(w_in_ref, w_bias_ref, w_out_ref, wx_ref, wu_ref, wb_ref):
    wx_ref[...] = jnp.zeros_like(wx_ref)
    wu_ref[...] = jnp.zeros_like(wu_ref)
    eye = (iota((DIM, DIM), 0) == iota((DIM, DIM), 1)).astype(BF16)
    w_out_t = dot_nt(eye, w_out_ref[...]).astype(BF16)
    for q in range(HALF_Q):
        rows, cols = slice(q * DIM, (q + 1) * DIM), slice(q * WIDE, (q + 1) * WIDE)
        low = slice(TILE + q * DIM, TILE + (q + 1) * DIM)
        wx_ref[rows, cols] = w_in_ref[0:DIM, :]
        wx_ref[low, cols] = w_in_ref[DIM:2 * DIM, :]
        wu_ref[rows, cols] = w_out_t
        wb_ref[:, cols] = w_bias_ref[...]


def mlp_half(s, agg, state, up_low, wx, wu, bias, acc_in, acc_out, acc_bias):
    lanes = slice(s * TILE, (s + 1) * TILE)
    x = jnp.concatenate([agg[:, lanes], state[:, lanes]], axis=1)
    up = up_low[:, lanes]
    pre = dot_nn(x, wx[...]) + bias[...]
    gate = 0.5 * jnp.tanh(0.5 * pre) + 0.5
    act = pre * gate
    slope = gate + act * (1.0 - gate)
    grad_pre = dot_nn(up, wu[...]) * slope
    low = grad_pre.astype(BF16)
    acc_in[...] += dot_tn(x, low)
    acc_out[...] += dot_tn(up, act.astype(BF16))
    acc_bias[...] += jnp.sum(grad_pre, axis=0, keepdims=True)
    return dot_nt(low, wx[...])


def store_sums(acc_in, acc_out, acc_bias, sums_ref):
    first = jnp.zeros((DIM, WIDE), F32)
    second = jnp.zeros((DIM, WIDE), F32)
    third = jnp.zeros((DIM, WIDE), F32)
    fourth = jnp.zeros((1, WIDE), F32)
    for q in range(HALF_Q):
        cols = slice(q * WIDE, (q + 1) * WIDE)
        first += acc_in[q * DIM:(q + 1) * DIM, cols]
        second += acc_in[TILE + q * DIM:TILE + (q + 1) * DIM, cols]
        third += acc_out[q * DIM:(q + 1) * DIM, cols]
        fourth += acc_bias[:, cols]
    sums_ref[0:DIM, :] = first
    sums_ref[DIM:2 * DIM, :] = second
    sums_ref[2 * DIM:3 * DIM, :] = third
    sums_ref[3 * DIM:3 * DIM + 8, :] = jnp.concatenate([fourth, jnp.zeros((7, WIDE), F32)], axis=0)


def clear(acc_in, acc_out, acc_bias):
    acc_in[...] = jnp.zeros_like(acc_in)
    acc_out[...] = jnp.zeros_like(acc_out)
    acc_bias[...] = jnp.zeros_like(acc_bias)


MLP_SCRATCH = [
    pltpu.VMEM((256, HALF_Q * WIDE), BF16),
    pltpu.VMEM((TILE, HALF_Q * WIDE), BF16),
    pltpu.VMEM((1, HALF_Q * WIDE), F32),
    pltpu.VMEM((256, HALF_Q * WIDE), F32),
    pltpu.VMEM((TILE, HALF_Q * WIDE), F32),
    pltpu.VMEM((1, HALF_Q * WIDE), F32),
]
SUM_ROWS = 3 * DIM + 8


def pick_rows(asked, grad_agg, picked_ref, chunks=4):
    rows, slots = grad_agg.shape[0], asked.shape[0]
    step = slots // chunks
    for c in range(chunks):
        part = slice(c * step, (c + 1) * step)
        picked_ref[part, :] = dot_nn(onehot(asked[part], rows), grad_agg[...]).astype(BF16)


def dense_kernel(capacity, masked, tiles_ref, count_ref, agg_ref, state_ref, up_ref, w_in_ref,
                 w_bias_ref, w_out_ref, asked_ref, next_ref, picked_ref, sums_ref,
                 wx, wu, wb, acc_in, acc_out, acc_bias, grad_agg):
    step = pl.program_id(0)
    rows = agg_ref.shape[0]

    @pl.when(step == 0)
    def _():
        build_weights(w_in_ref, w_bias_ref, w_out_ref, wx, wu, wb)
        clear(acc_in, acc_out, acc_bias)

    up = up_ref[...].astype(F32)
    up_low = up_ref[...].astype(BF16)
    if masked:
        tile = lax.shift_right_logical(iota((rows, 1), 0) + step * rows, 7)
        dead = (tile == tiles_ref[1, 0]) | ((tile == tiles_ref[1, 1]) & (count_ref[1, 0] > 1))
        up_low = jnp.where(dead, 0.0, up).astype(BF16)
    aggs, states = [], []
    for s in range(2):
        grad_x = mlp_half(s, agg_ref[...], state_ref[...], up_low, wx, wu, wb, acc_in, acc_out, acc_bias)
        aggs.append(grad_x[:, :TILE])
        states.append(grad_x[:, TILE:])
    grad_agg[pl.ds(pl.multiple_of(step * rows, rows), rows), :] = jnp.concatenate(aggs, axis=1).astype(BF16)
    next_ref[...] = up + jnp.concatenate(states, axis=1)

    @pl.when(step == pl.num_programs(0) - 1)
    def _():
        store_sums(acc_in, acc_out, acc_bias, sums_ref)
        asked = slot_columns(asked_ref[:, 0, :], capacity, (0,))[0]
        pick_rows(asked, grad_agg, picked_ref)


def dense_pass(masked, capacity, tiles, count, agg, state, up, w_in, w_bias, w_out, asked):
    rows, feat = agg.shape
    slots = asked.shape[0] * capacity
    block = 256
    row_spec = pl.BlockSpec((block, feat), lambda i: (i, 0))

    def whole(shape):
        return pl.BlockSpec(shape, lambda i: (0,) * len(shape))

    return pl.pallas_call(
        functools.partial(dense_kernel, capacity, masked),
        grid=(rows // block,),
        in_specs=[SMEM, SMEM, row_spec, row_spec, row_spec, whole(w_in.shape), whole(w_bias.shape),
                  whole(w_out.shape), whole(asked.shape)],
        out_specs=[row_spec, whole((slots, feat)), whole((SUM_ROWS, WIDE))],
        out_shape=[
            jax.ShapeDtypeStruct((rows, feat), F32),
            jax.ShapeDtypeStruct((slots, feat), BF16),
            jax.ShapeDtypeStruct((SUM_ROWS, WIDE), F32),
        ],
        scratch_shapes=MLP_SCRATCH + [pltpu.VMEM((rows, feat), BF16)],
        compiler_params=params(),
        cost_estimate=cost(5.4e9, 4 << 20, 2 << 20),
        name="dense_masked" if masked else "dense",
    )(tiles, count, agg, state, up, w_in, w_bias, w_out, asked)


def tables_kernel(capacity, tiles_ref, count_ref, ids_ref, table_ref, one_a, one_b, zero_a, zero_b,
                  t_ref, s2_ref, h2_ref, s1_ref, h1_ref, r_ref):
    source, relation = slot_columns(ids_ref[...], capacity, (0, 64))
    source, relation = source - 1, relation - 1
    width = r_ref.shape[1]
    pad = width - table_ref.shape[0]
    table = jnp.concatenate([table_ref[...], jnp.zeros((pad, table_ref.shape[1]), BF16)], axis=0)
    select = onehot(relation, width)
    r_ref[...] = select
    t_ref[...] = dot_nn(select, table).astype(BF16)
    for hop, s_ref, h_ref, a, b in ((1, s2_ref, h2_ref, one_a, one_b), (0, s1_ref, h1_ref, zero_a, zero_b)):
        column = compact_column(source, (tiles_ref[hop, 0], tiles_ref[hop, 1]), count_ref[hop, 0])
        select = onehot(column, 2 * TILE)
        s_ref[...] = select
        h_ref[...] = dot_nn(select, jnp.concatenate([a[...], b[...]], axis=0)).astype(BF16)


def slot_tables(capacity, tiles, count, ids, table, state_one, state_zero):
    feat = table.shape[1]
    slots = ids.shape[0] * capacity
    width = -(-table.shape[0] // TILE) * TILE

    def whole(shape):
        return pl.BlockSpec(shape, lambda i, *_: (0,) * len(shape))

    def tile(hop, k):
        return pl.BlockSpec((TILE, feat), lambda i, tiles, count: (tiles[hop, k], 0))

    shape = jax.ShapeDtypeStruct((slots, feat), BF16)
    return pl.pallas_call(
        functools.partial(tables_kernel, capacity),
        grid_spec=pltpu.PrefetchScalarGridSpec(
            num_scalar_prefetch=2,
            grid=(1,),
            in_specs=[whole(ids.shape), whole(table.shape), tile(1, 0), tile(1, 1), tile(0, 0), tile(0, 1)],
            out_specs=[whole((slots, feat))] * 5 + [whole((slots, width))],
        ),
        out_shape=[shape] * 5 + [jax.ShapeDtypeStruct((slots, width), BF16)],
        compiler_params=params(),
        cost_estimate=cost(2e9, 6 << 20),
        name="tables",
    )(tiles, count, ids, table, state_one, state_one, state_zero, state_zero)


def contribution_kernel(answer_ref, t_ref, s_ref, out_ref):
    out_ref[...] = dot_tn(s_ref[...], answer_ref[...] * t_ref[...]).astype(BF16)


def contribution(answer, table, select):
    return pl.pallas_call(
        contribution_kernel,
        in_specs=[VMEM] * 3,
        out_specs=VMEM,
        out_shape=jax.ShapeDtypeStruct((select.shape[1], answer.shape[1]), BF16),
        compiler_params=params(),
        cost_estimate=cost(2e8, 3 << 20),
        name="contribution",
    )(answer, table, select)


def relation_kernel(answer_ref, h_ref, r_ref, out_ref):
    out_ref[...] = dot_tn(r_ref[...], answer_ref[...] * h_ref[...])


def relation_part(answer, states, select):
    return pl.pallas_call(
        relation_kernel,
        in_specs=[VMEM] * 3,
        out_specs=VMEM,
        out_shape=jax.ShapeDtypeStruct((select.shape[1], answer.shape[1]), F32),
        compiler_params=params(),
        cost_estimate=cost(4e8, 3 << 20),
        name="relation_part",
    )(answer, states, select)


def live_kernel(capacity, tiles_ref, count_ref, agg_a, agg_b, state_a, state_b, up_a, up_b, c0, c1, c2, c3,
                w_in_ref, w_bias_ref, w_out_ref, asked_ref, rest_ref, picked_ref, next_ref, sums_ref,
                wx, wu, wb, acc_in, acc_out, acc_bias):
    build_weights(w_in_ref, w_bias_ref, w_out_ref, wx, wu, wb)
    clear(acc_in, acc_out, acc_bias)
    count = count_ref[1, 0]
    source = (c0[...].astype(F32) + c1[...].astype(F32)) + (c2[...].astype(F32) + c3[...].astype(F32))
    up = jnp.concatenate([up_a[...], up_b[...]], axis=0) + source
    keep = (iota((2 * TILE, 1), 0) < TILE) | (count > 1)
    up_low = jnp.where(keep, up, 0.0).astype(BF16)
    agg = jnp.concatenate([agg_a[...], agg_b[...]], axis=0)
    state = jnp.concatenate([state_a[...], state_b[...]], axis=0)
    aggs, states = [], []
    for s in range(2):
        grad_x = mlp_half(s, agg, state, up_low, wx, wu, wb, acc_in, acc_out, acc_bias)
        aggs.append(grad_x[:, :TILE])
        states.append(grad_x[:, TILE:])
    grad_agg = jnp.concatenate(aggs, axis=1).astype(BF16)
    next_ref[...] = up + jnp.concatenate(states, axis=1)
    store_sums(acc_in, acc_out, acc_bias, sums_ref)
    asked = slot_columns(asked_ref[:, 0, :], capacity, (0,))[0]
    column = compact_column(asked, (tiles_ref[1, 0], tiles_ref[1, 1]), count)
    live = dot_nn(onehot(column, 2 * TILE), grad_agg)
    picked_ref[...] = jnp.where(column >= 0, live, rest_ref[...].astype(F32)).astype(BF16)


def live_pass(capacity, tiles, count, agg, state, up, parts, w_in, w_bias, w_out, asked, rest):
    feat = agg.shape[1]

    def whole(shape):
        return pl.BlockSpec(shape, lambda i, *_: (0,) * len(shape))

    def tile(k):
        return pl.BlockSpec((TILE, feat), lambda i, tiles, count: (tiles[1, k], 0))

    return pl.pallas_call(
        functools.partial(live_kernel, capacity),
        grid_spec=pltpu.PrefetchScalarGridSpec(
            num_scalar_prefetch=2,
            grid=(1,),
            in_specs=[tile(0), tile(1)] * 3 + [whole(parts[0].shape)] * 4
            + [whole(w_in.shape), whole(w_bias.shape), whole(w_out.shape), whole(asked.shape), whole(rest.shape)],
            out_specs=[whole(rest.shape), whole((2 * TILE, feat)), whole((SUM_ROWS, WIDE))],
            scratch_shapes=MLP_SCRATCH,
        ),
        out_shape=[
            jax.ShapeDtypeStruct(rest.shape, BF16),
            jax.ShapeDtypeStruct((2 * TILE, feat), F32),
            jax.ShapeDtypeStruct((SUM_ROWS, WIDE), F32),
        ],
        compiler_params=params(),
        cost_estimate=cost(1.6e9, 4 << 20, 1 << 19),
        name="live",
    )(tiles, count, agg, agg, state, state, up, up, *parts, w_in, w_bias, w_out, asked, rest)


GAP = SUM_ROWS


def pack_kernel(answer_ref, h_ref, r_ref, before_ref, w2_ref, w1a_ref, w1b_ref, out_ref):
    total = before_ref[...] + dot_tn(r_ref[...], answer_ref[...] * h_ref[...])
    used, rows = total.shape[0], out_ref.shape[0]
    feat = total.shape[1]
    out_ref[...] = jnp.zeros_like(out_ref)
    out_ref[0:used, 0:feat] = total.astype(BF16)
    layers = (w1a_ref[...] + w1b_ref[...], w2_ref[...])
    parts = []
    for layer in layers:
        parts += [layer[:, :TILE], layer[:, TILE:]]
    parts = jnp.concatenate(parts, axis=0).astype(BF16)
    out_ref[0:4 * GAP, feat:feat + TILE] = parts


def pack_sums(answer, states, select, before, w2, w1a, w1b, rows):
    feat = answer.shape[1]
    return pl.pallas_call(
        pack_kernel,
        in_specs=[VMEM] * 7,
        out_specs=VMEM,
        out_shape=jax.ShapeDtypeStruct((rows, feat + TILE), BF16),
        compiler_params=params(),
        cost_estimate=cost(4e8, 4 << 20),
        name="pack_sums",
    )(answer, states, select, before, w2, w1a, w1b)


def combine_kernel(feat, scale_relations, scale_weights, in_ref, out_ref):
    total = jnp.sum(in_ref[...].astype(F32), axis=0)
    lane = iota(total.shape, 1)
    total = total * jnp.where(lane < feat, scale_relations, scale_weights)
    out_ref[...] = jnp.broadcast_to(total.astype(BF16)[None], out_ref.shape)


def combine(chunks, feat, scale_relations, scale_weights):
    return pl.pallas_call(
        functools.partial(combine_kernel, feat, scale_relations, scale_weights),
        in_specs=[VMEM],
        out_specs=VMEM,
        out_shape=jax.ShapeDtypeStruct(chunks.shape, BF16),
        compiler_params=params(),
        cost_estimate=cost(1e6, 1 << 20),
        name="combine",
    )(chunks)


def unpack_kernel(feat, in_ref, relation_ref, w_in_ref, w_bias_ref, w_out_ref):
    groups = relation_ref.shape[0]
    relation_ref[...] = in_ref[0:groups, 0:feat].astype(F32)
    for layer in range(2):
        at = 2 * layer * GAP
        left = in_ref[at:at + GAP, feat:feat + TILE].astype(F32)
        right = in_ref[at + GAP:at + 2 * GAP, feat:feat + TILE].astype(F32)
        both = jnp.concatenate([left, right], axis=1)
        w_in_ref[layer] = both[0:2 * DIM]
        w_out_ref[layer] = both[2 * DIM:3 * DIM].T
        w_bias_ref[layer:layer + 1, :] = both[3 * DIM:3 * DIM + 1]


def unpack(gathered, groups, feat):
    return pl.pallas_call(
        functools.partial(unpack_kernel, feat),
        in_specs=[VMEM],
        out_specs=[VMEM] * 4,
        out_shape=[
            jax.ShapeDtypeStruct((groups, feat), F32),
            jax.ShapeDtypeStruct((2, 2 * DIM, WIDE), F32),
            jax.ShapeDtypeStruct((2, WIDE), F32),
            jax.ShapeDtypeStruct((2, WIDE, DIM), F32),
        ],
        compiler_params=params(),
        cost_estimate=cost(1e6, 2 << 20),
        name="unpack",
    )(gathered)


def final_kernel(tiles_ref, count_ref, quarter_ref, next_ref, live_ref, c0, c1, c2, c3, out_ref):
    tile = 2 * quarter_ref[0] + pl.program_id(0)
    value = next_ref[...]
    for k in range(2):
        rows = slice(k * TILE, (k + 1) * TILE)
        is_live = (tile == tiles_ref[1, k]) & (count_ref[1, 0] > k)
        value = jnp.where(is_live, live_ref[rows, :], value)
    for k in range(2):
        rows = slice(k * TILE, (k + 1) * TILE)
        is_live = (tile == tiles_ref[0, k]) & (count_ref[0, 0] > k)
        source = (c0[rows, :].astype(F32) + c1[rows, :].astype(F32)) + (
            c2[rows, :].astype(F32) + c3[rows, :].astype(F32)
        )
        value = jnp.where(is_live, value + source, value)
    out_ref[...] = value.astype(BF16)


def final_pass(tiles, count, quarter_id, after, live, parts, quarter):
    feat = after.shape[1]
    blocks = quarter // TILE

    def whole(shape):
        return pl.BlockSpec(shape, lambda i, *_: (0,) * len(shape))

    return pl.pallas_call(
        final_kernel,
        grid_spec=pltpu.PrefetchScalarGridSpec(
            num_scalar_prefetch=3,
            grid=(blocks,),
            in_specs=[pl.BlockSpec((TILE, feat), lambda i, t, c, q: (q[0] * blocks + i, 0)), whole(live.shape)]
            + [whole(parts[0].shape)] * 4,
            out_specs=pl.BlockSpec((TILE, feat), lambda i, *_: (i, 0)),
        ),
        out_shape=jax.ShapeDtypeStruct((quarter, feat), BF16),
        compiler_params=params(),
        cost_estimate=cost(1e6, 1 << 20),
        name="final",
    )(tiles, count, quarter_id, after, live, *parts)


def shards(state_zero, state_one, aggregate_one, aggregate_two, cotangent, relation_table, update_in, update_bias,
           update_out, frontier_tiles, frontier_count, edge_source, edge_relation, edge_target, edge_owner):
    block_rows, feat = state_zero.shape
    groups = relation_table.shape[0]
    group_size = lax.axis_size("rel")
    peers = lax.axis_size("ent")
    quarter = block_rows // group_size
    edges = edge_source.shape[0]
    capacity = 3 * edges // (2 * peers)
    slots = peers * capacity
    sum_rows = 8 * peers

    def exchange(chunks):
        return lax.all_to_all(chunks, "ent", split_axis=0, concat_axis=0, tiled=True)

    def over_rel(part):
        turned = [
            lax.ppermute(part, "rel", [(i, (i + k) % group_size) for i in range(group_size)])
            for k in range(1, group_size)
        ]
        return [part] + turned

    def layer(index):
        return update_in[index], update_bias[index][None, :], update_out[index]

    row = lambda values: values.reshape(1, edges)
    request, ids = pl.pallas_call(
        functools.partial(slots_kernel, peers),
        in_specs=[VMEM] * 4,
        out_specs=[VMEM] * 2,
        out_shape=[
            jax.ShapeDtypeStruct((peers, 1, 128), F32),
            jax.ShapeDtypeStruct((peers, 128), F32),
        ],
        compiler_params=params(),
        cost_estimate=cost(1e8, 1 << 20),
        name="slots",
    )(row(edge_owner), row(edge_target), row(edge_source), row(edge_relation))
    asked = exchange(request)

    upstream_one, picked_two, sums_two = dense_pass(
        False, capacity, frontier_tiles, frontier_count, aggregate_two, state_one, cotangent, *layer(1), asked
    )
    answered_two = exchange(picked_two.reshape(peers, capacity, feat)).reshape(slots, feat)
    after, rest, sums_rest = dense_pass(
        True, capacity, frontier_tiles, frontier_count, aggregate_one, state_zero, upstream_one, *layer(0), asked
    )
    edge_table, select_two, states_two, select_one, states_one, select_rel = slot_tables(
        capacity, frontier_tiles, frontier_count, ids, relation_table, state_one, state_zero
    )
    parts = over_rel(contribution(answered_two, edge_table, select_two))
    picked_one, after_live, sums_live = live_pass(
        capacity, frontier_tiles, frontier_count, aggregate_one, state_zero, upstream_one, parts, *layer(0), asked, rest
    )
    answered_one = exchange(picked_one.reshape(peers, capacity, feat)).reshape(slots, feat)
    relation_two = relation_part(answered_two, states_two, select_rel)

    parts = over_rel(contribution(answered_one, edge_table, select_one))
    packed = pack_sums(
        answered_one, states_one, select_rel, relation_two, sums_two, sums_rest, sums_live, sum_rows
    )
    scale_weights = 1.0 / math.sqrt(block_rows * peers * QUERIES)
    scale_relations = math.sqrt(groups * group_size / (edges * peers * group_size))
    chunks = exchange(packed.reshape(peers, 8, feat + TILE))
    gathered = exchange(combine(chunks, feat, scale_relations, scale_weights)).reshape(sum_rows, feat + TILE)
    quarter_id = lax.axis_index("rel").astype(jnp.int32).reshape(1)
    grad_zero = final_pass(frontier_tiles, frontier_count, quarter_id, after, after_live, parts, quarter)
    return (grad_zero,) + tuple(unpack(gathered, groups, feat))


def solution(mesh):
    in_specs = (
        P("ent", None),
        P("ent", None),
        P("ent", None),
        P("ent", None),
        P("ent", None),
        P("rel", None),
        P(),
        P(),
        P(),
        P(None, "ent"),
        P(None, "ent"),
        P(("ent", "rel")),
        P(("ent", "rel")),
        P(("ent", "rel")),
        P(("ent", "rel"), None),
    )
    out_specs = (P(("ent", "rel"), None), P("rel", None), P(), P(), P())
    return jax.shard_map(shards, mesh=mesh, in_specs=in_specs, out_specs=out_specs, check_vma=False)
```

```python
import functools
import math

import jax
import jax.numpy as jnp
from jax import lax
from jax.experimental import pallas as pl
from jax.experimental.pallas import tpu as pltpu
from jax.sharding import PartitionSpec as P

QUERIES = 8
DIM = 32
TILE = 128
WIDE = 256
HALF_Q = 4
F32 = jnp.float32
BF16 = jnp.bfloat16
VMEM = pl.BlockSpec(memory_space=pltpu.VMEM)
SMEM = pl.BlockSpec(memory_space=pltpu.SMEM)


def iota(shape, dim):
    return lax.broadcasted_iota(jnp.int32, shape, dim)


def dot_nn(a, b):
    return lax.dot_general(a, b, (((1,), (0,)), ((), ())), preferred_element_type=F32)


def dot_nt(a, b):
    return lax.dot_general(a, b, (((1,), (1,)), ((), ())), preferred_element_type=F32)


def dot_tn(a, b):
    return lax.dot_general(a, b, (((0,), (0,)), ((), ())), preferred_element_type=F32)


def params(vmem=20 << 20):
    return pltpu.CompilerParams(vmem_limit_bytes=vmem)


def cost(flops, nbytes, trans=0):
    return pl.CostEstimate(flops=int(flops), bytes_accessed=int(nbytes), transcendentals=int(trans))


def slots_kernel(peers, owner_ref, target_ref, source_ref, relation_ref, request_ref, ids_ref):
    edges = owner_ref.shape[1]
    owner = owner_ref[...]
    hit = (iota((peers, edges), 0) == owner).astype(F32)
    hit_low = hit.astype(BF16)
    below = (iota((TILE, TILE), 0) < iota((TILE, TILE), 1)).astype(BF16)
    offset = jnp.zeros((peers, 1), F32)
    pieces = []
    for b in range(edges // TILE):
        block = hit_low[:, b * TILE:(b + 1) * TILE]
        pieces.append(dot_nn(block, below) + offset)
        offset = offset + jnp.sum(hit[:, b * TILE:(b + 1) * TILE], axis=1, keepdims=True)
    before = jnp.concatenate(pieces, axis=1)
    earlier = jnp.sum(before * hit, axis=0, keepdims=True).astype(jnp.int32)
    place = (iota((32, edges), 0) == earlier).astype(F32)

    def spread(values):
        high = lax.shift_right_logical(values, 5)
        low = values & 31
        return [place * high.astype(F32), place * low.astype(F32)]

    zero = jnp.zeros((64, edges), F32)
    first = jnp.concatenate(spread(target_ref[...]) + [zero], axis=0).astype(BF16)
    request_ref[:, 0, :] = dot_nt(hit_low, first)
    second = jnp.concatenate(
        spread(source_ref[...] + 1) + spread(relation_ref[...] + 1), axis=0
    ).astype(BF16)
    ids_ref[...] = dot_nt(hit_low, second)


def slot_columns(table, capacity, bases):
    peers = table.shape[0]
    slots = peers * capacity
    row = iota((slots, peers), 0)
    start = iota((slots, peers), 1) * capacity
    expand = ((row >= start) & (row < start + capacity)).astype(BF16)
    spread = dot_nn(expand, table.astype(BF16))
    row = iota((slots, 128), 0)
    group = ((row.astype(F32) + 0.5) * (1.0 / capacity)).astype(jnp.int32)
    place = row - group * capacity
    lane = iota((slots, 128), 1)
    columns = []
    for base in bases:
        weight = jnp.where(lane == place + base, 32.0, 0.0) + jnp.where(
            lane == place + (base + 32), 1.0, 0.0
        )
        columns.append(jnp.sum(spread * weight, axis=1, keepdims=True).astype(jnp.int32))
    return columns


def compact_column(column, tiles, count):
    tile = lax.shift_right_arithmetic(column, 7)
    inner = column & 127
    result = jnp.full(column.shape, -1, jnp.int32)
    for k in range(len(tiles)):
        live = (tile == tiles[k]) & (count > k)
        result = jnp.where(live, inner + k * TILE, result)
    return result


def onehot(column, width):
    return (iota((column.shape[0], width), 1) == column).astype(F32).astype(BF16)


def build_weights(layer, w_in_ref, w_bias_ref, w_out_ref, wx_ref, wu_ref, wb_ref):
    wx_ref[...] = jnp.zeros_like(wx_ref)
    wu_ref[...] = jnp.zeros_like(wu_ref)
    for q in range(HALF_Q):
        rows, cols = slice(q * DIM, (q + 1) * DIM), slice(q * WIDE, (q + 1) * WIDE)
        low = slice(TILE + q * DIM, TILE + (q + 1) * DIM)
        wx_ref[rows, cols] = w_in_ref[layer, 0:DIM, :]
        wx_ref[low, cols] = w_in_ref[layer, DIM:2 * DIM, :]
        wu_ref[rows, cols] = w_out_ref[layer]
        wb_ref[:, cols] = w_bias_ref[layer:layer + 1, :]


def mlp_half(s, agg, state, up_low, wx, wu, bias, acc_in, acc_out, acc_bias):
    lanes = slice(s * TILE, (s + 1) * TILE)
    x = jnp.concatenate([agg[:, lanes], state[:, lanes]], axis=1)
    up = up_low[:, lanes]
    pre = dot_nn(x, wx[...]) + bias[...]
    gate = 0.5 * jnp.tanh(0.5 * pre) + 0.5
    act = pre * gate
    slope = gate + act * (1.0 - gate)
    grad_pre = dot_nn(up, wu[...]) * slope
    low = grad_pre.astype(BF16)
    acc_in[...] += dot_tn(x, low)
    acc_out[...] += dot_tn(up, act.astype(BF16))
    acc_bias[...] += jnp.sum(grad_pre, axis=0, keepdims=True)
    return dot_nt(low, wx[...])


def store_sums(acc_in, acc_out, acc_bias, sums_ref):
    first = jnp.zeros((DIM, WIDE), F32)
    second = jnp.zeros((DIM, WIDE), F32)
    third = jnp.zeros((DIM, WIDE), F32)
    fourth = jnp.zeros((1, WIDE), F32)
    for q in range(HALF_Q):
        cols = slice(q * WIDE, (q + 1) * WIDE)
        first += acc_in[q * DIM:(q + 1) * DIM, cols]
        second += acc_in[TILE + q * DIM:TILE + (q + 1) * DIM, cols]
        third += acc_out[q * DIM:(q + 1) * DIM, cols]
        fourth += acc_bias[:, cols]
    sums_ref[0:DIM, :] = first
    sums_ref[DIM:2 * DIM, :] = second
    sums_ref[2 * DIM:3 * DIM, :] = third
    sums_ref[3 * DIM:3 * DIM + 8, :] = jnp.concatenate([fourth, jnp.zeros((7, WIDE), F32)], axis=0)


def clear(acc_in, acc_out, acc_bias):
    acc_in[...] = jnp.zeros_like(acc_in)
    acc_out[...] = jnp.zeros_like(acc_out)
    acc_bias[...] = jnp.zeros_like(acc_bias)


WEIGHT_SHAPES = [
    ((2 * TILE, HALF_Q * WIDE), BF16),
    ((TILE, HALF_Q * WIDE), BF16),
    ((1, HALF_Q * WIDE), F32),
]
SUM_SHAPES = [
    ((2 * TILE, HALF_Q * WIDE), F32),
    ((TILE, HALF_Q * WIDE), F32),
    ((1, HALF_Q * WIDE), F32),
]
SUM_ROWS = 3 * DIM + 8


def scratch(shapes):
    return [pltpu.VMEM(shape, dtype) for shape, dtype in shapes]


def whole(shape):
    return pl.BlockSpec(shape, lambda i, *_: (0,) * len(shape))


def pick_rows(asked, grad_agg, picked_ref, chunks=4):
    rows, slots = grad_agg.shape[0], asked.shape[0]
    step = slots // chunks
    for c in range(chunks):
        part = slice(c * step, (c + 1) * step)
        picked_ref[part, :] = dot_nn(onehot(asked[part], rows), grad_agg[...]).astype(BF16)


def dense_step(step, agg_ref, state_ref, up, up_low, wx, wu, wb, acc_in, acc_out, acc_bias, grad_agg, next_ref):
    rows = agg_ref.shape[0]
    aggs, states = [], []
    for s in range(2):
        grad_x = mlp_half(s, agg_ref[...], state_ref[...], up_low, wx, wu, wb, acc_in, acc_out, acc_bias)
        aggs.append(grad_x[:, :TILE])
        states.append(grad_x[:, TILE:])
    grad_agg[pl.ds(pl.multiple_of(step * rows, rows), rows), :] = jnp.concatenate(aggs, axis=1).astype(BF16)
    next_ref[...] = up + jnp.concatenate(states, axis=1)


def first_kernel(capacity, agg_ref, state_ref, up_ref, w_in_ref, w_bias_ref, w_out_ref, asked_ref,
                 next_ref, picked_ref, sums_ref, wx, wu, wb, acc_in, acc_out, acc_bias, grad_agg):
    step = pl.program_id(0)

    @pl.when(step == 0)
    def _():
        build_weights(1, w_in_ref, w_bias_ref, w_out_ref, wx, wu, wb)
        clear(acc_in, acc_out, acc_bias)

    up_low = up_ref[...]
    dense_step(step, agg_ref, state_ref, up_low.astype(F32), up_low, wx, wu, wb, acc_in, acc_out, acc_bias,
               grad_agg, next_ref)

    @pl.when(step == pl.num_programs(0) - 1)
    def _():
        store_sums(acc_in, acc_out, acc_bias, sums_ref)
        asked = slot_columns(asked_ref[:, 0, :], capacity, (0,))[0]
        pick_rows(asked, grad_agg, picked_ref)


def first_pass(capacity, agg, state, up, w_in, w_bias, w_out, asked):
    rows, feat = agg.shape
    slots = asked.shape[0] * capacity
    block = 256
    row_spec = pl.BlockSpec((block, feat), lambda i: (i, 0))
    return pl.pallas_call(
        functools.partial(first_kernel, capacity),
        grid=(rows // block,),
        in_specs=[row_spec, row_spec, row_spec, whole(w_in.shape), whole(w_bias.shape), whole(w_out.shape),
                  whole(asked.shape)],
        out_specs=[row_spec, whole((slots, feat)), whole((SUM_ROWS, WIDE))],
        out_shape=[
            jax.ShapeDtypeStruct((rows, feat), F32),
            jax.ShapeDtypeStruct((slots, feat), BF16),
            jax.ShapeDtypeStruct((SUM_ROWS, WIDE), F32),
        ],
        scratch_shapes=scratch(WEIGHT_SHAPES + SUM_SHAPES) + [pltpu.VMEM((rows, feat), BF16)],
        compiler_params=params(),
        cost_estimate=cost(5.4e9, 4 << 20, 2 << 20),
        name="first",
    )(agg, state, up, w_in, w_bias, w_out, asked)


def rest_kernel(capacity, tiles_ref, count_ref, agg_ref, state_ref, up_ref, w_in_ref, w_bias_ref, w_out_ref,
                asked_ref, next_ref, picked_ref, sums_ref, live_ref, wx, wu, wb,
                acc_in, acc_out, acc_bias, grad_agg):
    step = pl.program_id(0)
    rows = agg_ref.shape[0]
    count = count_ref[0, 1]

    @pl.when(step == 0)
    def _():
        build_weights(0, w_in_ref, w_bias_ref, w_out_ref, wx, wu, wb)
        clear(acc_in, acc_out, acc_bias)

    up = up_ref[...]
    tile = lax.shift_right_logical(iota((rows, 1), 0) + step * rows, 7)
    dead = (tile == tiles_ref[1, 0]) | ((tile == tiles_ref[1, 1]) & (count > 1))
    up_low = jnp.where(dead, 0.0, up).astype(BF16)
    dense_step(step, agg_ref, state_ref, up, up_low, wx, wu, wb, acc_in, acc_out, acc_bias, grad_agg, next_ref)

    @pl.when(step == pl.num_programs(0) - 1)
    def _():
        store_sums(acc_in, acc_out, acc_bias, sums_ref)
        asked = slot_columns(asked_ref[:, 0, :], capacity, (0,))[0]
        live_ref[...] = onehot(compact_column(asked, (tiles_ref[1, 0], tiles_ref[1, 1]), count), 2 * TILE)
        pick_rows(asked, grad_agg, picked_ref)


def rest_pass(capacity, tiles, count, agg, state, up, w_in, w_bias, w_out, asked):
    rows, feat = agg.shape
    slots = asked.shape[0] * capacity
    block = 256
    row_spec = pl.BlockSpec((block, feat), lambda i: (i, 0))
    return pl.pallas_call(
        functools.partial(rest_kernel, capacity),
        grid=(rows // block,),
        in_specs=[SMEM, SMEM, row_spec, row_spec, row_spec, whole(w_in.shape), whole(w_bias.shape),
                  whole(w_out.shape), whole(asked.shape)],
        out_specs=[row_spec, whole((slots, feat)), whole((SUM_ROWS, WIDE)), whole((slots, 2 * TILE))]
        + [whole(shape) for shape, _ in WEIGHT_SHAPES],
        out_shape=[
            jax.ShapeDtypeStruct((rows, feat), F32),
            jax.ShapeDtypeStruct((slots, feat), BF16),
            jax.ShapeDtypeStruct((SUM_ROWS, WIDE), F32),
            jax.ShapeDtypeStruct((slots, 2 * TILE), BF16),
        ]
        + [jax.ShapeDtypeStruct(shape, dtype) for shape, dtype in WEIGHT_SHAPES],
        scratch_shapes=scratch(SUM_SHAPES) + [pltpu.VMEM((rows, feat), BF16)],
        compiler_params=params(),
        cost_estimate=cost(5.4e9, 4 << 20, 2 << 20),
        name="rest",
    )(tiles, count, agg, state, up, w_in, w_bias, w_out, asked)


def tables_two_kernel(capacity, tiles_ref, count_ref, ids_ref, table_ref, t_ref, s_ref):
    source, relation = slot_columns(ids_ref[...], capacity, (0, 64))
    width = -(-table_ref.shape[0] // TILE) * TILE
    pad = width - table_ref.shape[0]
    table = jnp.concatenate([table_ref[...], jnp.zeros((pad, table_ref.shape[1]), BF16)], axis=0)
    t_ref[...] = dot_nn(onehot(relation - 1, width), table).astype(BF16)
    column = compact_column(source - 1, (tiles_ref[1, 0], tiles_ref[1, 1]), count_ref[0, 1])
    s_ref[...] = onehot(column, 2 * TILE).T


def tables_two(capacity, tiles, count, ids, table):
    feat = table.shape[1]
    slots = ids.shape[0] * capacity
    return pl.pallas_call(
        functools.partial(tables_two_kernel, capacity),
        in_specs=[SMEM, SMEM, VMEM, VMEM],
        out_specs=[VMEM, VMEM],
        out_shape=[
            jax.ShapeDtypeStruct((slots, feat), BF16),
            jax.ShapeDtypeStruct((2 * TILE, slots), BF16),
        ],
        compiler_params=params(),
        cost_estimate=cost(1e9, 2 << 20),
        name="tables_two",
    )(tiles, count, ids, table)


def tables_one_kernel(capacity, tiles_ref, count_ref, ids_ref, answer_ref, one_a, one_b, zero_a, zero_b,
                      s_ref, h_ref, r_ref, total_ref):
    source, relation = slot_columns(ids_ref[...], capacity, (0, 64))
    columns = [
        compact_column(source - 1, (tiles_ref[hop, 0], tiles_ref[hop, 1]), count_ref[0, hop]) for hop in range(2)
    ]
    select = onehot(columns[0], 2 * TILE)
    s_ref[...] = select.T
    h_ref[...] = dot_nn(select, jnp.concatenate([zero_a[...], zero_b[...]], axis=0)).astype(BF16)
    states = dot_nn(onehot(columns[1], 2 * TILE), jnp.concatenate([one_a[...], one_b[...]], axis=0)).astype(BF16)
    turned = onehot(relation - 1, r_ref.shape[0]).T
    r_ref[...] = turned
    total_ref[...] = dot_nn(turned, answer_ref[...] * states)


def tables_one(capacity, tiles, count, ids, answer, state_one, state_zero, groups):
    feat = answer.shape[1]
    slots = ids.shape[0] * capacity
    width = -(-groups // TILE) * TILE

    def tile(hop, k):
        return pl.BlockSpec((TILE, feat), lambda i, tiles, count: (tiles[hop, k], 0))

    return pl.pallas_call(
        functools.partial(tables_one_kernel, capacity),
        grid_spec=pltpu.PrefetchScalarGridSpec(
            num_scalar_prefetch=2,
            grid=(1,),
            in_specs=[whole(ids.shape), whole(answer.shape), tile(1, 0), tile(1, 1), tile(0, 0), tile(0, 1)],
            out_specs=[whole((2 * TILE, slots)), whole((slots, feat)), whole((width, slots)), whole((width, feat))],
        ),
        out_shape=[
            jax.ShapeDtypeStruct((2 * TILE, slots), BF16),
            jax.ShapeDtypeStruct((slots, feat), BF16),
            jax.ShapeDtypeStruct((width, slots), BF16),
            jax.ShapeDtypeStruct((width, feat), F32),
        ],
        compiler_params=params(24 << 20),
        cost_estimate=cost(2e9, 4 << 20),
        name="tables_one",
    )(tiles, count, ids, answer, state_one, state_one, state_zero, state_zero)


def contribution_kernel(answer_ref, t_ref, s_ref, out_ref):
    out_ref[...] = dot_nn(s_ref[...], answer_ref[...] * t_ref[...]).astype(BF16)


def contribution(answer, table, select):
    return pl.pallas_call(
        contribution_kernel,
        in_specs=[VMEM] * 3,
        out_specs=VMEM,
        out_shape=jax.ShapeDtypeStruct((select.shape[0], answer.shape[1]), BF16),
        compiler_params=params(8 << 20),
        cost_estimate=cost(2e8, 3 << 20),
        name="contribution",
    )(answer, table, select)


def live_kernel(tiles_ref, count_ref, agg_a, agg_b, state_a, state_b, up_a, up_b, c0, c1, c2, c3,
                wx, wu, wb, live_ref, rest_ref, picked_ref, next_ref, sums_ref, acc_in, acc_out, acc_bias):
    clear(acc_in, acc_out, acc_bias)
    source = (c0[...].astype(F32) + c1[...].astype(F32)) + (c2[...].astype(F32) + c3[...].astype(F32))
    up = jnp.concatenate([up_a[...], up_b[...]], axis=0) + source
    keep = (iota((2 * TILE, 1), 0) < TILE) | (count_ref[0, 1] > 1)
    up_low = jnp.where(keep, up, 0.0).astype(BF16)
    agg = jnp.concatenate([agg_a[...], agg_b[...]], axis=0)
    state = jnp.concatenate([state_a[...], state_b[...]], axis=0)
    aggs, states = [], []
    for s in range(2):
        grad_x = mlp_half(s, agg, state, up_low, wx, wu, wb, acc_in, acc_out, acc_bias)
        aggs.append(grad_x[:, :TILE])
        states.append(grad_x[:, TILE:])
    grad_agg = jnp.concatenate(aggs, axis=1).astype(BF16)
    next_ref[...] = up + jnp.concatenate(states, axis=1)
    store_sums(acc_in, acc_out, acc_bias, sums_ref)
    picked_ref[...] = (dot_nn(live_ref[...], grad_agg) + rest_ref[...].astype(F32)).astype(BF16)


def live_pass(tiles, count, agg, state, up, parts, weights, live, rest):
    feat = agg.shape[1]

    def tile(k):
        return pl.BlockSpec((TILE, feat), lambda i, tiles, count: (tiles[1, k], 0))

    return pl.pallas_call(
        live_kernel,
        grid_spec=pltpu.PrefetchScalarGridSpec(
            num_scalar_prefetch=2,
            grid=(1,),
            in_specs=[tile(0), tile(1)] * 3 + [whole(parts[0].shape)] * 4
            + [whole(w.shape) for w in weights] + [whole(live.shape), whole(rest.shape)],
            out_specs=[whole(rest.shape), whole((2 * TILE, feat)), whole((SUM_ROWS, WIDE))],
            scratch_shapes=scratch(SUM_SHAPES),
        ),
        out_shape=[
            jax.ShapeDtypeStruct(rest.shape, BF16),
            jax.ShapeDtypeStruct((2 * TILE, feat), F32),
            jax.ShapeDtypeStruct((SUM_ROWS, WIDE), F32),
        ],
        compiler_params=params(),
        cost_estimate=cost(1.6e9, 4 << 20, 1 << 19),
        name="live",
    )(tiles, count, agg, agg, state, state, up, up, *parts, *weights, live, rest)


GAP = SUM_ROWS


def pack_kernel(answer_ref, t_ref, s_ref, h_ref, r_ref, before_ref, w2_ref, w1a_ref, w1b_ref, part_ref, out_ref):
    answer = answer_ref[...]
    part_ref[...] = dot_nn(s_ref[...], answer * t_ref[...]).astype(BF16)
    total = before_ref[...] + dot_nn(r_ref[...], answer * h_ref[...])
    used, feat = total.shape
    out_ref[used:, 0:feat] = jnp.zeros((out_ref.shape[0] - used, feat), BF16)
    out_ref[4 * GAP:, feat:feat + TILE] = jnp.zeros((out_ref.shape[0] - 4 * GAP, TILE), BF16)
    out_ref[0:used, 0:feat] = total.astype(BF16)
    layers = (w1a_ref[...] + w1b_ref[...], w2_ref[...])
    parts = []
    for layer in layers:
        parts += [layer[:, :TILE], layer[:, TILE:]]
    out_ref[0:4 * GAP, feat:feat + TILE] = jnp.concatenate(parts, axis=0).astype(BF16)


def pack_sums(answer, table, select, states, select_rel, before, w2, w1a, w1b, rows):
    feat = answer.shape[1]
    return pl.pallas_call(
        pack_kernel,
        in_specs=[VMEM] * 9,
        out_specs=[VMEM, VMEM],
        out_shape=[
            jax.ShapeDtypeStruct((select.shape[0], feat), BF16),
            jax.ShapeDtypeStruct((rows, feat + TILE), BF16),
        ],
        compiler_params=params(),
        cost_estimate=cost(4e8, 4 << 20),
        name="pack_sums",
    )(answer, table, select, states, select_rel, before, w2, w1a, w1b)


def combine_kernel(feat, scale_relations, scale_weights, in_ref, out_ref):
    total = jnp.sum(in_ref[...].astype(F32), axis=0)
    lane = iota(total.shape, 1)
    total = total * jnp.where(lane < feat, scale_relations, scale_weights)
    out_ref[...] = jnp.broadcast_to(total.astype(BF16)[None], out_ref.shape)


def combine(chunks, feat, scale_relations, scale_weights):
    return pl.pallas_call(
        functools.partial(combine_kernel, feat, scale_relations, scale_weights),
        in_specs=[VMEM],
        out_specs=VMEM,
        out_shape=jax.ShapeDtypeStruct(chunks.shape, BF16),
        compiler_params=params(),
        cost_estimate=cost(1e6, 1 << 20),
        name="combine",
    )(chunks)


def unpack_kernel(feat, in_ref, relation_ref, w_in_ref, w_bias_ref, w_out_ref):
    groups = relation_ref.shape[0]
    relation_ref[...] = in_ref[0:groups, 0:feat].astype(F32)
    for layer in range(2):
        at = 2 * layer * GAP
        left = in_ref[at:at + GAP, feat:feat + TILE].astype(F32)
        right = in_ref[at + GAP:at + 2 * GAP, feat:feat + TILE].astype(F32)
        both = jnp.concatenate([left, right], axis=1)
        w_in_ref[layer] = both[0:2 * DIM]
        w_out_ref[layer] = both[2 * DIM:3 * DIM]
        w_bias_ref[layer:layer + 1, :] = both[3 * DIM:3 * DIM + 1]


def unpack(gathered, groups, feat):
    return pl.pallas_call(
        functools.partial(unpack_kernel, feat),
        in_specs=[VMEM],
        out_specs=[VMEM] * 4,
        out_shape=[
            jax.ShapeDtypeStruct((groups, feat), F32),
            jax.ShapeDtypeStruct((2, 2 * DIM, WIDE), F32),
            jax.ShapeDtypeStruct((2, WIDE), F32),
            jax.ShapeDtypeStruct((2, DIM, WIDE), F32),
        ],
        compiler_params=params(),
        cost_estimate=cost(1e6, 2 << 20),
        name="unpack",
    )(gathered)


def final_kernel(tiles_ref, count_ref, quarter_ref, next_ref, live_ref, c0, c1, c2, c3, out_ref):
    tile = 2 * quarter_ref[0] + pl.program_id(0)
    value = next_ref[...]
    for k in range(2):
        rows = slice(k * TILE, (k + 1) * TILE)
        is_live = (tile == tiles_ref[1, k]) & (count_ref[0, 1] > k)
        value = jnp.where(is_live, live_ref[rows, :], value)
    for k in range(2):
        rows = slice(k * TILE, (k + 1) * TILE)
        is_live = (tile == tiles_ref[0, k]) & (count_ref[0, 0] > k)
        source = (c0[rows, :].astype(F32) + c1[rows, :].astype(F32)) + (
            c2[rows, :].astype(F32) + c3[rows, :].astype(F32)
        )
        value = jnp.where(is_live, value + source, value)
    out_ref[...] = value.astype(BF16)


def final_pass(tiles, count, quarter_id, after, live, parts, quarter):
    feat = after.shape[1]
    blocks = quarter // TILE
    return pl.pallas_call(
        final_kernel,
        grid_spec=pltpu.PrefetchScalarGridSpec(
            num_scalar_prefetch=3,
            grid=(blocks,),
            in_specs=[pl.BlockSpec((TILE, feat), lambda i, t, c, q: (q[0] * blocks + i, 0)), whole(live.shape)]
            + [whole(parts[0].shape)] * 4,
            out_specs=pl.BlockSpec((TILE, feat), lambda i, *_: (i, 0)),
        ),
        out_shape=jax.ShapeDtypeStruct((quarter, feat), BF16),
        compiler_params=params(),
        cost_estimate=cost(1e6, 1 << 20),
        name="final",
    )(tiles, count, quarter_id, after, live, *parts)


def shards(state_zero, state_one, aggregate_one, aggregate_two, cotangent, relation_table, update_in, update_bias,
           update_out, frontier_tiles, frontier_count, edge_source, edge_relation, edge_target, edge_owner):
    block_rows, feat = state_zero.shape
    groups = relation_table.shape[0]
    group_size = lax.axis_size("rel")
    peers = lax.axis_size("ent")
    quarter = block_rows // group_size
    edges = edge_source.shape[0]
    capacity = 3 * edges // (2 * peers)
    slots = peers * capacity
    sum_rows = 8 * peers

    def exchange(chunks):
        return lax.all_to_all(chunks, "ent", split_axis=0, concat_axis=0, tiled=True)

    def over_rel(part):
        turned = [
            lax.ppermute(part, "rel", [(i, (i + k) % group_size) for i in range(group_size)])
            for k in range(1, group_size)
        ]
        return [part] + turned

    row = lambda values: values.reshape(1, edges)
    count = jnp.swapaxes(frontier_count, 0, 1)
    weights = (update_in, update_bias, jnp.swapaxes(update_out, 1, 2))
    request, ids = pl.pallas_call(
        functools.partial(slots_kernel, peers),
        in_specs=[VMEM] * 4,
        out_specs=[VMEM] * 2,
        out_shape=[
            jax.ShapeDtypeStruct((peers, 1, 128), F32),
            jax.ShapeDtypeStruct((peers, 128), F32),
        ],
        compiler_params=params(8 << 20),
        cost_estimate=cost(1e8, 1 << 20),
        name="slots",
    )(row(edge_owner), row(edge_target), row(edge_source), row(edge_relation))
    asked = exchange(request)

    upstream_one, picked_two, sums_two = first_pass(
        capacity, aggregate_two, state_one, cotangent, *weights, asked
    )
    answered_two = exchange(picked_two.reshape(peers, capacity, feat)).reshape(slots, feat)
    after, rest, sums_rest, live, *built = rest_pass(
        capacity, frontier_tiles, count, aggregate_one, state_zero, upstream_one, *weights, asked
    )
    edge_table, select_two = tables_two(capacity, frontier_tiles, count, ids, relation_table)
    answered_two, rest, edge_table, select_two = lax.optimization_barrier(
        (answered_two, rest, edge_table, select_two)
    )
    parts = over_rel(contribution(answered_two, edge_table, select_two))
    picked_one, after_live, sums_live = live_pass(
        frontier_tiles, count, aggregate_one, state_zero, upstream_one, parts, built, live, rest
    )
    answered_one = exchange(picked_one.reshape(peers, capacity, feat)).reshape(slots, feat)
    select_one, states_one, select_rel, relation_two = tables_one(
        capacity, frontier_tiles, count, ids, answered_two, state_one, state_zero, groups
    )
    part, packed = pack_sums(
        answered_one, edge_table, select_one, states_one, select_rel, relation_two,
        sums_two, sums_rest, sums_live, sum_rows,
    )
    parts = over_rel(part)
    scale_weights = 1.0 / math.sqrt(block_rows * peers * QUERIES)
    scale_relations = math.sqrt(groups * group_size / (edges * peers * group_size))
    chunks = exchange(packed.reshape(peers, 8, feat + TILE))
    gathered = exchange(combine(chunks, feat, scale_relations, scale_weights)).reshape(sum_rows, feat + TILE)
    quarter_id = lax.axis_index("rel").astype(jnp.int32).reshape(1)
    grad_zero = final_pass(frontier_tiles, count, quarter_id, after, after_live, parts, quarter)
    relation, grad_in, grad_bias, grad_out = unpack(gathered, groups, feat)
    return grad_zero, relation, grad_in, grad_bias, jnp.swapaxes(grad_out, 1, 2)


def solution(mesh):
    in_specs = (
        P("ent", None),
        P("ent", None),
        P("ent", None),
        P("ent", None),
        P("ent", None),
        P("rel", None),
        P(),
        P(),
        P(),
        P(None, "ent"),
        P(None, "ent"),
        P(("ent", "rel")),
        P(("ent", "rel")),
        P(("ent", "rel")),
        P(("ent", "rel"), None),
    )
    out_specs = (P(("ent", "rel"), None), P("rel", None), P(), P(), P())
    return jax.shard_map(shards, mesh=mesh, in_specs=in_specs, out_specs=out_specs, check_vma=False)
```

```python
import functools
import math

import jax
import jax.numpy as jnp
from jax import lax
from jax.experimental import pallas as pl
from jax.experimental.pallas import tpu as pltpu
from jax.sharding import PartitionSpec as P

QUERIES = 8
DIM = 32
TILE = 128
WIDE = 256
HALF_Q = 4
F32 = jnp.float32
BF16 = jnp.bfloat16
VMEM = pl.BlockSpec(memory_space=pltpu.VMEM)
SMEM = pl.BlockSpec(memory_space=pltpu.SMEM)
HBM = pl.BlockSpec(memory_space=pltpu.HBM)


def in_hbm(array):
    return pltpu.with_memory_space_constraint(array, pltpu.HBM)


def iota(shape, dim):
    return lax.broadcasted_iota(jnp.int32, shape, dim)


def dot_nn(a, b):
    return lax.dot_general(a, b, (((1,), (0,)), ((), ())), preferred_element_type=F32)


def dot_nt(a, b):
    return lax.dot_general(a, b, (((1,), (1,)), ((), ())), preferred_element_type=F32)


def dot_tn(a, b):
    return lax.dot_general(a, b, (((0,), (0,)), ((), ())), preferred_element_type=F32)


def params(vmem=20 << 20):
    return pltpu.CompilerParams(vmem_limit_bytes=vmem)


def cost(flops, nbytes, trans=0):
    return pl.CostEstimate(flops=int(flops), bytes_accessed=int(nbytes), transcendentals=int(trans))


def slots_kernel(peers, owner_hbm, target_hbm, source_hbm, relation_hbm, request_ref, ids_ref,
                 owner_ref, target_ref, source_ref, relation_ref, sems):
    pairs = ((owner_hbm, owner_ref), (target_hbm, target_ref), (source_hbm, source_ref), (relation_hbm, relation_ref))
    copies = [pltpu.make_async_copy(a, b, sems.at[i]) for i, (a, b) in enumerate(pairs)]
    for copy in copies:
        copy.start()
    for copy in copies:
        copy.wait()
    edges = owner_ref.shape[1]
    owner = owner_ref[...]
    hit = (iota((peers, edges), 0) == owner).astype(F32)
    hit_low = hit.astype(BF16)
    below = (iota((TILE, TILE), 0) < iota((TILE, TILE), 1)).astype(BF16)
    offset = jnp.zeros((peers, 1), F32)
    pieces = []
    for b in range(edges // TILE):
        block = hit_low[:, b * TILE:(b + 1) * TILE]
        pieces.append(dot_nn(block, below) + offset)
        offset = offset + jnp.sum(hit[:, b * TILE:(b + 1) * TILE], axis=1, keepdims=True)
    before = jnp.concatenate(pieces, axis=1)
    earlier = jnp.sum(before * hit, axis=0, keepdims=True).astype(jnp.int32)
    place = (iota((32, edges), 0) == earlier).astype(F32)

    def spread(values):
        high = lax.shift_right_logical(values, 5)
        low = values & 31
        return [place * high.astype(F32), place * low.astype(F32)]

    zero = jnp.zeros((64, edges), F32)
    first = jnp.concatenate(spread(target_ref[...]) + [zero], axis=0).astype(BF16)
    request_ref[:, 0, :] = dot_nt(hit_low, first)
    second = jnp.concatenate(
        spread(source_ref[...] + 1) + spread(relation_ref[...] + 1), axis=0
    ).astype(BF16)
    ids_ref[...] = dot_nt(hit_low, second)


def slot_columns(table, capacity, bases):
    peers = table.shape[0]
    slots = peers * capacity
    row = iota((slots, peers), 0)
    start = iota((slots, peers), 1) * capacity
    expand = ((row >= start) & (row < start + capacity)).astype(BF16)
    spread = dot_nn(expand, table.astype(BF16))
    row = iota((slots, 128), 0)
    group = ((row.astype(F32) + 0.5) * (1.0 / capacity)).astype(jnp.int32)
    place = row - group * capacity
    lane = iota((slots, 128), 1)
    columns = []
    for base in bases:
        weight = jnp.where(lane == place + base, 32.0, 0.0) + jnp.where(
            lane == place + (base + 32), 1.0, 0.0
        )
        columns.append(jnp.sum(spread * weight, axis=1, keepdims=True).astype(jnp.int32))
    return columns


def compact_column(column, tiles, count):
    tile = lax.shift_right_arithmetic(column, 7)
    inner = column & 127
    result = jnp.full(column.shape, -1, jnp.int32)
    for k in range(len(tiles)):
        live = (tile == tiles[k]) & (count > k)
        result = jnp.where(live, inner + k * TILE, result)
    return result


def onehot(column, width):
    return (iota((column.shape[0], width), 1) == column).astype(F32).astype(BF16)


def build_weights(layer, w_in_ref, w_bias_ref, w_out_ref, wx_ref, wu_ref, wb_ref):
    wx_ref[...] = jnp.zeros_like(wx_ref)
    wu_ref[...] = jnp.zeros_like(wu_ref)
    for q in range(HALF_Q):
        rows, cols = slice(q * DIM, (q + 1) * DIM), slice(q * WIDE, (q + 1) * WIDE)
        low = slice(TILE + q * DIM, TILE + (q + 1) * DIM)
        wx_ref[rows, cols] = w_in_ref[layer, 0:DIM, :]
        wx_ref[low, cols] = w_in_ref[layer, DIM:2 * DIM, :]
        wu_ref[rows, cols] = w_out_ref[layer]
        wb_ref[:, cols] = w_bias_ref[layer:layer + 1, :]


def mlp_half(s, agg, state, up_low, wx, wu, bias, acc_in, acc_out, acc_bias):
    lanes = slice(s * TILE, (s + 1) * TILE)
    x = jnp.concatenate([agg[:, lanes], state[:, lanes]], axis=1)
    up = up_low[:, lanes]
    pre = dot_nn(x, wx[...]) + bias[...]
    gate = 0.5 * jnp.tanh(0.5 * pre) + 0.5
    act = pre * gate
    slope = gate + act * (1.0 - gate)
    grad_pre = dot_nn(up, wu[...]) * slope
    low = grad_pre.astype(BF16)
    acc_in[...] += dot_tn(x, low)
    acc_out[...] += dot_tn(up, act.astype(BF16))
    acc_bias[...] += jnp.sum(grad_pre, axis=0, keepdims=True)
    return dot_nt(low, wx[...])


def store_sums(acc_in, acc_out, acc_bias, sums_ref):
    first = jnp.zeros((DIM, WIDE), F32)
    second = jnp.zeros((DIM, WIDE), F32)
    third = jnp.zeros((DIM, WIDE), F32)
    fourth = jnp.zeros((1, WIDE), F32)
    for q in range(HALF_Q):
        cols = slice(q * WIDE, (q + 1) * WIDE)
        first += acc_in[q * DIM:(q + 1) * DIM, cols]
        second += acc_in[TILE + q * DIM:TILE + (q + 1) * DIM, cols]
        third += acc_out[q * DIM:(q + 1) * DIM, cols]
        fourth += acc_bias[:, cols]
    sums_ref[0:DIM, :] = first
    sums_ref[DIM:2 * DIM, :] = second
    sums_ref[2 * DIM:3 * DIM, :] = third
    sums_ref[3 * DIM:3 * DIM + 8, :] = jnp.concatenate([fourth, jnp.zeros((7, WIDE), F32)], axis=0)


def clear(acc_in, acc_out, acc_bias):
    acc_in[...] = jnp.zeros_like(acc_in)
    acc_out[...] = jnp.zeros_like(acc_out)
    acc_bias[...] = jnp.zeros_like(acc_bias)


WEIGHT_SHAPES = [
    ((2 * TILE, HALF_Q * WIDE), BF16),
    ((TILE, HALF_Q * WIDE), BF16),
    ((1, HALF_Q * WIDE), F32),
]
SUM_SHAPES = [
    ((2 * TILE, HALF_Q * WIDE), F32),
    ((TILE, HALF_Q * WIDE), F32),
    ((1, HALF_Q * WIDE), F32),
]
SUM_ROWS = 3 * DIM + 8


def scratch(shapes):
    return [pltpu.VMEM(shape, dtype) for shape, dtype in shapes]


def whole(shape):
    return pl.BlockSpec(shape, lambda i, *_: (0,) * len(shape))


def pick_rows(asked, grad_agg, picked_ref, chunks=4):
    rows, slots = grad_agg.shape[0], asked.shape[0]
    step = slots // chunks
    for c in range(chunks):
        part = slice(c * step, (c + 1) * step)
        picked_ref[part, :] = dot_nn(onehot(asked[part], rows), grad_agg[...]).astype(BF16)


def dense_step(step, agg_ref, state_ref, up, up_low, wx, wu, wb, acc_in, acc_out, acc_bias, grad_agg, next_ref):
    rows = agg_ref.shape[0]
    aggs, states = [], []
    for s in range(2):
        grad_x = mlp_half(s, agg_ref[...], state_ref[...], up_low, wx, wu, wb, acc_in, acc_out, acc_bias)
        aggs.append(grad_x[:, :TILE])
        states.append(grad_x[:, TILE:])
    grad_agg[pl.ds(pl.multiple_of(step * rows, rows), rows), :] = jnp.concatenate(aggs, axis=1).astype(BF16)
    next_ref[...] = up + jnp.concatenate(states, axis=1)


def first_kernel(capacity, blocks, agg_hbm, state_hbm, up_hbm, w_in_ref, w_bias_ref, w_out_ref, asked_ref,
                 next_ref, picked_ref, sums_ref, wx, wu, wb, acc_in, acc_out, acc_bias, grad_agg,
                 agg_buf, state_buf, up_buf, sems):
    rows = agg_hbm.shape[0] // blocks

    def copies(step):
        part = pl.ds(pl.multiple_of(step * rows, rows), rows)
        pairs = ((agg_hbm, agg_buf), (state_hbm, state_buf), (up_hbm, up_buf))
        return [pltpu.make_async_copy(a.at[part], b.at[part], sems.at[step, i]) for i, (a, b) in enumerate(pairs)]

    for step in range(blocks):
        for copy in copies(step):
            copy.start()
    build_weights(1, w_in_ref, w_bias_ref, w_out_ref, wx, wu, wb)
    clear(acc_in, acc_out, acc_bias)

    @pl.loop(0, blocks)
    def _(step):
        for copy in copies(step):
            copy.wait()
        part = pl.ds(pl.multiple_of(step * rows, rows), rows)
        up_low = up_buf[part, :]
        dense_step(step, agg_buf.at[part], state_buf.at[part], up_low.astype(F32), up_low, wx, wu, wb,
                   acc_in, acc_out, acc_bias, grad_agg, next_ref.at[part])

    store_sums(acc_in, acc_out, acc_bias, sums_ref)
    asked = slot_columns(asked_ref[:, 0, :], capacity, (0,))[0]
    pick_rows(asked, grad_agg, picked_ref)


def first_pass(capacity, agg, state, up, w_in, w_bias, w_out, asked):
    rows, feat = agg.shape
    slots = asked.shape[0] * capacity
    blocks = rows // 256
    return pl.pallas_call(
        functools.partial(first_kernel, capacity, blocks),
        in_specs=[HBM, HBM, HBM, VMEM, VMEM, VMEM, VMEM],
        out_specs=[VMEM] * 3,
        out_shape=[
            jax.ShapeDtypeStruct((rows, feat), F32),
            jax.ShapeDtypeStruct((slots, feat), BF16),
            jax.ShapeDtypeStruct((SUM_ROWS, WIDE), F32),
        ],
        scratch_shapes=scratch(WEIGHT_SHAPES + SUM_SHAPES)
        + [pltpu.VMEM((rows, feat), BF16)] * 4
        + [pltpu.SemaphoreType.DMA((blocks, 3))],
        compiler_params=params(),
        cost_estimate=cost(5.4e9, 4 << 20, 2 << 20),
        name="first",
    )(in_hbm(agg), in_hbm(state), in_hbm(up), w_in, w_bias, w_out, asked)


def rest_kernel(capacity, tiles_ref, count_ref, agg_ref, state_ref, up_ref, w_in_ref, w_bias_ref, w_out_ref,
                asked_ref, next_ref, picked_ref, sums_ref, live_ref, wx, wu, wb,
                acc_in, acc_out, acc_bias, grad_agg):
    step = pl.program_id(0)
    rows = agg_ref.shape[0]
    count = count_ref[0, 1]

    @pl.when(step == 0)
    def _():
        build_weights(0, w_in_ref, w_bias_ref, w_out_ref, wx, wu, wb)
        clear(acc_in, acc_out, acc_bias)

    up = up_ref[...]
    tile = lax.shift_right_logical(iota((rows, 1), 0) + step * rows, 7)
    dead = (tile == tiles_ref[1, 0]) | ((tile == tiles_ref[1, 1]) & (count > 1))
    up_low = jnp.where(dead, 0.0, up).astype(BF16)
    dense_step(step, agg_ref, state_ref, up, up_low, wx, wu, wb, acc_in, acc_out, acc_bias, grad_agg, next_ref)

    @pl.when(step == pl.num_programs(0) - 1)
    def _():
        store_sums(acc_in, acc_out, acc_bias, sums_ref)
        asked = slot_columns(asked_ref[:, 0, :], capacity, (0,))[0]
        live_ref[...] = onehot(compact_column(asked, (tiles_ref[1, 0], tiles_ref[1, 1]), count), 2 * TILE)
        pick_rows(asked, grad_agg, picked_ref)


def rest_pass(capacity, tiles, count, agg, state, up, w_in, w_bias, w_out, asked):
    rows, feat = agg.shape
    slots = asked.shape[0] * capacity
    block = 256
    row_spec = pl.BlockSpec((block, feat), lambda i: (i, 0))
    return pl.pallas_call(
        functools.partial(rest_kernel, capacity),
        grid=(rows // block,),
        in_specs=[SMEM, SMEM, row_spec, row_spec, row_spec, whole(w_in.shape), whole(w_bias.shape),
                  whole(w_out.shape), whole(asked.shape)],
        out_specs=[row_spec, whole((slots, feat)), whole((SUM_ROWS, WIDE)), whole((slots, 2 * TILE))],
        out_shape=[
            jax.ShapeDtypeStruct((rows, feat), F32),
            jax.ShapeDtypeStruct((slots, feat), BF16),
            jax.ShapeDtypeStruct((SUM_ROWS, WIDE), F32),
            jax.ShapeDtypeStruct((slots, 2 * TILE), BF16),
        ],
        scratch_shapes=scratch(WEIGHT_SHAPES + SUM_SHAPES) + [pltpu.VMEM((rows, feat), BF16)],
        compiler_params=params(),
        cost_estimate=cost(5.4e9, 4 << 20, 2 << 20),
        name="rest",
    )(tiles, count, agg, state, up, w_in, w_bias, w_out, asked)


def as_row(column):
    return jnp.broadcast_to(column.astype(F32), (column.shape[0], TILE)).T[0:8].astype(jnp.int32)


def onehot_rows(row, width):
    return (iota((width, row.shape[1]), 0) == row).astype(F32).astype(BF16)


def tables_two_kernel(capacity, tiles_ref, count_ref, ids_ref, table_ref, t_ref, rows_ref):
    source, relation = slot_columns(ids_ref[...], capacity, (0, 64))
    width = -(-table_ref.shape[0] // TILE) * TILE
    pad = width - table_ref.shape[0]
    table = jnp.concatenate([table_ref[...], jnp.zeros((pad, table_ref.shape[1]), BF16)], axis=0)
    t_ref[...] = dot_nn(onehot(relation - 1, width), table).astype(BF16)
    rows_ref[0] = as_row(relation - 1)
    for hop in range(2):
        column = compact_column(source - 1, (tiles_ref[hop, 0], tiles_ref[hop, 1]), count_ref[0, hop])
        rows_ref[1 + hop] = as_row(column)


def tables_two(capacity, tiles, count, ids, table):
    feat = table.shape[1]
    slots = ids.shape[0] * capacity
    return pl.pallas_call(
        functools.partial(tables_two_kernel, capacity),
        in_specs=[SMEM, SMEM, VMEM, VMEM],
        out_specs=[VMEM, VMEM],
        out_shape=[
            jax.ShapeDtypeStruct((slots, feat), BF16),
            jax.ShapeDtypeStruct((3, 8, slots), jnp.int32),
        ],
        compiler_params=params(),
        cost_estimate=cost(1e9, 2 << 20),
        name="tables_two",
    )(tiles, count, ids, table)


def tables_one_kernel(capacity, tiles_ref, count_ref, ids_ref, rows_ref, answer_ref, one_a, one_b, zero_a, zero_b,
                      h_ref, total_ref):
    source = slot_columns(ids_ref[...], capacity, (0,))[0] - 1
    columns = [
        compact_column(source, (tiles_ref[hop, 0], tiles_ref[hop, 1]), count_ref[0, hop]) for hop in range(2)
    ]
    h_ref[...] = dot_nn(onehot(columns[0], 2 * TILE), jnp.concatenate([zero_a[...], zero_b[...]], axis=0)).astype(BF16)
    states = dot_nn(onehot(columns[1], 2 * TILE), jnp.concatenate([one_a[...], one_b[...]], axis=0)).astype(BF16)
    total_ref[...] = dot_nn(onehot_rows(rows_ref[0, 0:1, :], total_ref.shape[0]), answer_ref[...] * states)


def tables_one(capacity, tiles, count, ids, rows, answer, state_one, state_zero, groups):
    slots, feat = answer.shape
    width = -(-groups // TILE) * TILE

    def tile(hop, k):
        return pl.BlockSpec((TILE, feat), lambda i, tiles, count: (tiles[hop, k], 0))

    return pl.pallas_call(
        functools.partial(tables_one_kernel, capacity),
        grid_spec=pltpu.PrefetchScalarGridSpec(
            num_scalar_prefetch=2,
            grid=(1,),
            in_specs=[whole(ids.shape), whole(rows.shape), whole(answer.shape), tile(1, 0), tile(1, 1), tile(0, 0),
                      tile(0, 1)],
            out_specs=[whole((slots, feat)), whole((width, feat))],
        ),
        out_shape=[
            jax.ShapeDtypeStruct((slots, feat), BF16),
            jax.ShapeDtypeStruct((width, feat), F32),
        ],
        compiler_params=params(),
        cost_estimate=cost(2e9, 4 << 20),
        name="tables_one",
    )(tiles, count, ids, rows, answer, state_one, state_one, state_zero, state_zero)


def contribution_kernel(answer_ref, t_ref, rows_ref, out_ref):
    select = onehot_rows(rows_ref[2, 0:1, :], 2 * TILE)
    out_ref[...] = dot_nn(select, answer_ref[...] * t_ref[...]).astype(BF16)


def contribution(answer, table, rows):
    return pl.pallas_call(
        contribution_kernel,
        in_specs=[VMEM] * 3,
        out_specs=VMEM,
        out_shape=jax.ShapeDtypeStruct((2 * TILE, answer.shape[1]), BF16),
        compiler_params=params(8 << 20),
        cost_estimate=cost(2e8, 3 << 20),
        name="contribution",
    )(answer, table, rows)


def live_kernel(tiles_ref, count_ref, agg_a, agg_b, state_a, state_b, up_a, up_b, c0, c1, c2, c3,
                w_in_ref, w_bias_ref, w_out_ref, live_ref, rest_ref, picked_ref, next_ref, sums_ref,
                wx, wu, wb, acc_in, acc_out, acc_bias):
    build_weights(0, w_in_ref, w_bias_ref, w_out_ref, wx, wu, wb)
    clear(acc_in, acc_out, acc_bias)
    source = (c0[...].astype(F32) + c1[...].astype(F32)) + (c2[...].astype(F32) + c3[...].astype(F32))
    up = jnp.concatenate([up_a[...], up_b[...]], axis=0) + source
    keep = (iota((2 * TILE, 1), 0) < TILE) | (count_ref[0, 1] > 1)
    up_low = jnp.where(keep, up, 0.0).astype(BF16)
    agg = jnp.concatenate([agg_a[...], agg_b[...]], axis=0)
    state = jnp.concatenate([state_a[...], state_b[...]], axis=0)
    aggs, states = [], []
    for s in range(2):
        grad_x = mlp_half(s, agg, state, up_low, wx, wu, wb, acc_in, acc_out, acc_bias)
        aggs.append(grad_x[:, :TILE])
        states.append(grad_x[:, TILE:])
    grad_agg = jnp.concatenate(aggs, axis=1).astype(BF16)
    next_ref[...] = up + jnp.concatenate(states, axis=1)
    store_sums(acc_in, acc_out, acc_bias, sums_ref)
    picked_ref[...] = (dot_nn(live_ref[...], grad_agg) + rest_ref[...].astype(F32)).astype(BF16)


def live_pass(tiles, count, agg, state, up, parts, weights, live, rest):
    feat = agg.shape[1]

    def tile(k):
        return pl.BlockSpec((TILE, feat), lambda i, tiles, count: (tiles[1, k], 0))

    return pl.pallas_call(
        live_kernel,
        grid_spec=pltpu.PrefetchScalarGridSpec(
            num_scalar_prefetch=2,
            grid=(1,),
            in_specs=[tile(0), tile(1)] * 3 + [whole(parts[0].shape)] * 4
            + [whole(w.shape) for w in weights] + [whole(live.shape), whole(rest.shape)],
            out_specs=[whole(rest.shape), whole((2 * TILE, feat)), whole((SUM_ROWS, WIDE))],
            scratch_shapes=scratch(WEIGHT_SHAPES + SUM_SHAPES),
        ),
        out_shape=[
            jax.ShapeDtypeStruct(rest.shape, BF16),
            jax.ShapeDtypeStruct((2 * TILE, feat), F32),
            jax.ShapeDtypeStruct((SUM_ROWS, WIDE), F32),
        ],
        compiler_params=params(),
        cost_estimate=cost(1.6e9, 4 << 20, 1 << 19),
        name="live",
    )(tiles, count, agg, agg, state, state, up, up, *parts, *weights, live, rest)


GAP = SUM_ROWS


def pack_kernel(answer_ref, t_ref, h_ref, rows_ref, before_ref, w2_ref, w1a_ref, w1b_ref, part_ref, out_ref):
    answer = answer_ref[...]
    part_ref[...] = dot_nn(onehot_rows(rows_ref[1, 0:1, :], 2 * TILE), answer * t_ref[...]).astype(BF16)
    select = onehot_rows(rows_ref[0, 0:1, :], before_ref.shape[0])
    total = before_ref[...] + dot_nn(select, answer * h_ref[...])
    used, feat = total.shape
    out_ref[used:, 0:feat] = jnp.zeros((out_ref.shape[0] - used, feat), BF16)
    out_ref[4 * GAP:, feat:feat + TILE] = jnp.zeros((out_ref.shape[0] - 4 * GAP, TILE), BF16)
    out_ref[0:used, 0:feat] = total.astype(BF16)
    layers = (w1a_ref[...] + w1b_ref[...], w2_ref[...])
    parts = []
    for layer in layers:
        parts += [layer[:, :TILE], layer[:, TILE:]]
    out_ref[0:4 * GAP, feat:feat + TILE] = jnp.concatenate(parts, axis=0).astype(BF16)


def pack_sums(answer, table, states, ids, before, w2, w1a, w1b, rows):
    feat = answer.shape[1]
    return pl.pallas_call(
        pack_kernel,
        in_specs=[VMEM] * 8,
        out_specs=[VMEM, VMEM],
        out_shape=[
            jax.ShapeDtypeStruct((2 * TILE, feat), BF16),
            jax.ShapeDtypeStruct((rows, feat + TILE), BF16),
        ],
        compiler_params=params(),
        cost_estimate=cost(4e8, 4 << 20),
        name="pack_sums",
    )(answer, table, states, ids, before, w2, w1a, w1b)


def combine_kernel(feat, scale_relations, scale_weights, in_ref, out_ref):
    total = jnp.sum(in_ref[...].astype(F32), axis=0)
    lane = iota(total.shape, 1)
    total = total * jnp.where(lane < feat, scale_relations, scale_weights)
    out_ref[...] = jnp.broadcast_to(total.astype(BF16)[None], out_ref.shape)


def combine(chunks, feat, scale_relations, scale_weights):
    return pl.pallas_call(
        functools.partial(combine_kernel, feat, scale_relations, scale_weights),
        in_specs=[VMEM],
        out_specs=VMEM,
        out_shape=jax.ShapeDtypeStruct(chunks.shape, BF16),
        compiler_params=params(),
        cost_estimate=cost(1e6, 1 << 20),
        name="combine",
    )(chunks)


def unpack_kernel(feat, in_ref, relation_ref, w_in_ref, w_bias_ref, w_out_ref):
    groups = relation_ref.shape[0]
    relation_ref[...] = in_ref[0:groups, 0:feat].astype(F32)
    for layer in range(2):
        at = 2 * layer * GAP
        left = in_ref[at:at + GAP, feat:feat + TILE].astype(F32)
        right = in_ref[at + GAP:at + 2 * GAP, feat:feat + TILE].astype(F32)
        both = jnp.concatenate([left, right], axis=1)
        w_in_ref[layer] = both[0:2 * DIM]
        w_out_ref[layer] = both[2 * DIM:3 * DIM]
        w_bias_ref[layer:layer + 1, :] = both[3 * DIM:3 * DIM + 1]


def unpack(gathered, groups, feat):
    return pl.pallas_call(
        functools.partial(unpack_kernel, feat),
        in_specs=[VMEM],
        out_specs=[VMEM] * 4,
        out_shape=[
            jax.ShapeDtypeStruct((groups, feat), F32),
            jax.ShapeDtypeStruct((2, 2 * DIM, WIDE), F32),
            jax.ShapeDtypeStruct((2, WIDE), F32),
            jax.ShapeDtypeStruct((2, DIM, WIDE), F32),
        ],
        compiler_params=params(),
        cost_estimate=cost(1e6, 2 << 20),
        name="unpack",
    )(gathered)


def final_kernel(tiles_ref, count_ref, quarter_ref, next_ref, live_ref, c0, c1, c2, c3, out_ref):
    tile = 2 * quarter_ref[0] + pl.program_id(0)
    value = next_ref[...]
    for k in range(2):
        rows = slice(k * TILE, (k + 1) * TILE)
        is_live = (tile == tiles_ref[1, k]) & (count_ref[0, 1] > k)
        value = jnp.where(is_live, live_ref[rows, :], value)
    for k in range(2):
        rows = slice(k * TILE, (k + 1) * TILE)
        is_live = (tile == tiles_ref[0, k]) & (count_ref[0, 0] > k)
        source = (c0[rows, :].astype(F32) + c1[rows, :].astype(F32)) + (
            c2[rows, :].astype(F32) + c3[rows, :].astype(F32)
        )
        value = jnp.where(is_live, value + source, value)
    out_ref[...] = value.astype(BF16)


def final_pass(tiles, count, quarter_id, after, live, parts, quarter):
    feat = after.shape[1]
    blocks = quarter // TILE
    return pl.pallas_call(
        final_kernel,
        grid_spec=pltpu.PrefetchScalarGridSpec(
            num_scalar_prefetch=3,
            grid=(blocks,),
            in_specs=[pl.BlockSpec((TILE, feat), lambda i, t, c, q: (q[0] * blocks + i, 0)), whole(live.shape)]
            + [whole(parts[0].shape)] * 4,
            out_specs=pl.BlockSpec((TILE, feat), lambda i, *_: (i, 0)),
        ),
        out_shape=jax.ShapeDtypeStruct((quarter, feat), BF16),
        compiler_params=params(),
        cost_estimate=cost(1e6, 1 << 20),
        name="final",
    )(tiles, count, quarter_id, after, live, *parts)


def shards(state_zero, state_one, aggregate_one, aggregate_two, cotangent, relation_table, update_in, update_bias,
           update_out, frontier_tiles, frontier_count, edge_source, edge_relation, edge_target, edge_owner):
    block_rows, feat = state_zero.shape
    groups = relation_table.shape[0]
    group_size = lax.axis_size("rel")
    peers = lax.axis_size("ent")
    quarter = block_rows // group_size
    edges = edge_source.shape[0]
    capacity = 3 * edges // (2 * peers)
    slots = peers * capacity
    sum_rows = 8 * peers

    def exchange(chunks):
        return lax.all_to_all(chunks, "ent", split_axis=0, concat_axis=0, tiled=True)

    def over_rel(part):
        turned = [
            lax.ppermute(part, "rel", [(i, (i + k) % group_size) for i in range(group_size)])
            for k in range(1, group_size)
        ]
        return [part] + turned

    row = lambda values: values.reshape(1, edges)
    count = jnp.swapaxes(frontier_count, 0, 1)
    weights = (update_in, update_bias, jnp.swapaxes(update_out, 1, 2))
    request, ids = pl.pallas_call(
        functools.partial(slots_kernel, peers),
        in_specs=[HBM] * 4,
        out_specs=[VMEM] * 2,
        out_shape=[
            jax.ShapeDtypeStruct((peers, 1, 128), F32),
            jax.ShapeDtypeStruct((peers, 128), F32),
        ],
        scratch_shapes=[pltpu.VMEM((1, edges), jnp.int32)] * 4 + [pltpu.SemaphoreType.DMA((4,))],
        compiler_params=params(8 << 20),
        cost_estimate=cost(1e8, 1 << 20),
        name="slots",
    )(*(in_hbm(row(values)) for values in (edge_owner, edge_target, edge_source, edge_relation)))
    asked = exchange(request)

    upstream_one, picked_two, sums_two = first_pass(
        capacity, aggregate_two, state_one, cotangent, *weights, asked
    )
    sums_two = in_hbm(sums_two)
    answered_two = exchange(picked_two.reshape(peers, capacity, feat)).reshape(slots, feat)
    after, rest, sums_rest, live = rest_pass(
        capacity, frontier_tiles, count, aggregate_one, state_zero, upstream_one, *weights, asked
    )
    edge_table, rows = tables_two(capacity, frontier_tiles, count, ids, relation_table)
    answered_two, rest, edge_table, rows = lax.optimization_barrier((answered_two, rest, edge_table, rows))
    parts = over_rel(contribution(answered_two, edge_table, rows))
    states_one, relation_two = tables_one(
        capacity, frontier_tiles, count, ids, rows, answered_two, state_one, state_zero, groups
    )
    parts[0], rest, states_one, relation_two = lax.optimization_barrier((parts[0], rest, states_one, relation_two))
    picked_one, after_live, sums_live = live_pass(
        frontier_tiles, count, aggregate_one, state_zero, upstream_one, parts, weights, live, rest
    )
    answered_one = exchange(picked_one.reshape(peers, capacity, feat)).reshape(slots, feat)
    part, packed = pack_sums(
        answered_one, edge_table, states_one, rows, relation_two, sums_two, sums_rest, sums_live, sum_rows
    )
    parts = over_rel(part)
    scale_weights = 1.0 / math.sqrt(block_rows * peers * QUERIES)
    scale_relations = math.sqrt(groups * group_size / (edges * peers * group_size))
    chunks = exchange(packed.reshape(peers, 8, feat + TILE))
    gathered = exchange(combine(chunks, feat, scale_relations, scale_weights)).reshape(sum_rows, feat + TILE)
    quarter_id = lax.axis_index("rel").astype(jnp.int32).reshape(1)
    grad_zero = final_pass(frontier_tiles, count, quarter_id, after, after_live, parts, quarter)
    relation, grad_in, grad_bias, grad_out = unpack(gathered, groups, feat)
    return grad_zero, relation, grad_in, grad_bias, jnp.swapaxes(grad_out, 1, 2)


def solution(mesh):
    in_specs = (
        P("ent", None),
        P("ent", None),
        P("ent", None),
        P("ent", None),
        P("ent", None),
        P("rel", None),
        P(),
        P(),
        P(),
        P(None, "ent"),
        P(None, "ent"),
        P(("ent", "rel")),
        P(("ent", "rel")),
        P(("ent", "rel")),
        P(("ent", "rel"), None),
    )
    out_specs = (P(("ent", "rel"), None), P("rel", None), P(), P(), P())
    return jax.shard_map(shards, mesh=mesh, in_specs=in_specs, out_specs=out_specs, check_vma=False)
```

```python
import functools
import math

import jax
import jax.numpy as jnp
from jax import lax
from jax.experimental import pallas as pl
from jax.experimental.pallas import tpu as pltpu
from jax.sharding import PartitionSpec as P

QUERIES = 8
DIM = 32
TILE = 128
WIDE = 256
HALF_Q = 4
F32 = jnp.float32
BF16 = jnp.bfloat16
VMEM = pl.BlockSpec(memory_space=pltpu.VMEM)
SMEM = pl.BlockSpec(memory_space=pltpu.SMEM)
HBM = pl.BlockSpec(memory_space=pltpu.HBM)


def in_hbm(array):
    return pltpu.with_memory_space_constraint(array, pltpu.HBM)


def iota(shape, dim):
    return lax.broadcasted_iota(jnp.int32, shape, dim)


def dot_nn(a, b):
    return lax.dot_general(a, b, (((1,), (0,)), ((), ())), preferred_element_type=F32)


def dot_nt(a, b):
    return lax.dot_general(a, b, (((1,), (1,)), ((), ())), preferred_element_type=F32)


def dot_tn(a, b):
    return lax.dot_general(a, b, (((0,), (0,)), ((), ())), preferred_element_type=F32)


def params(vmem=20 << 20):
    return pltpu.CompilerParams(vmem_limit_bytes=vmem)


def cost(flops, nbytes, trans=0):
    return pl.CostEstimate(flops=int(flops), bytes_accessed=int(nbytes), transcendentals=int(trans))


def slots_kernel(peers, owner_hbm, target_hbm, source_hbm, relation_hbm, request_ref, ids_ref,
                 owner_ref, target_ref, source_ref, relation_ref, sems):
    pairs = ((owner_hbm, owner_ref), (target_hbm, target_ref), (source_hbm, source_ref), (relation_hbm, relation_ref))
    copies = [pltpu.make_async_copy(a, b, sems.at[i]) for i, (a, b) in enumerate(pairs)]
    for copy in copies:
        copy.start()
    for copy in copies:
        copy.wait()
    edges = owner_ref.shape[1]
    owner = owner_ref[...]
    hit = (iota((peers, edges), 0) == owner).astype(F32)
    hit_low = hit.astype(BF16)
    below = (iota((TILE, TILE), 0) < iota((TILE, TILE), 1)).astype(BF16)
    offset = jnp.zeros((peers, 1), F32)
    pieces = []
    for b in range(edges // TILE):
        block = hit_low[:, b * TILE:(b + 1) * TILE]
        pieces.append(dot_nn(block, below) + offset)
        offset = offset + jnp.sum(hit[:, b * TILE:(b + 1) * TILE], axis=1, keepdims=True)
    before = jnp.concatenate(pieces, axis=1)
    earlier = jnp.sum(before * hit, axis=0, keepdims=True).astype(jnp.int32)
    place = (iota((32, edges), 0) == earlier).astype(F32)

    def spread(values):
        high = lax.shift_right_logical(values, 5)
        low = values & 31
        return [place * high.astype(F32), place * low.astype(F32)]

    zero = jnp.zeros((64, edges), F32)
    first = jnp.concatenate(spread(target_ref[...]) + [zero], axis=0).astype(BF16)
    request_ref[:, 0, :] = dot_nt(hit_low, first)
    second = jnp.concatenate(
        spread(source_ref[...] + 1) + spread(relation_ref[...] + 1), axis=0
    ).astype(BF16)
    ids_ref[...] = dot_nt(hit_low, second)


def slot_columns(table, capacity, bases):
    peers = table.shape[0]
    slots = peers * capacity
    row = iota((slots, peers), 0)
    start = iota((slots, peers), 1) * capacity
    expand = ((row >= start) & (row < start + capacity)).astype(BF16)
    spread = dot_nn(expand, table.astype(BF16))
    row = iota((slots, 128), 0)
    group = ((row.astype(F32) + 0.5) * (1.0 / capacity)).astype(jnp.int32)
    place = row - group * capacity
    lane = iota((slots, 128), 1)
    columns = []
    for base in bases:
        weight = jnp.where(lane == place + base, 32.0, 0.0) + jnp.where(
            lane == place + (base + 32), 1.0, 0.0
        )
        columns.append(jnp.sum(spread * weight, axis=1, keepdims=True).astype(jnp.int32))
    return columns


def compact_column(column, tiles, count):
    tile = lax.shift_right_arithmetic(column, 7)
    inner = column & 127
    result = jnp.full(column.shape, -1, jnp.int32)
    for k in range(len(tiles)):
        live = (tile == tiles[k]) & (count > k)
        result = jnp.where(live, inner + k * TILE, result)
    return result


def onehot(column, width):
    return (iota((column.shape[0], width), 1) == column).astype(F32).astype(BF16)


def build_weights(layer, w_in_ref, w_bias_ref, w_out_ref, wx_ref, wu_ref, wb_ref):
    wx_ref[...] = jnp.zeros_like(wx_ref)
    wu_ref[...] = jnp.zeros_like(wu_ref)
    for q in range(HALF_Q):
        rows, cols = slice(q * DIM, (q + 1) * DIM), slice(q * WIDE, (q + 1) * WIDE)
        low = slice(TILE + q * DIM, TILE + (q + 1) * DIM)
        wx_ref[rows, cols] = 0.5 * w_in_ref[layer, 0:DIM, :]
        wx_ref[low, cols] = 0.5 * w_in_ref[layer, DIM:2 * DIM, :]
        wu_ref[rows, cols] = w_out_ref[layer]
        wb_ref[:, cols] = 0.5 * w_bias_ref[layer:layer + 1, :]


def mlp_half(s, agg, state, up_low, wx, wu, bias, acc_in, acc_out):
    lanes = slice(s * TILE, (s + 1) * TILE)
    x = jnp.concatenate([agg[:, lanes], state[:, lanes]], axis=1)
    up = up_low[:, lanes]
    x_turned, up_turned = x.T, up.T
    half = dot_nn(x, wx[...]) + bias[...]
    bend = jnp.tanh(half)
    above = 1.0 + bend
    act_low = (half * above).astype(BF16)
    slope = above * (1.0 + half * (1.0 - bend))
    low = (dot_nn(up, wu[...]) * slope).astype(BF16)
    ones = jnp.ones((16, x.shape[0]), BF16)
    for q in range(HALF_Q):
        cols = slice(q * WIDE, (q + 1) * WIDE)
        rows = slice(q * DIM, (q + 1) * DIM)
        low_rows = slice(TILE + q * DIM, TILE + (q + 1) * DIM)
        own = jnp.concatenate([x_turned[rows], x_turned[low_rows], ones], axis=0)
        acc_in[...] += dot_nn(own, low[:, cols])
        acc_out[...] += dot_nn(up_turned[rows], act_low[:, cols])
    return dot_nt(low, wx[...])


def store_sums(acc_in, acc_out, sums_ref):
    sums_ref[0:2 * DIM, :] = 0.5 * acc_in[0:2 * DIM, :]
    sums_ref[2 * DIM:3 * DIM, :] = acc_out[...]
    sums_ref[3 * DIM:3 * DIM + 8, :] = 0.5 * acc_in[2 * DIM:2 * DIM + 8, :]


def clear(acc_in, acc_out):
    acc_in[...] = jnp.zeros_like(acc_in)
    acc_out[...] = jnp.zeros_like(acc_out)


WEIGHT_SHAPES = [
    ((2 * TILE, HALF_Q * WIDE), BF16),
    ((TILE, HALF_Q * WIDE), BF16),
    ((1, HALF_Q * WIDE), F32),
]
SUM_SHAPES = [((2 * DIM + 16, WIDE), F32), ((DIM, WIDE), F32)]
SUM_ROWS = 3 * DIM + 8


def scratch(shapes):
    return [pltpu.VMEM(shape, dtype) for shape, dtype in shapes]


def whole(shape):
    return pl.BlockSpec(shape, lambda i, *_: (0,) * len(shape))


def pick_rows(asked, grad_agg, picked_ref, chunks=4):
    rows, slots = grad_agg.shape[0], asked.shape[0]
    step = slots // chunks
    for c in range(chunks):
        part = slice(c * step, (c + 1) * step)
        picked_ref[part, :] = dot_nn(onehot(asked[part], rows), grad_agg[...]).astype(BF16)


def dense_step(step, agg_ref, state_ref, up, up_low, wx, wu, wb, acc_in, acc_out, grad_agg, next_ref):
    rows = agg_ref.shape[0]
    aggs, states = [], []
    for s in range(2):
        grad_x = mlp_half(s, agg_ref[...], state_ref[...], up_low, wx, wu, wb, acc_in, acc_out)
        aggs.append(grad_x[:, :TILE])
        states.append(grad_x[:, TILE:])
    grad_agg[pl.ds(pl.multiple_of(step * rows, rows), rows), :] = jnp.concatenate(aggs, axis=1).astype(BF16)
    next_ref[...] = up + jnp.concatenate(states, axis=1)


def first_kernel(blocks, agg_hbm, state_hbm, up_hbm, w_in_ref, w_bias_ref, w_out_ref,
                 next_ref, grad_agg, sums_hbm, wx, wu, wb, acc_in, acc_out, sums_ref,
                 agg_buf, state_buf, up_buf, sems):
    rows = agg_hbm.shape[0] // blocks

    def copies(step):
        part = pl.ds(pl.multiple_of(step * rows, rows), rows)
        pairs = ((agg_hbm, agg_buf), (state_hbm, state_buf), (up_hbm, up_buf))
        return [pltpu.make_async_copy(a.at[part], b.at[part], sems.at[step, i]) for i, (a, b) in enumerate(pairs)]

    for step in range(blocks):
        for copy in copies(step):
            copy.start()
    build_weights(1, w_in_ref, w_bias_ref, w_out_ref, wx, wu, wb)
    clear(acc_in, acc_out)

    @pl.loop(0, blocks)
    def _(step):
        for copy in copies(step):
            copy.wait()
        part = pl.ds(pl.multiple_of(step * rows, rows), rows)
        up_low = up_buf[part, :]
        dense_step(step, agg_buf.at[part], state_buf.at[part], up_low.astype(F32), up_low, wx, wu, wb,
                   acc_in, acc_out, grad_agg, next_ref.at[part])

    store_sums(acc_in, acc_out, sums_ref)
    copy = pltpu.make_async_copy(sums_ref, sums_hbm, sems.at[0, 0])
    copy.start()
    copy.wait()


def first_pass(agg, state, up, w_in, w_bias, w_out):
    rows, feat = agg.shape
    blocks = rows // 256
    return pl.pallas_call(
        functools.partial(first_kernel, blocks),
        in_specs=[HBM, HBM, HBM, VMEM, VMEM, VMEM],
        out_specs=[VMEM, VMEM, HBM],
        out_shape=[
            jax.ShapeDtypeStruct((rows, feat), F32),
            jax.ShapeDtypeStruct((rows, feat), BF16),
            pltpu.HBM((SUM_ROWS, WIDE), F32),
        ],
        scratch_shapes=scratch(WEIGHT_SHAPES + SUM_SHAPES)
        + [pltpu.VMEM((SUM_ROWS, WIDE), F32)]
        + [pltpu.VMEM((rows, feat), BF16)] * 3
        + [pltpu.SemaphoreType.DMA((blocks, 3))],
        compiler_params=params(),
        cost_estimate=cost(5.4e9, 4 << 20, 2 << 20),
        name="first",
    )(in_hbm(agg), in_hbm(state), in_hbm(up), w_in, w_bias, w_out)


def pick_kernel(capacity, asked_ref, grad_agg, picked_ref):
    asked = slot_columns(asked_ref[:, 0, :], capacity, (0,))[0]
    pick_rows(asked, grad_agg, picked_ref)


def pick(capacity, asked, grad_agg):
    slots, feat = asked.shape[0] * capacity, grad_agg.shape[1]
    return pl.pallas_call(
        functools.partial(pick_kernel, capacity),
        in_specs=[VMEM, VMEM],
        out_specs=VMEM,
        out_shape=jax.ShapeDtypeStruct((slots, feat), BF16),
        compiler_params=params(12 << 20),
        cost_estimate=cost(8e8, 1 << 20),
        name="pick",
    )(asked, grad_agg)


def rest_kernel(capacity, tiles_ref, count_ref, agg_ref, state_ref, up_ref, w_in_ref, w_bias_ref, w_out_ref,
                asked_ref, next_ref, picked_ref, sums_ref, live_ref, wx, wu, wb,
                acc_in, acc_out, grad_agg):
    step = pl.program_id(0)
    rows = agg_ref.shape[0]
    count = count_ref[0, 1]

    @pl.when(step == 0)
    def _():
        build_weights(0, w_in_ref, w_bias_ref, w_out_ref, wx, wu, wb)
        clear(acc_in, acc_out)

    up = up_ref[...]
    tile = lax.shift_right_logical(iota((rows, 1), 0) + step * rows, 7)
    dead = (tile == tiles_ref[1, 0]) | ((tile == tiles_ref[1, 1]) & (count > 1))
    up_low = jnp.where(dead, 0.0, up).astype(BF16)
    dense_step(step, agg_ref, state_ref, up, up_low, wx, wu, wb, acc_in, acc_out, grad_agg, next_ref)

    @pl.when(step == pl.num_programs(0) - 1)
    def _():
        store_sums(acc_in, acc_out, sums_ref)
        asked = slot_columns(asked_ref[:, 0, :], capacity, (0,))[0]
        live_ref[...] = onehot(compact_column(asked, (tiles_ref[1, 0], tiles_ref[1, 1]), count), 2 * TILE)
        pick_rows(asked, grad_agg, picked_ref)


def rest_pass(capacity, tiles, count, agg, state, up, w_in, w_bias, w_out, asked):
    rows, feat = agg.shape
    slots = asked.shape[0] * capacity
    block = 256
    row_spec = pl.BlockSpec((block, feat), lambda i: (i, 0))
    return pl.pallas_call(
        functools.partial(rest_kernel, capacity),
        grid=(rows // block,),
        in_specs=[SMEM, SMEM, row_spec, row_spec, row_spec, whole(w_in.shape), whole(w_bias.shape),
                  whole(w_out.shape), whole(asked.shape)],
        out_specs=[row_spec, whole((slots, feat)), whole((SUM_ROWS, WIDE)), whole((slots, 2 * TILE))],
        out_shape=[
            pltpu.HBM((rows, feat), F32),
            pltpu.HBM((slots, feat), BF16),
            pltpu.HBM((SUM_ROWS, WIDE), F32),
            pltpu.HBM((slots, 2 * TILE), BF16),
        ],
        scratch_shapes=scratch(WEIGHT_SHAPES + SUM_SHAPES) + [pltpu.VMEM((rows, feat), BF16)],
        compiler_params=params(),
        cost_estimate=cost(5.4e9, 4 << 20, 2 << 20),
        name="rest",
    )(tiles, count, agg, state, up, w_in, w_bias, w_out, asked)


def as_row(column):
    return jnp.broadcast_to(column.astype(F32), (column.shape[0], TILE)).T[0:8].astype(jnp.int32)


def onehot_rows(row, width):
    return (iota((width, row.shape[1]), 0) == row).astype(F32).astype(BF16)


def tables_two_kernel(capacity, tiles_ref, count_ref, ids_ref, table_ref, t_ref, rows_ref):
    source, relation = slot_columns(ids_ref[...], capacity, (0, 64))
    width = -(-table_ref.shape[0] // TILE) * TILE
    pad = width - table_ref.shape[0]
    table = jnp.concatenate([table_ref[...], jnp.zeros((pad, table_ref.shape[1]), BF16)], axis=0)
    t_ref[...] = dot_nn(onehot(relation - 1, width), table).astype(BF16)
    rows_ref[0] = as_row(relation - 1)
    for hop in range(2):
        column = compact_column(source - 1, (tiles_ref[hop, 0], tiles_ref[hop, 1]), count_ref[0, hop])
        rows_ref[1 + hop] = as_row(column)


def tables_two(capacity, tiles, count, ids, table):
    feat = table.shape[1]
    slots = ids.shape[0] * capacity
    return pl.pallas_call(
        functools.partial(tables_two_kernel, capacity),
        in_specs=[SMEM, SMEM, VMEM, VMEM],
        out_specs=[VMEM, VMEM],
        out_shape=[
            jax.ShapeDtypeStruct((slots, feat), BF16),
            jax.ShapeDtypeStruct((3, 8, slots), jnp.int32),
        ],
        compiler_params=params(),
        cost_estimate=cost(1e9, 2 << 20),
        name="tables_two",
    )(tiles, count, ids, table)


def tables_one_kernel(capacity, tiles_ref, count_ref, ids_ref, rows_ref, answer_ref, one_a, one_b, zero_a, zero_b,
                      h_ref, total_ref):
    source = slot_columns(ids_ref[...], capacity, (0,))[0] - 1
    columns = [
        compact_column(source, (tiles_ref[hop, 0], tiles_ref[hop, 1]), count_ref[0, hop]) for hop in range(2)
    ]
    h_ref[...] = dot_nn(onehot(columns[0], 2 * TILE), jnp.concatenate([zero_a[...], zero_b[...]], axis=0)).astype(BF16)
    states = dot_nn(onehot(columns[1], 2 * TILE), jnp.concatenate([one_a[...], one_b[...]], axis=0)).astype(BF16)
    total_ref[...] = dot_nn(onehot_rows(rows_ref[0, 0:1, :], total_ref.shape[0]), answer_ref[...] * states)


def tables_one(capacity, tiles, count, ids, rows, answer, state_one, state_zero, groups):
    slots, feat = answer.shape
    width = -(-groups // TILE) * TILE

    def tile(hop, k):
        return pl.BlockSpec((TILE, feat), lambda i, tiles, count: (tiles[hop, k], 0))

    return pl.pallas_call(
        functools.partial(tables_one_kernel, capacity),
        grid_spec=pltpu.PrefetchScalarGridSpec(
            num_scalar_prefetch=2,
            grid=(1,),
            in_specs=[whole(ids.shape), whole(rows.shape), whole(answer.shape), tile(1, 0), tile(1, 1), tile(0, 0),
                      tile(0, 1)],
            out_specs=[whole((slots, feat)), whole((width, feat))],
        ),
        out_shape=[
            jax.ShapeDtypeStruct((slots, feat), BF16),
            jax.ShapeDtypeStruct((width, feat), F32),
        ],
        compiler_params=params(),
        cost_estimate=cost(2e9, 4 << 20),
        name="tables_one",
    )(tiles, count, ids, rows, answer, state_one, state_one, state_zero, state_zero)


def contribution_kernel(answer_ref, t_ref, rows_ref, out_ref):
    select = onehot_rows(rows_ref[2, 0:1, :], 2 * TILE)
    out_ref[...] = dot_nn(select, answer_ref[...] * t_ref[...]).astype(BF16)


def contribution(answer, table, rows):
    return pl.pallas_call(
        contribution_kernel,
        in_specs=[VMEM] * 3,
        out_specs=VMEM,
        out_shape=jax.ShapeDtypeStruct((2 * TILE, answer.shape[1]), BF16),
        compiler_params=params(8 << 20),
        cost_estimate=cost(2e8, 3 << 20),
        name="contribution",
    )(answer, table, rows)


def live_kernel(tiles_ref, count_ref, agg_a, agg_b, state_a, state_b, up_a, up_b, c0, c1, c2, c3,
                w_in_ref, w_bias_ref, w_out_ref, live_ref, rest_ref, picked_ref, next_ref, sums_ref,
                wx, wu, wb, acc_in, acc_out):
    build_weights(0, w_in_ref, w_bias_ref, w_out_ref, wx, wu, wb)
    clear(acc_in, acc_out)
    source = (c0[...].astype(F32) + c1[...].astype(F32)) + (c2[...].astype(F32) + c3[...].astype(F32))
    up = jnp.concatenate([up_a[...], up_b[...]], axis=0) + source
    keep = (iota((2 * TILE, 1), 0) < TILE) | (count_ref[0, 1] > 1)
    up_low = jnp.where(keep, up, 0.0).astype(BF16)
    agg = jnp.concatenate([agg_a[...], agg_b[...]], axis=0)
    state = jnp.concatenate([state_a[...], state_b[...]], axis=0)
    aggs, states = [], []
    for s in range(2):
        grad_x = mlp_half(s, agg, state, up_low, wx, wu, wb, acc_in, acc_out)
        aggs.append(grad_x[:, :TILE])
        states.append(grad_x[:, TILE:])
    grad_agg = jnp.concatenate(aggs, axis=1).astype(BF16)
    next_ref[...] = up + jnp.concatenate(states, axis=1)
    store_sums(acc_in, acc_out, sums_ref)
    picked_ref[...] = (dot_nn(live_ref[...], grad_agg) + rest_ref[...].astype(F32)).astype(BF16)


def live_pass(tiles, count, agg, state, up, parts, weights, live, rest):
    feat = agg.shape[1]

    def tile(k):
        return pl.BlockSpec((TILE, feat), lambda i, tiles, count: (tiles[1, k], 0))

    return pl.pallas_call(
        live_kernel,
        grid_spec=pltpu.PrefetchScalarGridSpec(
            num_scalar_prefetch=2,
            grid=(1,),
            in_specs=[tile(0), tile(1)] * 3 + [whole(parts[0].shape)] * 4
            + [whole(w.shape) for w in weights] + [whole(live.shape), whole(rest.shape)],
            out_specs=[whole(rest.shape), whole((2 * TILE, feat)), whole((SUM_ROWS, WIDE))],
            scratch_shapes=scratch(WEIGHT_SHAPES + SUM_SHAPES),
        ),
        out_shape=[
            jax.ShapeDtypeStruct(rest.shape, BF16),
            jax.ShapeDtypeStruct((2 * TILE, feat), F32),
            jax.ShapeDtypeStruct((SUM_ROWS, WIDE), F32),
        ],
        compiler_params=params(),
        cost_estimate=cost(1.6e9, 4 << 20, 1 << 19),
        name="live",
    )(tiles, count, agg, agg, state, state, up, up, *parts, *weights, live, rest)


GAP = SUM_ROWS


def pack_kernel(answer_ref, t_ref, h_ref, rows_ref, before_ref, w2_ref, w1a_ref, w1b_ref, part_ref, out_ref):
    answer = answer_ref[...]
    part_ref[...] = dot_nn(onehot_rows(rows_ref[1, 0:1, :], 2 * TILE), answer * t_ref[...]).astype(BF16)
    select = onehot_rows(rows_ref[0, 0:1, :], before_ref.shape[0])
    total = before_ref[...] + dot_nn(select, answer * h_ref[...])
    used, feat = total.shape
    out_ref[used:, 0:feat] = jnp.zeros((out_ref.shape[0] - used, feat), BF16)
    out_ref[4 * GAP:, feat:feat + TILE] = jnp.zeros((out_ref.shape[0] - 4 * GAP, TILE), BF16)
    out_ref[0:used, 0:feat] = total.astype(BF16)
    layers = (w1a_ref[...] + w1b_ref[...], w2_ref[...])
    parts = []
    for layer in layers:
        parts += [layer[:, :TILE], layer[:, TILE:]]
    out_ref[0:4 * GAP, feat:feat + TILE] = jnp.concatenate(parts, axis=0).astype(BF16)


def pack_sums(answer, table, states, ids, before, w2, w1a, w1b, rows):
    feat = answer.shape[1]
    return pl.pallas_call(
        pack_kernel,
        in_specs=[VMEM] * 8,
        out_specs=[VMEM, VMEM],
        out_shape=[
            jax.ShapeDtypeStruct((2 * TILE, feat), BF16),
            jax.ShapeDtypeStruct((rows, feat + TILE), BF16),
        ],
        compiler_params=params(),
        cost_estimate=cost(4e8, 4 << 20),
        name="pack_sums",
    )(answer, table, states, ids, before, w2, w1a, w1b)


def combine_kernel(feat, scale_relations, scale_weights, in_ref, out_ref):
    total = jnp.sum(in_ref[...].astype(F32), axis=0)
    lane = iota(total.shape, 1)
    total = total * jnp.where(lane < feat, scale_relations, scale_weights)
    out_ref[...] = jnp.broadcast_to(total.astype(BF16)[None], out_ref.shape)


def combine(chunks, feat, scale_relations, scale_weights):
    return pl.pallas_call(
        functools.partial(combine_kernel, feat, scale_relations, scale_weights),
        in_specs=[VMEM],
        out_specs=VMEM,
        out_shape=jax.ShapeDtypeStruct(chunks.shape, BF16),
        compiler_params=params(),
        cost_estimate=cost(1e6, 1 << 20),
        name="combine",
    )(chunks)


def unpack_kernel(feat, in_ref, relation_ref, w_in_ref, w_bias_ref, w_out_ref):
    groups = relation_ref.shape[0]
    relation_ref[...] = in_ref[0:groups, 0:feat].astype(F32)
    for layer in range(2):
        at = 2 * layer * GAP
        left = in_ref[at:at + GAP, feat:feat + TILE].astype(F32)
        right = in_ref[at + GAP:at + 2 * GAP, feat:feat + TILE].astype(F32)
        both = jnp.concatenate([left, right], axis=1)
        w_in_ref[layer] = both[0:2 * DIM]
        w_out_ref[layer] = both[2 * DIM:3 * DIM]
        w_bias_ref[layer:layer + 1, :] = both[3 * DIM:3 * DIM + 1]


def unpack(gathered, groups, feat):
    return pl.pallas_call(
        functools.partial(unpack_kernel, feat),
        in_specs=[VMEM],
        out_specs=[VMEM] * 4,
        out_shape=[
            jax.ShapeDtypeStruct((groups, feat), F32),
            jax.ShapeDtypeStruct((2, 2 * DIM, WIDE), F32),
            jax.ShapeDtypeStruct((2, WIDE), F32),
            jax.ShapeDtypeStruct((2, DIM, WIDE), F32),
        ],
        compiler_params=params(),
        cost_estimate=cost(1e6, 2 << 20),
        name="unpack",
    )(gathered)


def final_kernel(tiles_ref, count_ref, quarter_ref, next_ref, live_ref, c0, c1, c2, c3, out_ref):
    tile = 2 * quarter_ref[0] + pl.program_id(0)
    value = next_ref[...]
    for k in range(2):
        rows = slice(k * TILE, (k + 1) * TILE)
        is_live = (tile == tiles_ref[1, k]) & (count_ref[0, 1] > k)
        value = jnp.where(is_live, live_ref[rows, :], value)
    for k in range(2):
        rows = slice(k * TILE, (k + 1) * TILE)
        is_live = (tile == tiles_ref[0, k]) & (count_ref[0, 0] > k)
        source = (c0[rows, :].astype(F32) + c1[rows, :].astype(F32)) + (
            c2[rows, :].astype(F32) + c3[rows, :].astype(F32)
        )
        value = jnp.where(is_live, value + source, value)
    out_ref[...] = value.astype(BF16)


def final_pass(tiles, count, quarter_id, after, live, parts, quarter):
    feat = after.shape[1]
    blocks = quarter // TILE
    return pl.pallas_call(
        final_kernel,
        grid_spec=pltpu.PrefetchScalarGridSpec(
            num_scalar_prefetch=3,
            grid=(blocks,),
            in_specs=[pl.BlockSpec((TILE, feat), lambda i, t, c, q: (q[0] * blocks + i, 0)), whole(live.shape)]
            + [whole(parts[0].shape)] * 4,
            out_specs=pl.BlockSpec((TILE, feat), lambda i, *_: (i, 0)),
        ),
        out_shape=jax.ShapeDtypeStruct((quarter, feat), BF16),
        compiler_params=params(),
        cost_estimate=cost(1e6, 1 << 20),
        name="final",
    )(tiles, count, quarter_id, after, live, *parts)


def shards(state_zero, state_one, aggregate_one, aggregate_two, cotangent, relation_table, update_in, update_bias,
           update_out, frontier_tiles, frontier_count, edge_source, edge_relation, edge_target, edge_owner):
    block_rows, feat = state_zero.shape
    groups = relation_table.shape[0]
    group_size = lax.axis_size("rel")
    peers = lax.axis_size("ent")
    quarter = block_rows // group_size
    edges = edge_source.shape[0]
    capacity = 3 * edges // (2 * peers)
    slots = peers * capacity
    sum_rows = 8 * peers

    def exchange(chunks):
        return lax.all_to_all(chunks, "ent", split_axis=0, concat_axis=0, tiled=True)

    def over_rel(part):
        turned = [
            lax.ppermute(part, "rel", [(i, (i + k) % group_size) for i in range(group_size)])
            for k in range(1, group_size)
        ]
        return [part] + turned

    row = lambda values: values.reshape(1, edges)
    count = jnp.swapaxes(frontier_count, 0, 1)
    weights = (update_in, update_bias, jnp.swapaxes(update_out, 1, 2))
    request, ids = pl.pallas_call(
        functools.partial(slots_kernel, peers),
        in_specs=[HBM] * 4,
        out_specs=[VMEM] * 2,
        out_shape=[
            jax.ShapeDtypeStruct((peers, 1, 128), F32),
            jax.ShapeDtypeStruct((peers, 128), F32),
        ],
        scratch_shapes=[pltpu.VMEM((1, edges), jnp.int32)] * 4 + [pltpu.SemaphoreType.DMA((4,))],
        compiler_params=params(8 << 20),
        cost_estimate=cost(1e8, 1 << 20),
        name="slots",
    )(*(in_hbm(row(values)) for values in (edge_owner, edge_target, edge_source, edge_relation)))
    asked = exchange(request)

    upstream_one, grad_agg, sums_two = first_pass(aggregate_two, state_one, cotangent, *weights)
    picked_two = pick(capacity, asked, grad_agg)
    answered_two = exchange(picked_two.reshape(peers, capacity, feat)).reshape(slots, feat)
    after, rest, sums_rest, live = rest_pass(
        capacity, frontier_tiles, count, aggregate_one, state_zero, upstream_one, *weights, asked
    )
    edge_table, rows = tables_two(capacity, frontier_tiles, count, ids, relation_table)
    answered_two, rest, edge_table, rows = lax.optimization_barrier((answered_two, rest, edge_table, rows))
    parts = over_rel(contribution(answered_two, edge_table, rows))
    states_one, relation_two = tables_one(
        capacity, frontier_tiles, count, ids, rows, answered_two, state_one, state_zero, groups
    )
    parts[0], rest, states_one, relation_two = lax.optimization_barrier((parts[0], rest, states_one, relation_two))
    picked_one, after_live, sums_live = live_pass(
        frontier_tiles, count, aggregate_one, state_zero, upstream_one, parts, weights, live, rest
    )
    answered_one = exchange(picked_one.reshape(peers, capacity, feat)).reshape(slots, feat)
    part, packed = pack_sums(
        answered_one, edge_table, states_one, rows, relation_two, sums_two, sums_rest, sums_live, sum_rows
    )
    parts = over_rel(part)
    scale_weights = 1.0 / math.sqrt(block_rows * peers * QUERIES)
    scale_relations = math.sqrt(groups * group_size / (edges * peers * group_size))
    chunks = exchange(packed.reshape(peers, 8, feat + TILE))
    gathered = exchange(combine(chunks, feat, scale_relations, scale_weights)).reshape(sum_rows, feat + TILE)
    quarter_id = lax.axis_index("rel").astype(jnp.int32).reshape(1)
    grad_zero = final_pass(frontier_tiles, count, quarter_id, after, after_live, parts, quarter)
    relation, grad_in, grad_bias, grad_out = unpack(gathered, groups, feat)
    return grad_zero, relation, grad_in, grad_bias, jnp.swapaxes(grad_out, 1, 2)


def solution(mesh):
    in_specs = (
        P("ent", None),
        P("ent", None),
        P("ent", None),
        P("ent", None),
        P("ent", None),
        P("rel", None),
        P(),
        P(),
        P(),
        P(None, "ent"),
        P(None, "ent"),
        P(("ent", "rel")),
        P(("ent", "rel")),
        P(("ent", "rel")),
        P(("ent", "rel"), None),
    )
    out_specs = (P(("ent", "rel"), None), P("rel", None), P(), P(), P())
    return jax.shard_map(shards, mesh=mesh, in_specs=in_specs, out_specs=out_specs, check_vma=False)
```

```python
import functools
import math

import jax
import jax.numpy as jnp
from jax import lax
from jax.experimental import pallas as pl
from jax.experimental.pallas import tpu as pltpu
from jax.sharding import PartitionSpec as P

QUERIES = 8
DIM = 32
TILE = 128
WIDE = 256
HALF_Q = 4
F32 = jnp.float32
BF16 = jnp.bfloat16
VMEM = pl.BlockSpec(memory_space=pltpu.VMEM)
SMEM = pl.BlockSpec(memory_space=pltpu.SMEM)
HBM = pl.BlockSpec(memory_space=pltpu.HBM)


def in_hbm(array):
    return pltpu.with_memory_space_constraint(array, pltpu.HBM)


def iota(shape, dim):
    return lax.broadcasted_iota(jnp.int32, shape, dim)


def dot_nn(a, b):
    return lax.dot_general(a, b, (((1,), (0,)), ((), ())), preferred_element_type=F32)


def dot_nt(a, b):
    return lax.dot_general(a, b, (((1,), (1,)), ((), ())), preferred_element_type=F32)


def dot_tn(a, b):
    return lax.dot_general(a, b, (((0,), (0,)), ((), ())), preferred_element_type=F32)


def params(vmem=20 << 20):
    return pltpu.CompilerParams(vmem_limit_bytes=vmem)


def cost(flops, nbytes, trans=0):
    return pl.CostEstimate(flops=int(flops), bytes_accessed=int(nbytes), transcendentals=int(trans))


def slots_kernel(peers, tiles_ref, count_ref, owner_hbm, target_hbm, source_hbm, relation_hbm, request_ref, ids_ref,
                 owner_ref, target_ref, source_ref, relation_ref, sems):
    pairs = ((owner_hbm, owner_ref), (target_hbm, target_ref), (source_hbm, source_ref), (relation_hbm, relation_ref))
    copies = [pltpu.make_async_copy(a, b, sems.at[i]) for i, (a, b) in enumerate(pairs)]
    for copy in copies:
        copy.start()
    for copy in copies:
        copy.wait()
    edges = owner_ref.shape[1]
    hit = (iota((peers, edges), 0) == owner_ref[...]).astype(F32)
    below = (iota((TILE, TILE), 0) < iota((TILE, TILE), 1)).astype(BF16)
    tile = lax.shift_right_logical(source_ref[...], 7)
    request, tops = [], []
    for hop in (1, 0):
        live = (tile == tiles_ref[hop, 0]) | ((tile == tiles_ref[hop, 1]) & (count_ref[0, hop] > 1))
        own = jnp.where(live, hit, 0.0)
        own_low = own.astype(BF16)
        offset = jnp.zeros((peers, 1), F32)
        pieces = []
        for b in range(edges // TILE):
            block = slice(b * TILE, (b + 1) * TILE)
            pieces.append(dot_nn(own_low[:, block], below) + offset)
            offset = offset + jnp.sum(own[:, block], axis=1, keepdims=True)
        earlier = jnp.sum(jnp.concatenate(pieces, axis=1) * own, axis=0, keepdims=True).astype(jnp.int32)
        place = jnp.where((iota((32, edges), 0) == earlier) & live, 1.0, 0.0)

        def spread(values):
            high = lax.shift_right_logical(values, 5)
            low = values & 31
            return [place * high.astype(F32), place * low.astype(F32)]

        request += spread(target_ref[...])
        tops.append(jnp.max(offset, axis=0, keepdims=True))
        second = jnp.concatenate(
            spread(source_ref[...] + 1) + spread(relation_ref[...] + 1), axis=0
        ).astype(BF16)
        ids_ref[hop] = dot_nt(own_low, second)
    lane = iota((peers, 128), 1)
    sent = dot_nt(hit.astype(BF16), jnp.concatenate(request, axis=0).astype(BF16))
    sent = jnp.where(lane == 31, tops[0], sent)
    request_ref[:, 0, :] = jnp.where(lane == 95, tops[1], sent)


def slot_columns(table, capacity, bases, skip=0):
    peers = table.shape[0]
    slots = peers * capacity
    row = iota((slots, peers), 0)
    start = iota((slots, peers), 1) * capacity
    expand = ((row >= start) & (row < start + capacity)).astype(BF16)
    spread = dot_nn(expand, table.astype(BF16))
    row = iota((slots, 128), 0)
    group = ((row.astype(F32) + 0.5) * (1.0 / capacity)).astype(jnp.int32)
    place = row - group * capacity + skip
    lane = iota((slots, 128), 1)
    columns = []
    for base in bases:
        weight = jnp.where(lane == place + base, 32.0, 0.0) + jnp.where(
            lane == place + (base + 32), 1.0, 0.0
        )
        columns.append(jnp.sum(spread * weight, axis=1, keepdims=True).astype(jnp.int32))
    return columns


def compact_column(column, tiles, count):
    tile = lax.shift_right_arithmetic(column, 7)
    inner = column & 127
    result = jnp.full(column.shape, -1, jnp.int32)
    for k in range(len(tiles)):
        live = (tile == tiles[k]) & (count > k)
        result = jnp.where(live, inner + k * TILE, result)
    return result


def onehot(column, width):
    shape = (column.shape[0], width)
    lane = lax.broadcasted_iota(jnp.int16, shape, 1)
    hit = lane == jnp.broadcast_to(column, shape).astype(jnp.int16)
    return jnp.where(hit, jnp.ones((), BF16), jnp.zeros((), BF16))


def build_weights(layer, w_in_ref, w_bias_ref, w_out_ref, wx_ref, wu_ref, wb_ref):
    wx_ref[...] = jnp.zeros_like(wx_ref)
    wu_ref[...] = jnp.zeros_like(wu_ref)
    for q in range(HALF_Q):
        rows, cols = slice(q * DIM, (q + 1) * DIM), slice(q * WIDE, (q + 1) * WIDE)
        low = slice(TILE + q * DIM, TILE + (q + 1) * DIM)
        wx_ref[rows, cols] = 0.5 * w_in_ref[layer, 0:DIM, :]
        wx_ref[low, cols] = 0.5 * w_in_ref[layer, DIM:2 * DIM, :]
        wu_ref[rows, cols] = w_out_ref[layer]
        wb_ref[:, cols] = 0.5 * w_bias_ref[layer:layer + 1, :]


def mlp_half(s, agg, state, up_low, wx, wu, bias, acc_in, acc_out):
    lanes = slice(s * TILE, (s + 1) * TILE)
    x = jnp.concatenate([agg[:, lanes], state[:, lanes]], axis=1)
    up = up_low[:, lanes]
    x_turned, up_turned = x.T, up.T
    half = dot_nn(x, wx[...]) + bias[...]
    bend = jnp.tanh(half)
    above = 1.0 + bend
    act_low = (half * above).astype(BF16)
    slope = above * (1.0 + half * (1.0 - bend))
    low = (dot_nn(up, wu[...]) * slope).astype(BF16)
    ones = jnp.ones((16, x.shape[0]), BF16)
    for q in range(HALF_Q):
        cols = slice(q * WIDE, (q + 1) * WIDE)
        rows = slice(q * DIM, (q + 1) * DIM)
        low_rows = slice(TILE + q * DIM, TILE + (q + 1) * DIM)
        own = jnp.concatenate([x_turned[rows], x_turned[low_rows], ones], axis=0)
        acc_in[...] += dot_nn(own, low[:, cols])
        acc_out[...] += dot_nn(up_turned[rows], act_low[:, cols])
    return dot_nt(low, wx[...])


def store_sums(acc_in, acc_out, sums_ref):
    sums_ref[0:2 * DIM, :] = 0.5 * acc_in[0:2 * DIM, :]
    sums_ref[2 * DIM:3 * DIM, :] = acc_out[...]
    sums_ref[3 * DIM:3 * DIM + 8, :] = 0.5 * acc_in[2 * DIM:2 * DIM + 8, :]


def clear(acc_in, acc_out):
    acc_in[...] = jnp.zeros_like(acc_in)
    acc_out[...] = jnp.zeros_like(acc_out)


WEIGHT_SHAPES = [
    ((2 * TILE, HALF_Q * WIDE), BF16),
    ((TILE, HALF_Q * WIDE), BF16),
    ((1, HALF_Q * WIDE), F32),
]
SUM_SHAPES = [((2 * DIM + 16, WIDE), F32), ((DIM, WIDE), F32)]
SUM_ROWS = 3 * DIM + 8


def scratch(shapes):
    return [pltpu.VMEM(shape, dtype) for shape, dtype in shapes]


def whole(shape):
    return pl.BlockSpec(shape, lambda i, *_: (0,) * len(shape))


def pick_rows(asked, grad_agg, picked_ref, chunks=4):
    rows, slots = grad_agg.shape[0], asked.shape[0]
    step = slots // chunks
    for c in range(chunks):
        part = slice(c * step, (c + 1) * step)
        picked_ref[part, :] = dot_nn(onehot(asked[part], rows), grad_agg[...]).astype(BF16)


def dense_step(step, agg_ref, state_ref, up, up_low, wx, wu, wb, acc_in, acc_out, grad_agg, next_ref):
    rows = agg_ref.shape[0]
    aggs, states = [], []
    for s in range(2):
        grad_x = mlp_half(s, agg_ref[...], state_ref[...], up_low, wx, wu, wb, acc_in, acc_out)
        aggs.append(grad_x[:, :TILE])
        states.append(grad_x[:, TILE:])
    grad_agg[pl.ds(pl.multiple_of(step * rows, rows), rows), :] = jnp.concatenate(aggs, axis=1).astype(BF16)
    next_ref[...] = up + jnp.concatenate(states, axis=1)


def first_kernel(blocks, agg_hbm, state_hbm, up_hbm, w_in_ref, w_bias_ref, w_out_ref,
                 next_ref, grad_agg, sums_hbm, wx, wu, wb, acc_in, acc_out, sums_ref,
                 agg_buf, state_buf, up_buf, sems):
    rows = agg_hbm.shape[0] // blocks

    def copies(step):
        part = pl.ds(pl.multiple_of(step * rows, rows), rows)
        pairs = ((agg_hbm, agg_buf), (state_hbm, state_buf), (up_hbm, up_buf))
        return [pltpu.make_async_copy(a.at[part], b.at[part], sems.at[step, i]) for i, (a, b) in enumerate(pairs)]

    for step in range(blocks):
        for copy in copies(step):
            copy.start()
    build_weights(1, w_in_ref, w_bias_ref, w_out_ref, wx, wu, wb)
    clear(acc_in, acc_out)

    @pl.loop(0, blocks)
    def _(step):
        for copy in copies(step):
            copy.wait()
        part = pl.ds(pl.multiple_of(step * rows, rows), rows)
        up_low = up_buf[part, :]
        dense_step(step, agg_buf.at[part], state_buf.at[part], up_low.astype(F32), up_low, wx, wu, wb,
                   acc_in, acc_out, grad_agg, next_ref.at[part])

    store_sums(acc_in, acc_out, sums_ref)
    copy = pltpu.make_async_copy(sums_ref, sums_hbm, sems.at[0, 0])
    copy.start()
    copy.wait()


def first_pass(agg, state, up, w_in, w_bias, w_out):
    rows, feat = agg.shape
    blocks = rows // 512
    return pl.pallas_call(
        functools.partial(first_kernel, blocks),
        in_specs=[HBM, HBM, HBM, VMEM, VMEM, VMEM],
        out_specs=[VMEM, VMEM, HBM],
        out_shape=[
            jax.ShapeDtypeStruct((rows, feat), F32),
            jax.ShapeDtypeStruct((rows, feat), BF16),
            pltpu.HBM((SUM_ROWS, WIDE), F32),
        ],
        scratch_shapes=scratch(WEIGHT_SHAPES + SUM_SHAPES)
        + [pltpu.VMEM((SUM_ROWS, WIDE), F32)]
        + [pltpu.VMEM((rows, feat), BF16)] * 3
        + [pltpu.SemaphoreType.DMA((blocks, 3))],
        compiler_params=params(),
        cost_estimate=cost(5.4e9, 4 << 20, 2 << 20),
        name="first",
    )(in_hbm(agg), in_hbm(state), in_hbm(up), w_in, w_bias, w_out)


def pick_kernel(capacity, skip, base, asked_ref, grad_agg, picked_ref):
    asked = slot_columns(asked_ref[:, 0, :], capacity, (base,), skip)[0]
    pick_rows(asked, grad_agg, picked_ref)


def pick(capacity, skip, base, asked, grad_agg):
    slots, feat = asked.shape[0] * capacity, grad_agg.shape[1]
    return pl.pallas_call(
        functools.partial(pick_kernel, capacity, skip, base),
        in_specs=[VMEM, VMEM],
        out_specs=VMEM,
        out_shape=jax.ShapeDtypeStruct((slots, feat), BF16),
        compiler_params=params(12 << 20),
        cost_estimate=cost(8e8, 1 << 20),
        name="pick",
    )(asked, grad_agg)


def rest_kernel(capacity, tiles_ref, count_ref, agg_ref, state_ref, up_ref, w_in_ref, w_bias_ref, w_out_ref,
                asked_ref, next_ref, picked_ref, sums_ref, live_ref, grad_agg, wx, wu, wb,
                acc_in, acc_out):
    step = pl.program_id(0)
    rows = agg_ref.shape[0]
    count = count_ref[0, 1]

    @pl.when(step == 0)
    def _():
        build_weights(0, w_in_ref, w_bias_ref, w_out_ref, wx, wu, wb)
        clear(acc_in, acc_out)

    up = up_ref[...]
    tile = lax.shift_right_logical(iota((rows, 1), 0) + step * rows, 7)
    dead = (tile == tiles_ref[1, 0]) | ((tile == tiles_ref[1, 1]) & (count > 1))
    up_low = jnp.where(dead, 0.0, up).astype(BF16)
    dense_step(step, agg_ref, state_ref, up, up_low, wx, wu, wb, acc_in, acc_out, grad_agg, next_ref)

    @pl.when(step == pl.num_programs(0) - 1)
    def _():
        store_sums(acc_in, acc_out, sums_ref)
        asked = slot_columns(asked_ref[:, 0, :], capacity, (64,))[0]
        live_ref[...] = onehot(compact_column(asked, (tiles_ref[1, 0], tiles_ref[1, 1]), count), 2 * TILE)
        pick_rows(asked, grad_agg, picked_ref)


def rest_pass(capacity, tiles, count, agg, state, up, w_in, w_bias, w_out, asked):
    rows, feat = agg.shape
    slots = asked.shape[0] * capacity
    block = 256
    row_spec = pl.BlockSpec((block, feat), lambda i: (i, 0))
    return pl.pallas_call(
        functools.partial(rest_kernel, capacity),
        grid=(rows // block,),
        in_specs=[SMEM, SMEM, row_spec, row_spec, row_spec, whole(w_in.shape), whole(w_bias.shape),
                  whole(w_out.shape), whole(asked.shape)],
        out_specs=[row_spec, whole((slots, feat)), whole((SUM_ROWS, WIDE)), whole((slots, 2 * TILE)),
                   whole((rows, feat))],
        out_shape=[
            pltpu.HBM((rows, feat), F32),
            pltpu.HBM((slots, feat), BF16),
            pltpu.HBM((SUM_ROWS, WIDE), F32),
            pltpu.HBM((slots, 2 * TILE), BF16),
            pltpu.HBM((rows, feat), BF16),
        ],
        scratch_shapes=scratch(WEIGHT_SHAPES + SUM_SHAPES),
        compiler_params=params(),
        cost_estimate=cost(5.4e9, 4 << 20, 2 << 20),
        name="rest",
    )(tiles, count, agg, state, up, w_in, w_bias, w_out, asked)


def as_row(column):
    return jnp.broadcast_to(column.astype(F32), (column.shape[0], TILE)).T[0:8].astype(jnp.int32)


def onehot_rows(row, width):
    return (iota((width, row.shape[1]), 0) == row).astype(F32).astype(BF16)


def relation_rows(relation, table_ref):
    width = -(-table_ref.shape[0] // TILE) * TILE
    pad = width - table_ref.shape[0]
    table = jnp.concatenate([table_ref[...], jnp.zeros((pad, table_ref.shape[1]), BF16)], axis=0)
    return dot_nn(onehot(relation, width), table).astype(BF16)


def tables_two_kernel(capacity, tiles_ref, count_ref, ids_ref, table_ref, t_ref, rows_ref):
    for hop in range(2):
        source, relation = slot_columns(ids_ref[hop], capacity, (0, 64))
        if hop == 1:
            t_ref[...] = relation_rows(relation - 1, table_ref)
        rows_ref[hop] = as_row(relation - 1)
        column = compact_column(source - 1, (tiles_ref[hop, 0], tiles_ref[hop, 1]), count_ref[0, hop])
        rows_ref[2 + hop] = as_row(column)


def tables_two(capacity, tiles, count, ids, table):
    feat = table.shape[1]
    slots = ids.shape[1] * capacity
    return pl.pallas_call(
        functools.partial(tables_two_kernel, capacity),
        in_specs=[SMEM, SMEM, VMEM, VMEM],
        out_specs=[VMEM, VMEM],
        out_shape=[
            jax.ShapeDtypeStruct((slots, feat), BF16),
            jax.ShapeDtypeStruct((4, 8, slots), jnp.int32),
        ],
        compiler_params=params(),
        cost_estimate=cost(1e9, 2 << 20),
        name="tables_two",
    )(tiles, count, ids, table)


def tables_one_kernel(capacity, tiles_ref, count_ref, ids_ref, rows_ref, table_ref, answer_ref,
                      one_a, one_b, zero_a, zero_b, t_ref, h_ref, total_ref):
    states = []
    for hop, a, b in ((0, zero_a, zero_b), (1, one_a, one_b)):
        source, relation = slot_columns(ids_ref[hop], capacity, (0, 64))
        column = compact_column(source - 1, (tiles_ref[hop, 0], tiles_ref[hop, 1]), count_ref[0, hop])
        states.append(dot_nn(onehot(column, 2 * TILE), jnp.concatenate([a[...], b[...]], axis=0)).astype(BF16))
        if hop == 0:
            t_ref[...] = relation_rows(relation - 1, table_ref)
    h_ref[...] = states[0]
    total_ref[...] = dot_nn(onehot_rows(rows_ref[1, 0:1, :], total_ref.shape[0]), answer_ref[...] * states[1])


def tables_one(capacity, tiles, count, ids, rows, table, answer, state_one, state_zero):
    slots, feat = answer.shape
    width = -(-table.shape[0] // TILE) * TILE

    def tile(hop, k):
        return pl.BlockSpec((TILE, feat), lambda i, tiles, count: (tiles[hop, k], 0))

    return pl.pallas_call(
        functools.partial(tables_one_kernel, capacity),
        grid_spec=pltpu.PrefetchScalarGridSpec(
            num_scalar_prefetch=2,
            grid=(1,),
            in_specs=[whole(ids.shape), whole(rows.shape), whole(table.shape), whole(answer.shape), tile(1, 0),
                      tile(1, 1), tile(0, 0), tile(0, 1)],
            out_specs=[whole((slots, feat)), whole((slots, feat)), whole((width, feat))],
        ),
        out_shape=[
            jax.ShapeDtypeStruct((slots, feat), BF16),
            jax.ShapeDtypeStruct((slots, feat), BF16),
            jax.ShapeDtypeStruct((width, feat), F32),
        ],
        compiler_params=params(),
        cost_estimate=cost(2e9, 4 << 20),
        name="tables_one",
    )(tiles, count, ids, rows, table, answer, state_one, state_one, state_zero, state_zero)


def extra_kernel(hop, capacity, skip, tiles_ref, count_ref, ids_ref, table_ref, answer_ref, state_a, state_b,
                 part_ref, out_ref, total_ref):
    source, relation = slot_columns(ids_ref[hop], capacity, (0, 64), skip)
    column = compact_column(source - 1, (tiles_ref[hop, 0], tiles_ref[hop, 1]), count_ref[0, hop])
    select = onehot(column, 2 * TILE)
    answer = answer_ref[...]
    more = dot_nn(onehot_rows(as_row(column)[0:1], 2 * TILE), answer * relation_rows(relation - 1, table_ref))
    out_ref[...] = (part_ref[...].astype(F32) + more).astype(BF16)
    states = dot_nn(select, jnp.concatenate([state_a[...], state_b[...]], axis=0)).astype(BF16)
    total_ref[...] = dot_nn(onehot_rows(as_row(relation - 1)[0:1], total_ref.shape[0]), answer * states)


def extra(hop, capacity, skip, tiles, count, ids, table, answer, state, part):
    feat = answer.shape[1]
    width = -(-table.shape[0] // TILE) * TILE

    def tile(k):
        return pl.BlockSpec((TILE, feat), lambda i, tiles, count: (tiles[hop, k], 0))

    return pl.pallas_call(
        functools.partial(extra_kernel, hop, capacity, skip),
        grid_spec=pltpu.PrefetchScalarGridSpec(
            num_scalar_prefetch=2,
            grid=(1,),
            in_specs=[whole(ids.shape), whole(table.shape), whole(answer.shape), tile(0), tile(1), whole(part.shape)],
            out_specs=[whole(part.shape), whole((width, feat))],
        ),
        out_shape=[jax.ShapeDtypeStruct(part.shape, BF16), jax.ShapeDtypeStruct((width, feat), F32)],
        compiler_params=params(),
        cost_estimate=cost(1e9, 2 << 20),
        name="extra",
    )(tiles, count, ids, table, answer, state, state, part)


def contribution_kernel(answer_ref, t_ref, rows_ref, out_ref):
    select = onehot_rows(rows_ref[3, 0:1, :], 2 * TILE)
    out_ref[...] = dot_nn(select, answer_ref[...] * t_ref[...]).astype(BF16)


def contribution(answer, table, rows):
    return pl.pallas_call(
        contribution_kernel,
        in_specs=[VMEM] * 3,
        out_specs=VMEM,
        out_shape=jax.ShapeDtypeStruct((2 * TILE, answer.shape[1]), BF16),
        compiler_params=params(8 << 20),
        cost_estimate=cost(2e8, 3 << 20),
        name="contribution",
    )(answer, table, rows)


def live_kernel(tiles_ref, count_ref, agg_a, agg_b, state_a, state_b, up_a, up_b, c0, c1, c2, c3,
                w_in_ref, w_bias_ref, w_out_ref, live_ref, rest_ref, picked_ref, next_ref, sums_ref, grad_ref,
                wx, wu, wb, acc_in, acc_out):
    build_weights(0, w_in_ref, w_bias_ref, w_out_ref, wx, wu, wb)
    clear(acc_in, acc_out)
    source = (c0[...].astype(F32) + c1[...].astype(F32)) + (c2[...].astype(F32) + c3[...].astype(F32))
    up = jnp.concatenate([up_a[...], up_b[...]], axis=0) + source
    keep = (iota((2 * TILE, 1), 0) < TILE) | (count_ref[0, 1] > 1)
    up_low = jnp.where(keep, up, 0.0).astype(BF16)
    agg = jnp.concatenate([agg_a[...], agg_b[...]], axis=0)
    state = jnp.concatenate([state_a[...], state_b[...]], axis=0)
    aggs, states = [], []
    for s in range(2):
        grad_x = mlp_half(s, agg, state, up_low, wx, wu, wb, acc_in, acc_out)
        aggs.append(grad_x[:, :TILE])
        states.append(grad_x[:, TILE:])
    grad_agg = jnp.concatenate(aggs, axis=1).astype(BF16)
    next_ref[...] = up + jnp.concatenate(states, axis=1)
    store_sums(acc_in, acc_out, sums_ref)
    grad_ref[...] = grad_agg
    picked_ref[...] = (dot_nn(live_ref[...], grad_agg) + rest_ref[...].astype(F32)).astype(BF16)


def live_pass(tiles, count, agg, state, up, parts, weights, live, rest):
    feat = agg.shape[1]

    def tile(k):
        return pl.BlockSpec((TILE, feat), lambda i, tiles, count: (tiles[1, k], 0))

    return pl.pallas_call(
        live_kernel,
        grid_spec=pltpu.PrefetchScalarGridSpec(
            num_scalar_prefetch=2,
            grid=(1,),
            in_specs=[tile(0), tile(1)] * 3 + [whole(parts[0].shape)] * 4
            + [whole(w.shape) for w in weights] + [whole(live.shape), whole(rest.shape)],
            out_specs=[whole(rest.shape), whole((2 * TILE, feat)), whole((SUM_ROWS, WIDE)), whole((2 * TILE, feat))],
            scratch_shapes=scratch(WEIGHT_SHAPES + SUM_SHAPES),
        ),
        out_shape=[
            jax.ShapeDtypeStruct(rest.shape, BF16),
            jax.ShapeDtypeStruct((2 * TILE, feat), F32),
            jax.ShapeDtypeStruct((SUM_ROWS, WIDE), F32),
            jax.ShapeDtypeStruct((2 * TILE, feat), BF16),
        ],
        compiler_params=params(),
        cost_estimate=cost(1.6e9, 4 << 20, 1 << 19),
        name="live",
    )(tiles, count, agg, agg, state, state, up, up, *parts, *weights, live, rest)


def late_kernel(capacity, skip, tiles_ref, count_ref, asked_ref, rest_ref, live_ref, picked_ref):
    asked = slot_columns(asked_ref[:, 0, :], capacity, (64,), skip)[0]
    column = compact_column(asked, (tiles_ref[1, 0], tiles_ref[1, 1]), count_ref[0, 1])
    rest = dot_nn(onehot(asked, rest_ref.shape[0]), rest_ref[...])
    picked_ref[...] = (dot_nn(onehot(column, 2 * TILE), live_ref[...]) + rest).astype(BF16)


def late_pick(capacity, skip, tiles, count, asked, rest, live):
    slots, feat = asked.shape[0] * capacity, rest.shape[1]
    return pl.pallas_call(
        functools.partial(late_kernel, capacity, skip),
        in_specs=[SMEM, SMEM, VMEM, VMEM, VMEM],
        out_specs=VMEM,
        out_shape=jax.ShapeDtypeStruct((slots, feat), BF16),
        compiler_params=params(),
        cost_estimate=cost(8e8, 1 << 20),
        name="late_pick",
    )(tiles, count, asked, rest, live)


GAP = SUM_ROWS


def pack_kernel(answer_ref, t_ref, h_ref, rows_ref, before_ref, w2_ref, w1a_ref, w1b_ref, part_ref, out_ref):
    answer = answer_ref[...]
    part_ref[...] = dot_nn(onehot_rows(rows_ref[2, 0:1, :], 2 * TILE), answer * t_ref[...]).astype(BF16)
    select = onehot_rows(rows_ref[0, 0:1, :], before_ref.shape[0])
    total = before_ref[...] + dot_nn(select, answer * h_ref[...])
    used, feat = total.shape
    out_ref[used:, 0:feat] = jnp.zeros((out_ref.shape[0] - used, feat), BF16)
    out_ref[4 * GAP:, feat:feat + TILE] = jnp.zeros((out_ref.shape[0] - 4 * GAP, TILE), BF16)
    out_ref[0:used, 0:feat] = total.astype(BF16)
    layers = (w1a_ref[...] + w1b_ref[...], w2_ref[...])
    parts = []
    for layer in layers:
        parts += [layer[:, :TILE], layer[:, TILE:]]
    out_ref[0:4 * GAP, feat:feat + TILE] = jnp.concatenate(parts, axis=0).astype(BF16)


def pack_sums(answer, table, states, ids, before, w2, w1a, w1b, rows):
    feat = answer.shape[1]
    return pl.pallas_call(
        pack_kernel,
        in_specs=[VMEM] * 8,
        out_specs=[VMEM, VMEM],
        out_shape=[
            jax.ShapeDtypeStruct((2 * TILE, feat), BF16),
            jax.ShapeDtypeStruct((rows, feat + TILE), BF16),
        ],
        compiler_params=params(),
        cost_estimate=cost(4e8, 4 << 20),
        name="pack_sums",
    )(answer, table, states, ids, before, w2, w1a, w1b)


def combine_kernel(feat, scale_relations, scale_weights, in_ref, out_ref):
    total = jnp.sum(in_ref[...].astype(F32), axis=0)
    lane = iota(total.shape, 1)
    total = total * jnp.where(lane < feat, scale_relations, scale_weights)
    out_ref[...] = jnp.broadcast_to(total.astype(BF16)[None], out_ref.shape)


def combine(chunks, feat, scale_relations, scale_weights):
    return pl.pallas_call(
        functools.partial(combine_kernel, feat, scale_relations, scale_weights),
        in_specs=[VMEM],
        out_specs=VMEM,
        out_shape=jax.ShapeDtypeStruct(chunks.shape, BF16),
        compiler_params=params(),
        cost_estimate=cost(1e6, 1 << 20),
        name="combine",
    )(chunks)


def unpack_kernel(feat, in_ref, relation_ref, w_in_ref, w_bias_ref, w_out_ref):
    groups = relation_ref.shape[0]
    relation_ref[...] = in_ref[0:groups, 0:feat].astype(F32)
    for layer in range(2):
        at = 2 * layer * GAP
        left = in_ref[at:at + GAP, feat:feat + TILE].astype(F32)
        right = in_ref[at + GAP:at + 2 * GAP, feat:feat + TILE].astype(F32)
        both = jnp.concatenate([left, right], axis=1)
        w_in_ref[layer] = both[0:2 * DIM]
        w_out_ref[layer] = both[2 * DIM:3 * DIM]
        w_bias_ref[layer:layer + 1, :] = both[3 * DIM:3 * DIM + 1]


def unpack(gathered, groups, feat):
    return pl.pallas_call(
        functools.partial(unpack_kernel, feat),
        in_specs=[VMEM],
        out_specs=[VMEM] * 4,
        out_shape=[
            jax.ShapeDtypeStruct((groups, feat), F32),
            jax.ShapeDtypeStruct((2, 2 * DIM, WIDE), F32),
            jax.ShapeDtypeStruct((2, WIDE), F32),
            jax.ShapeDtypeStruct((2, DIM, WIDE), F32),
        ],
        compiler_params=params(),
        cost_estimate=cost(1e6, 2 << 20),
        name="unpack",
    )(gathered)


def final_kernel(tiles_ref, count_ref, quarter_ref, next_ref, live_ref, c0, c1, c2, c3, out_ref):
    tile = 2 * quarter_ref[0] + pl.program_id(0)
    value = next_ref[...]
    for k in range(2):
        rows = slice(k * TILE, (k + 1) * TILE)
        is_live = (tile == tiles_ref[1, k]) & (count_ref[0, 1] > k)
        value = jnp.where(is_live, live_ref[rows, :], value)
    for k in range(2):
        rows = slice(k * TILE, (k + 1) * TILE)
        is_live = (tile == tiles_ref[0, k]) & (count_ref[0, 0] > k)
        source = (c0[rows, :].astype(F32) + c1[rows, :].astype(F32)) + (
            c2[rows, :].astype(F32) + c3[rows, :].astype(F32)
        )
        value = jnp.where(is_live, value + source, value)
    out_ref[...] = value.astype(BF16)


def final_pass(tiles, count, quarter_id, after, live, parts, quarter):
    feat = after.shape[1]
    blocks = quarter // TILE
    return pl.pallas_call(
        final_kernel,
        grid_spec=pltpu.PrefetchScalarGridSpec(
            num_scalar_prefetch=3,
            grid=(blocks,),
            in_specs=[pl.BlockSpec((TILE, feat), lambda i, t, c, q: (q[0] * blocks + i, 0)), whole(live.shape)]
            + [whole(parts[0].shape)] * 4,
            out_specs=pl.BlockSpec((TILE, feat), lambda i, *_: (i, 0)),
        ),
        out_shape=jax.ShapeDtypeStruct((quarter, feat), BF16),
        compiler_params=params(),
        cost_estimate=cost(1e6, 1 << 20),
        name="final",
    )(tiles, count, quarter_id, after, live, *parts)


def shards(state_zero, state_one, aggregate_one, aggregate_two, cotangent, relation_table, update_in, update_bias,
           update_out, frontier_tiles, frontier_count, edge_source, edge_relation, edge_target, edge_owner):
    block_rows, feat = state_zero.shape
    groups = relation_table.shape[0]
    group_size = lax.axis_size("rel")
    peers = lax.axis_size("ent")
    quarter = block_rows // group_size
    edges = edge_source.shape[0]
    capacity = 3 * edges // (2 * peers)
    regular = 2 * capacity // 3
    over = capacity - regular
    slots = peers * regular
    sum_rows = 8 * peers

    def exchange(chunks):
        return lax.all_to_all(chunks, "ent", split_axis=0, concat_axis=0, tiled=True)

    def over_rel(part):
        turned = [
            lax.ppermute(part, "rel", [(i, (i + k) % group_size) for i in range(group_size)])
            for k in range(1, group_size)
        ]
        return [part] + turned

    row = lambda values: values.reshape(1, edges)
    count = jnp.swapaxes(frontier_count, 0, 1)
    weights = (update_in, update_bias, jnp.swapaxes(update_out, 1, 2))
    request, ids = pl.pallas_call(
        functools.partial(slots_kernel, peers),
        in_specs=[SMEM] * 2 + [HBM] * 4,
        out_specs=[VMEM] * 2,
        out_shape=[
            jax.ShapeDtypeStruct((peers, 1, 128), F32),
            jax.ShapeDtypeStruct((2, peers, 128), F32),
        ],
        scratch_shapes=[pltpu.VMEM((1, edges), jnp.int32)] * 4 + [pltpu.SemaphoreType.DMA((4,))],
        compiler_params=params(8 << 20),
        cost_estimate=cost(1e8, 1 << 20),
        name="slots",
    )(frontier_tiles, count, *(in_hbm(row(values)) for values in (edge_owner, edge_target, edge_source, edge_relation)))
    asked = exchange(request)
    more_two = jnp.max(asked[:, 0, 31]) > regular
    more_any = jnp.maximum(jnp.max(asked[:, 0, 31]), jnp.max(asked[:, 0, 95])) > regular

    upstream_one, grad_agg, sums_two = first_pass(aggregate_two, state_one, cotangent, *weights)
    picked_two = pick(regular, 0, 0, asked, grad_agg)
    answered_two = exchange(picked_two.reshape(peers, regular, feat)).reshape(slots, feat)
    after, rest, sums_rest, live, grad_rest = rest_pass(
        regular, frontier_tiles, count, aggregate_one, state_zero, upstream_one, *weights, asked
    )
    edge_table, rows = tables_two(regular, frontier_tiles, count, ids, relation_table)
    answered_two, rest, edge_table, rows, more_two, more_any = lax.optimization_barrier(
        (answered_two, rest, edge_table, rows, more_two, more_any)
    )

    def over_two(part):
        picked = pick(over, regular, 0, asked, grad_agg)
        answer = exchange(picked.reshape(peers, over, feat)).reshape(peers * over, feat)
        return extra(1, over, regular, frontier_tiles, count, ids, relation_table, answer, state_one, part)

    part = contribution(answered_two, edge_table, rows)
    part = lax.cond(more_two, lambda part: over_two(part)[0], lambda part: part, part)
    parts = over_rel(part)
    table_one, states_one, relation_two = tables_one(
        regular, frontier_tiles, count, ids, rows, relation_table, answered_two, state_one, state_zero
    )
    parts[0], rest, table_one, states_one, relation_two = lax.optimization_barrier(
        (parts[0], rest, table_one, states_one, relation_two)
    )
    picked_one, after_live, sums_live, grad_live = live_pass(
        frontier_tiles, count, aggregate_one, state_zero, upstream_one, parts, weights, live, rest
    )
    answered_one = exchange(picked_one.reshape(peers, regular, feat)).reshape(slots, feat)
    answered_one, more_any = lax.optimization_barrier((answered_one, more_any))
    part, packed = pack_sums(
        answered_one, table_one, states_one, rows, relation_two, sums_two, sums_rest, sums_live, sum_rows
    )

    def over_any(part, packed):
        first = over_two(part)[1]
        picked = late_pick(over, regular, frontier_tiles, count, asked, grad_rest, grad_live)
        answer = exchange(picked.reshape(peers, over, feat)).reshape(peers * over, feat)
        part, second = extra(0, over, regular, frontier_tiles, count, ids, relation_table, answer, state_zero, part)
        used = first.shape[0]
        total = packed[:used, :feat].astype(F32) + (first + second)
        return part, packed.at[:used, :feat].set(total.astype(BF16))

    part, packed = lax.cond(more_any, over_any, lambda part, packed: (part, packed), part, packed)
    parts = over_rel(part)
    scale_weights = 1.0 / math.sqrt(block_rows * peers * QUERIES)
    scale_relations = math.sqrt(groups * group_size / (edges * peers * group_size))
    chunks = exchange(packed.reshape(peers, 8, feat + TILE))
    gathered = exchange(combine(chunks, feat, scale_relations, scale_weights)).reshape(sum_rows, feat + TILE)
    quarter_id = lax.axis_index("rel").astype(jnp.int32).reshape(1)
    grad_zero = final_pass(frontier_tiles, count, quarter_id, after, after_live, parts, quarter)
    relation, grad_in, grad_bias, grad_out = unpack(gathered, groups, feat)
    return grad_zero, relation, grad_in, grad_bias, jnp.swapaxes(grad_out, 1, 2)


def solution(mesh):
    in_specs = (
        P("ent", None),
        P("ent", None),
        P("ent", None),
        P("ent", None),
        P("ent", None),
        P("rel", None),
        P(),
        P(),
        P(),
        P(None, "ent"),
        P(None, "ent"),
        P(("ent", "rel")),
        P(("ent", "rel")),
        P(("ent", "rel")),
        P(("ent", "rel"), None),
    )
    out_specs = (P(("ent", "rel"), None), P("rel", None), P(), P(), P())
    return jax.shard_map(shards, mesh=mesh, in_specs=in_specs, out_specs=out_specs, check_vma=False)
```

```python
import functools
import math

import jax
import jax.numpy as jnp
from jax import lax
from jax.experimental import pallas as pl
from jax.experimental.pallas import tpu as pltpu
from jax.sharding import PartitionSpec as P

QUERIES = 8
DIM = 32
TILE = 128
WIDE = 256
HALF_Q = 4
F32 = jnp.float32
BF16 = jnp.bfloat16
VMEM = pl.BlockSpec(memory_space=pltpu.VMEM)
SMEM = pl.BlockSpec(memory_space=pltpu.SMEM)
HBM = pl.BlockSpec(memory_space=pltpu.HBM)


def in_hbm(array):
    return pltpu.with_memory_space_constraint(array, pltpu.HBM)


def iota(shape, dim):
    return lax.broadcasted_iota(jnp.int32, shape, dim)


def dot_nn(a, b):
    return lax.dot_general(a, b, (((1,), (0,)), ((), ())), preferred_element_type=F32)


def dot_nt(a, b):
    return lax.dot_general(a, b, (((1,), (1,)), ((), ())), preferred_element_type=F32)


def dot_tn(a, b):
    return lax.dot_general(a, b, (((0,), (0,)), ((), ())), preferred_element_type=F32)


def params(vmem=20 << 20):
    return pltpu.CompilerParams(vmem_limit_bytes=vmem)


def cost(flops, nbytes, trans=0):
    return pl.CostEstimate(flops=int(flops), bytes_accessed=int(nbytes), transcendentals=int(trans))


def slots_kernel(peers, tiles_ref, count_ref, owner_hbm, target_hbm, source_hbm, relation_hbm, request_ref, ids_ref,
                 owner_ref, target_ref, source_ref, relation_ref, sems):
    pairs = ((owner_hbm, owner_ref), (target_hbm, target_ref), (source_hbm, source_ref), (relation_hbm, relation_ref))
    copies = [pltpu.make_async_copy(a, b, sems.at[i]) for i, (a, b) in enumerate(pairs)]
    for copy in copies:
        copy.start()
    for copy in copies:
        copy.wait()
    edges = owner_ref.shape[1]
    hit = (iota((peers, edges), 0) == owner_ref[...]).astype(F32)
    below = (iota((TILE, TILE), 0) < iota((TILE, TILE), 1)).astype(BF16)
    tile = lax.shift_right_logical(source_ref[...], 7)
    request, tops = [], []
    for hop in (1, 0):
        live = (tile == tiles_ref[hop, 0]) | ((tile == tiles_ref[hop, 1]) & (count_ref[0, hop] > 1))
        own = jnp.where(live, hit, 0.0)
        own_low = own.astype(BF16)
        offset = jnp.zeros((peers, 1), F32)
        pieces = []
        for b in range(edges // TILE):
            block = slice(b * TILE, (b + 1) * TILE)
            pieces.append(dot_nn(own_low[:, block], below) + offset)
            offset = offset + jnp.sum(own[:, block], axis=1, keepdims=True)
        earlier = jnp.sum(jnp.concatenate(pieces, axis=1) * own, axis=0, keepdims=True).astype(jnp.int32)
        place = jnp.where((iota((32, edges), 0) == earlier) & live, 1.0, 0.0)

        def spread(values):
            high = lax.shift_right_logical(values, 5)
            low = values & 31
            return [place * high.astype(F32), place * low.astype(F32)]

        request += spread(target_ref[...])
        tops.append(jnp.max(offset, axis=0, keepdims=True))
        second = jnp.concatenate(
            spread(source_ref[...] + 1) + spread(relation_ref[...] + 1), axis=0
        ).astype(BF16)
        ids_ref[hop] = dot_nt(own_low, second)
    lane = iota((peers, 128), 1)
    sent = dot_nt(hit.astype(BF16), jnp.concatenate(request, axis=0).astype(BF16))
    sent = jnp.where(lane == 31, tops[0], sent)
    request_ref[:, 0, :] = jnp.where(lane == 95, tops[1], sent)


def slot_columns(table, capacity, bases, skip=0):
    peers = table.shape[0]
    slots = peers * capacity
    row = iota((slots, peers), 0)
    start = iota((slots, peers), 1) * capacity
    expand = ((row >= start) & (row < start + capacity)).astype(BF16)
    spread = dot_nn(expand, table.astype(BF16))
    row = iota((slots, 128), 0)
    group = ((row.astype(F32) + 0.5) * (1.0 / capacity)).astype(jnp.int32)
    place = row - group * capacity + skip
    lane = iota((slots, 128), 1)
    columns = []
    for base in bases:
        weight = jnp.where(lane == place + base, 32.0, 0.0) + jnp.where(
            lane == place + (base + 32), 1.0, 0.0
        )
        columns.append(jnp.sum(spread * weight, axis=1, keepdims=True).astype(jnp.int32))
    return columns


def compact_column(column, tiles, count):
    tile = lax.shift_right_arithmetic(column, 7)
    inner = column & 127
    result = jnp.full(column.shape, -1, jnp.int32)
    for k in range(len(tiles)):
        live = (tile == tiles[k]) & (count > k)
        result = jnp.where(live, inner + k * TILE, result)
    return result


def onehot(column, width):
    shape = (column.shape[0], width)
    lane = lax.broadcasted_iota(jnp.int16, shape, 1)
    hit = lane == jnp.broadcast_to(column, shape).astype(jnp.int16)
    return jnp.where(hit, jnp.ones((), BF16), jnp.zeros((), BF16))


def build_weights(layer, w_in_ref, w_bias_ref, w_out_ref, wx_ref, wu_ref, wb_ref):
    wx_ref[...] = jnp.zeros_like(wx_ref)
    wu_ref[...] = jnp.zeros_like(wu_ref)
    for q in range(HALF_Q):
        rows, cols = slice(q * DIM, (q + 1) * DIM), slice(q * WIDE, (q + 1) * WIDE)
        low = slice(TILE + q * DIM, TILE + (q + 1) * DIM)
        wx_ref[rows, cols] = 0.5 * w_in_ref[layer, 0:DIM, :]
        wx_ref[low, cols] = 0.5 * w_in_ref[layer, DIM:2 * DIM, :]
        wu_ref[rows, cols] = w_out_ref[layer]
        wb_ref[:, cols] = 0.5 * w_bias_ref[layer:layer + 1, :]


def mlp_half(s, agg, state, up_low, wx, wu, bias, acc_in, acc_out):
    lanes = slice(s * TILE, (s + 1) * TILE)
    x = jnp.concatenate([agg[:, lanes], state[:, lanes]], axis=1)
    up = up_low[:, lanes]
    x_turned, up_turned = x.T, up.T
    half = dot_nn(x, wx[...]) + bias[...]
    bend = jnp.tanh(half)
    above = 1.0 + bend
    act_low = (half * above).astype(BF16)
    slope = above * (1.0 + half * (1.0 - bend))
    low = (dot_nn(up, wu[...]) * slope).astype(BF16)
    ones = jnp.ones((16, x.shape[0]), BF16)
    for q in range(HALF_Q):
        cols = slice(q * WIDE, (q + 1) * WIDE)
        rows = slice(q * DIM, (q + 1) * DIM)
        low_rows = slice(TILE + q * DIM, TILE + (q + 1) * DIM)
        own = jnp.concatenate([x_turned[rows], x_turned[low_rows], ones], axis=0)
        acc_in[...] += dot_nn(own, low[:, cols])
        acc_out[...] += dot_nn(up_turned[rows], act_low[:, cols])
    return dot_nt(low, wx[...])


def store_sums(acc_in, acc_out, sums_ref):
    sums_ref[0:2 * DIM, :] = 0.5 * acc_in[0:2 * DIM, :]
    sums_ref[2 * DIM:3 * DIM, :] = acc_out[...]
    sums_ref[3 * DIM:3 * DIM + 8, :] = 0.5 * acc_in[2 * DIM:2 * DIM + 8, :]


def clear(acc_in, acc_out):
    acc_in[...] = jnp.zeros_like(acc_in)
    acc_out[...] = jnp.zeros_like(acc_out)


WEIGHT_SHAPES = [
    ((2 * TILE, HALF_Q * WIDE), BF16),
    ((TILE, HALF_Q * WIDE), BF16),
    ((1, HALF_Q * WIDE), F32),
]
SUM_SHAPES = [((2 * DIM + 16, WIDE), F32), ((DIM, WIDE), F32)]
SUM_ROWS = 3 * DIM + 8


def scratch(shapes):
    return [pltpu.VMEM(shape, dtype) for shape, dtype in shapes]


def whole(shape):
    return pl.BlockSpec(shape, lambda i, *_: (0,) * len(shape))


def pick_rows(asked, grad_agg, picked_ref, chunks=4):
    rows, slots = grad_agg.shape[0], asked.shape[0]
    step = slots // chunks
    for c in range(chunks):
        part = slice(c * step, (c + 1) * step)
        picked_ref[part, :] = dot_nn(onehot(asked[part], rows), grad_agg[...]).astype(BF16)


def dense_step(step, agg_ref, state_ref, up, up_low, wx, wu, wb, acc_in, acc_out, grad_agg, next_ref):
    rows = agg_ref.shape[0]
    aggs, states = [], []
    for s in range(2):
        grad_x = mlp_half(s, agg_ref[...], state_ref[...], up_low, wx, wu, wb, acc_in, acc_out)
        aggs.append(grad_x[:, :TILE])
        states.append(grad_x[:, TILE:])
    grad_agg[pl.ds(pl.multiple_of(step * rows, rows), rows), :] = jnp.concatenate(aggs, axis=1).astype(BF16)
    next_ref[...] = up + jnp.concatenate(states, axis=1)


def first_kernel(blocks, agg_hbm, state_hbm, up_hbm, w_in_ref, w_bias_ref, w_out_ref,
                 next_hbm, grad_agg, grad_hbm, sums_hbm, wx, wu, wb, acc_in, acc_out, sums_ref,
                 agg_buf, state_buf, up_buf, next_buf, sems, out_sems):
    rows = agg_hbm.shape[0] // blocks

    def copies(step):
        part = pl.ds(pl.multiple_of(step * rows, rows), rows)
        pairs = ((agg_hbm, agg_buf), (state_hbm, state_buf), (up_hbm, up_buf))
        return [pltpu.make_async_copy(a.at[part], b.at[part], sems.at[step, i]) for i, (a, b) in enumerate(pairs)]

    for step in range(blocks):
        for copy in copies(step):
            copy.start()
    build_weights(1, w_in_ref, w_bias_ref, w_out_ref, wx, wu, wb)
    clear(acc_in, acc_out)

    @pl.loop(0, blocks)
    def _(step):
        for copy in copies(step):
            copy.wait()
        part = pl.ds(pl.multiple_of(step * rows, rows), rows)
        up_low = up_buf[part, :]
        dense_step(step, agg_buf.at[part], state_buf.at[part], up_low.astype(F32), up_low, wx, wu, wb,
                   acc_in, acc_out, grad_agg, next_buf.at[part])

    store_sums(acc_in, acc_out, sums_ref)
    pairs = ((next_buf, next_hbm), (grad_agg, grad_hbm), (sums_ref, sums_hbm))
    copies = [pltpu.make_async_copy(a, b, out_sems.at[i]) for i, (a, b) in enumerate(pairs)]
    for copy in copies:
        copy.start()
    for copy in copies:
        copy.wait()


def first_pass(agg, state, up, w_in, w_bias, w_out):
    rows, feat = agg.shape
    blocks = rows // 512
    return pl.pallas_call(
        functools.partial(first_kernel, blocks),
        in_specs=[HBM, HBM, HBM, VMEM, VMEM, VMEM],
        out_specs=[HBM, VMEM, HBM, HBM],
        out_shape=[
            pltpu.HBM((rows, feat), F32),
            jax.ShapeDtypeStruct((rows, feat), BF16),
            pltpu.HBM((rows, feat), BF16),
            pltpu.HBM((SUM_ROWS, WIDE), F32),
        ],
        scratch_shapes=scratch(WEIGHT_SHAPES + SUM_SHAPES)
        + [pltpu.VMEM((SUM_ROWS, WIDE), F32)]
        + [pltpu.VMEM((rows, feat), BF16)] * 3
        + [pltpu.VMEM((rows, feat), F32), pltpu.SemaphoreType.DMA((blocks, 3)), pltpu.SemaphoreType.DMA((3,))],
        compiler_params=params(),
        cost_estimate=cost(5.4e9, 4 << 20, 2 << 20),
        name="first",
    )(in_hbm(agg), in_hbm(state), in_hbm(up), w_in, w_bias, w_out)


def pick_kernel(capacity, skip, base, asked_ref, grad_agg, picked_ref, two_ref, any_ref):
    two, one = jnp.max(asked_ref[:, 0, 31:32]), jnp.max(asked_ref[:, 0, 95:96])
    two_ref[0] = (two > capacity).astype(jnp.int32)
    any_ref[0] = (jnp.maximum(two, one) > capacity).astype(jnp.int32)
    asked = slot_columns(asked_ref[:, 0, :], capacity, (base,), skip)[0]
    pick_rows(asked, grad_agg, picked_ref)


def pick(capacity, skip, base, asked, grad_agg):
    slots, feat = asked.shape[0] * capacity, grad_agg.shape[1]
    return pl.pallas_call(
        functools.partial(pick_kernel, capacity, skip, base),
        in_specs=[VMEM, VMEM],
        out_specs=[VMEM, SMEM, SMEM],
        out_shape=[
            jax.ShapeDtypeStruct((slots, feat), BF16),
            jax.ShapeDtypeStruct((1,), jnp.int32),
            jax.ShapeDtypeStruct((1,), jnp.int32),
        ],
        compiler_params=params(12 << 20),
        cost_estimate=cost(8e8, 1 << 20),
        name="pick",
    )(asked, grad_agg)


def rest_kernel(capacity, tiles_ref, count_ref, agg_ref, state_ref, up_ref, w_in_ref, w_bias_ref, w_out_ref,
                asked_ref, next_ref, picked_ref, sums_ref, live_ref, grad_agg, wx, wu, wb,
                acc_in, acc_out):
    step = pl.program_id(0)
    rows = agg_ref.shape[0]
    count = count_ref[0, 1]

    @pl.when(step == 0)
    def _():
        build_weights(0, w_in_ref, w_bias_ref, w_out_ref, wx, wu, wb)
        clear(acc_in, acc_out)

    up = up_ref[...]
    tile = lax.shift_right_logical(iota((rows, 1), 0) + step * rows, 7)
    dead = (tile == tiles_ref[1, 0]) | ((tile == tiles_ref[1, 1]) & (count > 1))
    up_low = jnp.where(dead, 0.0, up).astype(BF16)
    dense_step(step, agg_ref, state_ref, up, up_low, wx, wu, wb, acc_in, acc_out, grad_agg, next_ref)

    @pl.when(step == pl.num_programs(0) - 1)
    def _():
        store_sums(acc_in, acc_out, sums_ref)
        asked = slot_columns(asked_ref[:, 0, :], capacity, (64,))[0]
        live_ref[...] = onehot(compact_column(asked, (tiles_ref[1, 0], tiles_ref[1, 1]), count), 2 * TILE)
        pick_rows(asked, grad_agg, picked_ref)


def rest_pass(capacity, tiles, count, agg, state, up, w_in, w_bias, w_out, asked):
    rows, feat = agg.shape
    slots = asked.shape[0] * capacity
    block = 512
    row_spec = pl.BlockSpec((block, feat), lambda i: (i, 0))
    return pl.pallas_call(
        functools.partial(rest_kernel, capacity),
        grid=(rows // block,),
        in_specs=[SMEM, SMEM, row_spec, row_spec, row_spec, whole(w_in.shape), whole(w_bias.shape),
                  whole(w_out.shape), whole(asked.shape)],
        out_specs=[row_spec, whole((slots, feat)), whole((SUM_ROWS, WIDE)), whole((slots, 2 * TILE)),
                   whole((rows, feat))],
        out_shape=[
            pltpu.HBM((rows, feat), F32),
            pltpu.HBM((slots, feat), BF16),
            pltpu.HBM((SUM_ROWS, WIDE), F32),
            pltpu.HBM((slots, 2 * TILE), BF16),
            pltpu.HBM((rows, feat), BF16),
        ],
        scratch_shapes=scratch(WEIGHT_SHAPES + SUM_SHAPES),
        compiler_params=params(),
        cost_estimate=cost(5.4e9, 4 << 20, 2 << 20),
        name="rest",
    )(tiles, count, in_hbm(agg), in_hbm(state), in_hbm(up), w_in, w_bias, w_out, asked)


def as_row(column):
    return jnp.broadcast_to(column.astype(F32), (column.shape[0], TILE)).T[0:8].astype(jnp.int32)


def onehot_rows(row, width):
    return (iota((width, row.shape[1]), 0) == row).astype(F32).astype(BF16)


def relation_rows(relation, table_ref):
    width = -(-table_ref.shape[0] // TILE) * TILE
    pad = width - table_ref.shape[0]
    table = jnp.concatenate([table_ref[...], jnp.zeros((pad, table_ref.shape[1]), BF16)], axis=0)
    return dot_nn(onehot(relation, width), table).astype(BF16)


def tables_two_kernel(capacity, tiles_ref, count_ref, ids_ref, table_ref, t_ref, rows_ref):
    for hop in range(2):
        source, relation = slot_columns(ids_ref[hop], capacity, (0, 64))
        if hop == 1:
            t_ref[...] = relation_rows(relation - 1, table_ref)
        rows_ref[hop] = as_row(relation - 1)
        column = compact_column(source - 1, (tiles_ref[hop, 0], tiles_ref[hop, 1]), count_ref[0, hop])
        rows_ref[2 + hop] = as_row(column)


def tables_two(capacity, tiles, count, ids, table):
    feat = table.shape[1]
    slots = ids.shape[1] * capacity
    return pl.pallas_call(
        functools.partial(tables_two_kernel, capacity),
        in_specs=[SMEM, SMEM, VMEM, VMEM],
        out_specs=[VMEM, VMEM],
        out_shape=[
            jax.ShapeDtypeStruct((slots, feat), BF16),
            jax.ShapeDtypeStruct((4, 8, slots), jnp.int32),
        ],
        compiler_params=params(),
        cost_estimate=cost(1e9, 2 << 20),
        name="tables_two",
    )(tiles, count, ids, table)


def tables_one_kernel(capacity, tiles_ref, count_ref, ids_ref, rows_ref, table_ref, answer_ref,
                      one_a, one_b, zero_a, zero_b, t_ref, h_ref, total_ref):
    states = []
    for hop, a, b in ((0, zero_a, zero_b), (1, one_a, one_b)):
        source, relation = slot_columns(ids_ref[hop], capacity, (0, 64))
        column = compact_column(source - 1, (tiles_ref[hop, 0], tiles_ref[hop, 1]), count_ref[0, hop])
        states.append(dot_nn(onehot(column, 2 * TILE), jnp.concatenate([a[...], b[...]], axis=0)).astype(BF16))
        if hop == 0:
            t_ref[...] = relation_rows(relation - 1, table_ref)
    h_ref[...] = states[0]
    total_ref[...] = dot_nn(onehot_rows(rows_ref[1, 0:1, :], total_ref.shape[0]), answer_ref[...] * states[1])


def tables_one(capacity, tiles, count, ids, rows, table, answer, state_one, state_zero):
    slots, feat = answer.shape
    width = -(-table.shape[0] // TILE) * TILE

    def tile(hop, k):
        return pl.BlockSpec((TILE, feat), lambda i, tiles, count: (tiles[hop, k], 0))

    return pl.pallas_call(
        functools.partial(tables_one_kernel, capacity),
        grid_spec=pltpu.PrefetchScalarGridSpec(
            num_scalar_prefetch=2,
            grid=(1,),
            in_specs=[whole(ids.shape), whole(rows.shape), whole(table.shape), whole(answer.shape), tile(1, 0),
                      tile(1, 1), tile(0, 0), tile(0, 1)],
            out_specs=[whole((slots, feat)), whole((slots, feat)), whole((width, feat))],
        ),
        out_shape=[
            jax.ShapeDtypeStruct((slots, feat), BF16),
            jax.ShapeDtypeStruct((slots, feat), BF16),
            jax.ShapeDtypeStruct((width, feat), F32),
        ],
        compiler_params=params(),
        cost_estimate=cost(2e9, 4 << 20),
        name="tables_one",
    )(tiles, count, ids, rows, table, answer, state_one, state_one, state_zero, state_zero)


def extra_kernel(hop, capacity, skip, tiles_ref, count_ref, ids_ref, table_ref, answer_ref, state_a, state_b,
                 part_ref, out_ref, total_ref):
    source, relation = slot_columns(ids_ref[hop], capacity, (0, 64), skip)
    column = compact_column(source - 1, (tiles_ref[hop, 0], tiles_ref[hop, 1]), count_ref[0, hop])
    select = onehot(column, 2 * TILE)
    answer = answer_ref[...]
    more = dot_nn(onehot_rows(as_row(column)[0:1], 2 * TILE), answer * relation_rows(relation - 1, table_ref))
    out_ref[...] = (part_ref[...].astype(F32) + more).astype(BF16)
    states = dot_nn(select, jnp.concatenate([state_a[...], state_b[...]], axis=0)).astype(BF16)
    total_ref[...] = dot_nn(onehot_rows(as_row(relation - 1)[0:1], total_ref.shape[0]), answer * states)


def extra(hop, capacity, skip, tiles, count, ids, table, answer, state, part):
    feat = answer.shape[1]
    width = -(-table.shape[0] // TILE) * TILE

    def tile(k):
        return pl.BlockSpec((TILE, feat), lambda i, tiles, count: (tiles[hop, k], 0))

    return pl.pallas_call(
        functools.partial(extra_kernel, hop, capacity, skip),
        grid_spec=pltpu.PrefetchScalarGridSpec(
            num_scalar_prefetch=2,
            grid=(1,),
            in_specs=[whole(ids.shape), whole(table.shape), whole(answer.shape), tile(0), tile(1), whole(part.shape)],
            out_specs=[whole(part.shape), whole((width, feat))],
        ),
        out_shape=[jax.ShapeDtypeStruct(part.shape, BF16), jax.ShapeDtypeStruct((width, feat), F32)],
        compiler_params=params(),
        cost_estimate=cost(1e9, 2 << 20),
        name="extra",
    )(tiles, count, ids, table, answer, state, state, part)


def contribution_kernel(answer_ref, t_ref, rows_ref, out_ref):
    select = onehot_rows(rows_ref[3, 0:1, :], 2 * TILE)
    out_ref[...] = dot_nn(select, answer_ref[...] * t_ref[...]).astype(BF16)


def contribution(answer, table, rows):
    return pl.pallas_call(
        contribution_kernel,
        in_specs=[VMEM] * 3,
        out_specs=VMEM,
        out_shape=jax.ShapeDtypeStruct((2 * TILE, answer.shape[1]), BF16),
        compiler_params=params(8 << 20),
        cost_estimate=cost(2e8, 3 << 20),
        name="contribution",
    )(answer, table, rows)


def live_kernel(tiles_ref, count_ref, agg_a, agg_b, state_a, state_b, up_a, up_b, c0, c1, c2, c3,
                w_in_ref, w_bias_ref, w_out_ref, live_ref, rest_ref, picked_ref, next_ref, sums_ref, grad_ref,
                wx, wu, wb, acc_in, acc_out):
    build_weights(0, w_in_ref, w_bias_ref, w_out_ref, wx, wu, wb)
    clear(acc_in, acc_out)
    source = (c0[...].astype(F32) + c1[...].astype(F32)) + (c2[...].astype(F32) + c3[...].astype(F32))
    up = jnp.concatenate([up_a[...], up_b[...]], axis=0) + source
    keep = (iota((2 * TILE, 1), 0) < TILE) | (count_ref[0, 1] > 1)
    up_low = jnp.where(keep, up, 0.0).astype(BF16)
    agg = jnp.concatenate([agg_a[...], agg_b[...]], axis=0)
    state = jnp.concatenate([state_a[...], state_b[...]], axis=0)
    aggs, states = [], []
    for s in range(2):
        grad_x = mlp_half(s, agg, state, up_low, wx, wu, wb, acc_in, acc_out)
        aggs.append(grad_x[:, :TILE])
        states.append(grad_x[:, TILE:])
    grad_agg = jnp.concatenate(aggs, axis=1).astype(BF16)
    next_ref[...] = up + jnp.concatenate(states, axis=1)
    store_sums(acc_in, acc_out, sums_ref)
    grad_ref[...] = grad_agg
    picked_ref[...] = (dot_nn(live_ref[...], grad_agg) + rest_ref[...].astype(F32)).astype(BF16)


def live_pass(tiles, count, agg, state, up, parts, weights, live, rest):
    feat = agg.shape[1]

    def tile(k):
        return pl.BlockSpec((TILE, feat), lambda i, tiles, count: (tiles[1, k], 0))

    return pl.pallas_call(
        live_kernel,
        grid_spec=pltpu.PrefetchScalarGridSpec(
            num_scalar_prefetch=2,
            grid=(1,),
            in_specs=[tile(0), tile(1)] * 3 + [whole(parts[0].shape)] * 4
            + [whole(w.shape) for w in weights] + [whole(live.shape), whole(rest.shape)],
            out_specs=[whole(rest.shape), whole((2 * TILE, feat)), whole((SUM_ROWS, WIDE)), whole((2 * TILE, feat))],
            scratch_shapes=scratch(WEIGHT_SHAPES + SUM_SHAPES),
        ),
        out_shape=[
            jax.ShapeDtypeStruct(rest.shape, BF16),
            jax.ShapeDtypeStruct((2 * TILE, feat), F32),
            jax.ShapeDtypeStruct((SUM_ROWS, WIDE), F32),
            pltpu.HBM((2 * TILE, feat), BF16),
        ],
        compiler_params=params(),
        cost_estimate=cost(1.6e9, 4 << 20, 1 << 19),
        name="live",
    )(tiles, count, agg, agg, state, state, up, up, *parts, *weights, live, rest)


def late_kernel(capacity, skip, tiles_ref, count_ref, asked_ref, rest_ref, live_ref, picked_ref):
    asked = slot_columns(asked_ref[:, 0, :], capacity, (64,), skip)[0]
    column = compact_column(asked, (tiles_ref[1, 0], tiles_ref[1, 1]), count_ref[0, 1])
    rest = dot_nn(onehot(asked, rest_ref.shape[0]), rest_ref[...])
    picked_ref[...] = (dot_nn(onehot(column, 2 * TILE), live_ref[...]) + rest).astype(BF16)


def late_pick(capacity, skip, tiles, count, asked, rest, live):
    slots, feat = asked.shape[0] * capacity, rest.shape[1]
    return pl.pallas_call(
        functools.partial(late_kernel, capacity, skip),
        in_specs=[SMEM, SMEM, VMEM, VMEM, VMEM],
        out_specs=VMEM,
        out_shape=jax.ShapeDtypeStruct((slots, feat), BF16),
        compiler_params=params(),
        cost_estimate=cost(8e8, 1 << 20),
        name="late_pick",
    )(tiles, count, asked, rest, live)


GAP = SUM_ROWS


def pack_kernel(answer_ref, t_ref, h_ref, rows_ref, before_ref, w2_ref, w1a_ref, w1b_ref, part_ref, out_ref):
    answer = answer_ref[...]
    part_ref[...] = dot_nn(onehot_rows(rows_ref[2, 0:1, :], 2 * TILE), answer * t_ref[...]).astype(BF16)
    select = onehot_rows(rows_ref[0, 0:1, :], before_ref.shape[0])
    total = before_ref[...] + dot_nn(select, answer * h_ref[...])
    used, feat = total.shape
    out_ref[used:, 0:feat] = jnp.zeros((out_ref.shape[0] - used, feat), BF16)
    out_ref[4 * GAP:, feat:feat + TILE] = jnp.zeros((out_ref.shape[0] - 4 * GAP, TILE), BF16)
    out_ref[0:used, 0:feat] = total.astype(BF16)
    layers = (w1a_ref[...] + w1b_ref[...], w2_ref[...])
    parts = []
    for layer in layers:
        parts += [layer[:, :TILE], layer[:, TILE:]]
    out_ref[0:4 * GAP, feat:feat + TILE] = jnp.concatenate(parts, axis=0).astype(BF16)


def pack_sums(answer, table, states, ids, before, w2, w1a, w1b, rows):
    feat = answer.shape[1]
    return pl.pallas_call(
        pack_kernel,
        in_specs=[VMEM] * 8,
        out_specs=[VMEM, VMEM],
        out_shape=[
            jax.ShapeDtypeStruct((2 * TILE, feat), BF16),
            jax.ShapeDtypeStruct((rows, feat + TILE), BF16),
        ],
        compiler_params=params(),
        cost_estimate=cost(4e8, 4 << 20),
        name="pack_sums",
    )(answer, table, states, ids, before, w2, w1a, w1b)


def combine_kernel(feat, scale_relations, scale_weights, in_ref, out_ref):
    total = jnp.sum(in_ref[...].astype(F32), axis=0)
    lane = iota(total.shape, 1)
    total = total * jnp.where(lane < feat, scale_relations, scale_weights)
    out_ref[...] = jnp.broadcast_to(total.astype(BF16)[None], out_ref.shape)


def combine(chunks, feat, scale_relations, scale_weights):
    return pl.pallas_call(
        functools.partial(combine_kernel, feat, scale_relations, scale_weights),
        in_specs=[VMEM],
        out_specs=VMEM,
        out_shape=jax.ShapeDtypeStruct(chunks.shape, BF16),
        compiler_params=params(),
        cost_estimate=cost(1e6, 1 << 20),
        name="combine",
    )(chunks)


def unpack_kernel(feat, in_ref, relation_ref, w_in_ref, w_bias_ref, w_out_ref):
    groups = relation_ref.shape[0]
    relation_ref[...] = in_ref[0:groups, 0:feat].astype(F32)
    for layer in range(2):
        at = 2 * layer * GAP
        left = in_ref[at:at + GAP, feat:feat + TILE].astype(F32)
        right = in_ref[at + GAP:at + 2 * GAP, feat:feat + TILE].astype(F32)
        both = jnp.concatenate([left, right], axis=1)
        w_in_ref[layer] = both[0:2 * DIM]
        w_out_ref[layer] = both[2 * DIM:3 * DIM]
        w_bias_ref[layer:layer + 1, :] = both[3 * DIM:3 * DIM + 1]


def unpack(gathered, groups, feat):
    return pl.pallas_call(
        functools.partial(unpack_kernel, feat),
        in_specs=[VMEM],
        out_specs=[VMEM] * 4,
        out_shape=[
            jax.ShapeDtypeStruct((groups, feat), F32),
            jax.ShapeDtypeStruct((2, 2 * DIM, WIDE), F32),
            jax.ShapeDtypeStruct((2, WIDE), F32),
            jax.ShapeDtypeStruct((2, DIM, WIDE), F32),
        ],
        compiler_params=params(),
        cost_estimate=cost(1e6, 2 << 20),
        name="unpack",
    )(gathered)


def final_kernel(tiles_ref, count_ref, quarter_ref, next_ref, live_ref, c0, c1, c2, c3, out_ref):
    tile = 2 * quarter_ref[0] + pl.program_id(0)
    value = next_ref[...]
    for k in range(2):
        rows = slice(k * TILE, (k + 1) * TILE)
        is_live = (tile == tiles_ref[1, k]) & (count_ref[0, 1] > k)
        value = jnp.where(is_live, live_ref[rows, :], value)
    for k in range(2):
        rows = slice(k * TILE, (k + 1) * TILE)
        is_live = (tile == tiles_ref[0, k]) & (count_ref[0, 0] > k)
        source = (c0[rows, :].astype(F32) + c1[rows, :].astype(F32)) + (
            c2[rows, :].astype(F32) + c3[rows, :].astype(F32)
        )
        value = jnp.where(is_live, value + source, value)
    out_ref[...] = value.astype(BF16)


def final_pass(tiles, count, quarter_id, after, live, parts, quarter):
    feat = after.shape[1]
    blocks = quarter // TILE
    return pl.pallas_call(
        final_kernel,
        grid_spec=pltpu.PrefetchScalarGridSpec(
            num_scalar_prefetch=3,
            grid=(blocks,),
            in_specs=[pl.BlockSpec((TILE, feat), lambda i, t, c, q: (q[0] * blocks + i, 0)), whole(live.shape)]
            + [whole(parts[0].shape)] * 4,
            out_specs=pl.BlockSpec((TILE, feat), lambda i, *_: (i, 0)),
        ),
        out_shape=jax.ShapeDtypeStruct((quarter, feat), BF16),
        compiler_params=params(),
        cost_estimate=cost(1e6, 1 << 20),
        name="final",
    )(tiles, count, quarter_id, after, live, *parts)


def shards(state_zero, state_one, aggregate_one, aggregate_two, cotangent, relation_table, update_in, update_bias,
           update_out, frontier_tiles, frontier_count, edge_source, edge_relation, edge_target, edge_owner):
    block_rows, feat = state_zero.shape
    groups = relation_table.shape[0]
    group_size = lax.axis_size("rel")
    peers = lax.axis_size("ent")
    quarter = block_rows // group_size
    edges = edge_source.shape[0]
    capacity = 3 * edges // (2 * peers)
    regular = 2 * capacity // 3
    over = capacity - regular
    slots = peers * regular
    sum_rows = 8 * peers

    def exchange(chunks):
        return lax.all_to_all(chunks, "ent", split_axis=0, concat_axis=0, tiled=True)

    def over_rel(part):
        turned = [
            lax.ppermute(part, "rel", [(i, (i + k) % group_size) for i in range(group_size)])
            for k in range(1, group_size)
        ]
        return [part] + turned

    row = lambda values: values.reshape(1, edges)
    count = jnp.swapaxes(frontier_count, 0, 1)
    weights = (update_in, update_bias, jnp.swapaxes(update_out, 1, 2))
    request, ids = pl.pallas_call(
        functools.partial(slots_kernel, peers),
        in_specs=[SMEM] * 2 + [HBM] * 4,
        out_specs=[VMEM] * 2,
        out_shape=[
            jax.ShapeDtypeStruct((peers, 1, 128), F32),
            jax.ShapeDtypeStruct((2, peers, 128), F32),
        ],
        scratch_shapes=[pltpu.VMEM((1, edges), jnp.int32)] * 4 + [pltpu.SemaphoreType.DMA((4,))],
        compiler_params=params(8 << 20),
        cost_estimate=cost(1e8, 1 << 20),
        name="slots",
    )(in_hbm(frontier_tiles), in_hbm(count), *(in_hbm(row(values)) for values in (edge_owner, edge_target, edge_source, edge_relation)))
    asked = exchange(request)

    upstream_one, grad_agg, grad_kept, sums_two = first_pass(aggregate_two, state_one, cotangent, *weights)
    picked_two, more_two, more_any = pick(regular, 0, 0, asked, grad_agg)
    more_two, more_any = more_two[0], more_any[0]
    answered_two = exchange(picked_two.reshape(peers, regular, feat)).reshape(slots, feat)
    after, rest, sums_rest, live, grad_rest = rest_pass(
        regular, frontier_tiles, count, aggregate_one, state_zero, upstream_one, *weights, asked
    )
    edge_table, rows = tables_two(regular, frontier_tiles, count, ids, relation_table)
    answered_two, rest, edge_table, rows, more_two, more_any = lax.optimization_barrier(
        (answered_two, rest, edge_table, rows, more_two, more_any)
    )

    def over_two(part):
        picked = pick(over, regular, 0, asked, in_hbm(grad_kept))[0]
        answer = exchange(picked.reshape(peers, over, feat)).reshape(peers * over, feat)
        return extra(
            1, over, regular, frontier_tiles, count, in_hbm(ids), in_hbm(relation_table), answer, in_hbm(state_one), part
        )

    part = contribution(answered_two, edge_table, rows)
    part = lax.switch(more_two, (lambda part: part, lambda part: over_two(part)[0]), part)
    parts = over_rel(part)
    table_one, states_one, relation_two = tables_one(
        regular, frontier_tiles, count, ids, rows, relation_table, answered_two, state_one, state_zero
    )
    parts[0], rest, table_one, states_one, relation_two = lax.optimization_barrier(
        (parts[0], rest, table_one, states_one, relation_two)
    )
    picked_one, after_live, sums_live, grad_live = live_pass(
        frontier_tiles, count, aggregate_one, state_zero, upstream_one, parts, weights, live, rest
    )
    answered_one = exchange(picked_one.reshape(peers, regular, feat)).reshape(slots, feat)
    answered_one, more_any = lax.optimization_barrier((answered_one, more_any))
    part, packed = pack_sums(
        answered_one, table_one, states_one, rows, relation_two, sums_two, sums_rest, sums_live, sum_rows
    )

    def over_any(part, packed):
        first = over_two(part)[1]
        picked = late_pick(over, regular, frontier_tiles, count, asked, in_hbm(grad_rest), in_hbm(grad_live))
        answer = exchange(picked.reshape(peers, over, feat)).reshape(peers * over, feat)
        part, second = extra(
            0, over, regular, frontier_tiles, count, in_hbm(ids), in_hbm(relation_table), answer, in_hbm(state_zero), part
        )
        used = first.shape[0]
        total = packed[:used, :feat].astype(F32) + (first + second)
        return part, packed.at[:used, :feat].set(total.astype(BF16))

    part, packed = lax.switch(more_any, (lambda part, packed: (part, packed), over_any), part, packed)
    parts = over_rel(part)
    scale_weights = 1.0 / math.sqrt(block_rows * peers * QUERIES)
    scale_relations = math.sqrt(groups * group_size / (edges * peers * group_size))
    chunks = exchange(packed.reshape(peers, 8, feat + TILE))
    gathered = exchange(combine(chunks, feat, scale_relations, scale_weights)).reshape(sum_rows, feat + TILE)
    quarter_id = lax.axis_index("rel").astype(jnp.int32).reshape(1)
    grad_zero = final_pass(frontier_tiles, count, quarter_id, after, after_live, parts, quarter)
    relation, grad_in, grad_bias, grad_out = unpack(gathered, groups, feat)
    return grad_zero, relation, grad_in, grad_bias, jnp.swapaxes(grad_out, 1, 2)


def solution(mesh):
    in_specs = (
        P("ent", None),
        P("ent", None),
        P("ent", None),
        P("ent", None),
        P("ent", None),
        P("rel", None),
        P(),
        P(),
        P(),
        P(None, "ent"),
        P(None, "ent"),
        P(("ent", "rel")),
        P(("ent", "rel")),
        P(("ent", "rel")),
        P(("ent", "rel"), None),
    )
    out_specs = (P(("ent", "rel"), None), P("rel", None), P(), P(), P())
    return jax.shard_map(shards, mesh=mesh, in_specs=in_specs, out_specs=out_specs, check_vma=False)
```

```python
import functools
import math

import jax
import jax.numpy as jnp
from jax import lax
from jax.experimental import pallas as pl
from jax.experimental.pallas import tpu as pltpu
from jax.sharding import PartitionSpec as P

QUERIES = 8
DIM = 32
TILE = 128
WIDE = 256
HALF_Q = 4
F32 = jnp.float32
BF16 = jnp.bfloat16
VMEM = pl.BlockSpec(memory_space=pltpu.VMEM)
SMEM = pl.BlockSpec(memory_space=pltpu.SMEM)
HBM = pl.BlockSpec(memory_space=pltpu.HBM)


def in_hbm(array):
    return pltpu.with_memory_space_constraint(array, pltpu.HBM)


def iota(shape, dim):
    return lax.broadcasted_iota(jnp.int32, shape, dim)


def dot_nn(a, b):
    return lax.dot_general(a, b, (((1,), (0,)), ((), ())), preferred_element_type=F32)


def dot_nt(a, b):
    return lax.dot_general(a, b, (((1,), (1,)), ((), ())), preferred_element_type=F32)


def dot_tn(a, b):
    return lax.dot_general(a, b, (((0,), (0,)), ((), ())), preferred_element_type=F32)


def params(vmem=20 << 20):
    return pltpu.CompilerParams(vmem_limit_bytes=vmem)


def cost(flops, nbytes, trans=0):
    return pl.CostEstimate(flops=int(flops), bytes_accessed=int(nbytes), transcendentals=int(trans))


def slots_kernel(peers, tiles_hbm, count_hbm, owner_hbm, target_hbm, source_hbm, relation_hbm, request_ref, ids_ref,
                 tiles_ref, count_ref, owner_ref, target_ref, source_ref, relation_ref, sems):
    pairs = (
        (owner_hbm, owner_ref), (source_hbm, source_ref), (tiles_hbm, tiles_ref), (count_hbm, count_ref),
        (target_hbm, target_ref), (relation_hbm, relation_ref),
    )
    copies = [pltpu.make_async_copy(a, b, sems.at[i]) for i, (a, b) in enumerate(pairs)]
    for copy in copies:
        copy.start()
    for copy in copies:
        copy.wait()
    edges = owner_ref.shape[1]
    hit = (iota((peers, edges), 0) == owner_ref[...]).astype(F32)
    below = (iota((TILE, TILE), 0) < iota((TILE, TILE), 1)).astype(BF16)
    tile = lax.shift_right_logical(source_ref[...], 7)
    request, tops = [], []
    for hop in (1, 0):
        first, second = tiles_ref[hop:hop + 1, 0:1], tiles_ref[hop:hop + 1, 1:2]
        live = (tile == first) | ((tile == second) & (count_ref[0:1, hop:hop + 1] > 1))
        own = jnp.where(live, hit, 0.0)
        own_low = own.astype(BF16)
        offset = jnp.zeros((peers, 1), F32)
        pieces = []
        for b in range(edges // TILE):
            block = slice(b * TILE, (b + 1) * TILE)
            pieces.append(dot_nn(own_low[:, block], below) + offset)
            offset = offset + jnp.sum(own[:, block], axis=1, keepdims=True)
        earlier = jnp.sum(jnp.concatenate(pieces, axis=1) * own, axis=0, keepdims=True).astype(jnp.int32)
        place = jnp.where((iota((32, edges), 0) == earlier) & live, 1.0, 0.0)

        def spread(values):
            high = lax.shift_right_logical(values, 5)
            low = values & 31
            return [place * high.astype(F32), place * low.astype(F32)]

        request += spread(target_ref[...])
        tops.append(jnp.max(offset, axis=0, keepdims=True))
        second = jnp.concatenate(
            spread(source_ref[...] + 1) + spread(relation_ref[...] + 1), axis=0
        ).astype(BF16)
        ids_ref[hop] = dot_nt(own_low, second)
    lane = iota((peers, 128), 1)
    sent = dot_nt(hit.astype(BF16), jnp.concatenate(request, axis=0).astype(BF16))
    sent = jnp.where(lane == 31, tops[0], sent)
    request_ref[:, 0, :] = jnp.where(lane == 95, tops[1], sent)


def slot_columns(table, capacity, bases, skip=0):
    peers = table.shape[0]
    slots = peers * capacity
    row = iota((slots, peers), 0)
    start = iota((slots, peers), 1) * capacity
    expand = ((row >= start) & (row < start + capacity)).astype(BF16)
    spread = dot_nn(expand, table.astype(BF16))
    row = iota((slots, 128), 0)
    group = ((row.astype(F32) + 0.5) * (1.0 / capacity)).astype(jnp.int32)
    place = row - group * capacity + skip
    lane = iota((slots, 128), 1)
    columns = []
    for base in bases:
        weight = jnp.where(lane == place + base, 32.0, 0.0) + jnp.where(
            lane == place + (base + 32), 1.0, 0.0
        )
        columns.append(dot_nn((spread * weight).astype(BF16), jnp.ones((128, 128), BF16)).astype(jnp.int32))
    return columns


def compact_column(column, tiles, count):
    tile = lax.shift_right_arithmetic(column, 7)
    inner = column & 127
    result = jnp.full(column.shape, -1, jnp.int32)
    for k in range(len(tiles)):
        live = (tile == tiles[k]) & (count > k)
        result = jnp.where(live, inner + k * TILE, result)
    return result


def onehot(column, width):
    column = column.astype(jnp.int16)
    lane = lax.broadcasted_iota(jnp.int16, column.shape, 1)
    one, zero = jnp.ones((), BF16), jnp.zeros((), BF16)
    parts = [jnp.where(lane == column - t, one, zero) for t in range(0, width, TILE)]
    return jnp.concatenate(parts, axis=1)


def build_weights(layer, w_in_ref, w_bias_ref, w_out_ref, wx_ref, wu_ref, wb_ref):
    wx_ref[...] = jnp.zeros_like(wx_ref)
    wu_ref[...] = jnp.zeros_like(wu_ref)
    for q in range(HALF_Q):
        rows, cols = slice(q * DIM, (q + 1) * DIM), slice(q * WIDE, (q + 1) * WIDE)
        low = slice(TILE + q * DIM, TILE + (q + 1) * DIM)
        wx_ref[rows, cols] = 0.5 * w_in_ref[layer, 0:DIM, :]
        wx_ref[low, cols] = 0.5 * w_in_ref[layer, DIM:2 * DIM, :]
        wu_ref[rows, cols] = w_out_ref[layer]
        wb_ref[:, cols] = 0.5 * w_bias_ref[layer:layer + 1, :]


def mlp_half(s, agg, state, up_low, wx, wu, bias, acc_in, acc_out):
    lanes = slice(s * TILE, (s + 1) * TILE)
    x = jnp.concatenate([agg[:, lanes], state[:, lanes]], axis=1)
    up = up_low[:, lanes]
    x_turned, up_turned = x.T, up.T
    half = dot_nn(x, wx[...]) + bias[...]
    bend = jnp.tanh(half)
    above = 1.0 + bend
    act_low = (half * above).astype(BF16)
    slope = above * (1.0 + half * (1.0 - bend))
    low = (dot_nn(up, wu[...]) * slope).astype(BF16)
    ones = jnp.ones((16, x.shape[0]), BF16)
    for q in range(HALF_Q):
        cols = slice(q * WIDE, (q + 1) * WIDE)
        rows = slice(q * DIM, (q + 1) * DIM)
        low_rows = slice(TILE + q * DIM, TILE + (q + 1) * DIM)
        own = jnp.concatenate([x_turned[rows], x_turned[low_rows], ones], axis=0)
        acc_in[...] += dot_nn(own, low[:, cols])
        acc_out[...] += dot_nn(up_turned[rows], act_low[:, cols])
    return dot_nt(low, wx[...])


def store_sums(acc_in, acc_out, sums_ref):
    sums_ref[0:2 * DIM, :] = 0.5 * acc_in[0:2 * DIM, :]
    sums_ref[2 * DIM:3 * DIM, :] = acc_out[...]
    sums_ref[3 * DIM:3 * DIM + 8, :] = 0.5 * acc_in[2 * DIM:2 * DIM + 8, :]


def clear(acc_in, acc_out):
    acc_in[...] = jnp.zeros_like(acc_in)
    acc_out[...] = jnp.zeros_like(acc_out)


WEIGHT_SHAPES = [
    ((2 * TILE, HALF_Q * WIDE), BF16),
    ((TILE, HALF_Q * WIDE), BF16),
    ((1, HALF_Q * WIDE), F32),
]
SUM_SHAPES = [((2 * DIM + 16, WIDE), F32), ((DIM, WIDE), F32)]
SUM_ROWS = 3 * DIM + 8


def scratch(shapes):
    return [pltpu.VMEM(shape, dtype) for shape, dtype in shapes]


def whole(shape):
    return pl.BlockSpec(shape, lambda i, *_: (0,) * len(shape))


def pick_rows(asked, grad_agg, picked_ref, chunks=4):
    rows, slots = grad_agg.shape[0], asked.shape[0]
    step = slots // chunks
    for c in range(chunks):
        part = slice(c * step, (c + 1) * step)
        picked_ref[part, :] = dot_nn(onehot(asked[part], rows), grad_agg[...]).astype(BF16)


def dense_step(step, agg_ref, state_ref, up, up_low, wx, wu, wb, acc_in, acc_out, grad_agg, next_ref):
    rows = agg_ref.shape[0]
    aggs, states = [], []
    for s in range(2):
        grad_x = mlp_half(s, agg_ref[...], state_ref[...], up_low, wx, wu, wb, acc_in, acc_out)
        aggs.append(grad_x[:, :TILE])
        states.append(grad_x[:, TILE:])
    grad_agg[pl.ds(pl.multiple_of(step * rows, rows), rows), :] = jnp.concatenate(aggs, axis=1).astype(BF16)
    next_ref[...] = up + jnp.concatenate(states, axis=1)


def first_kernel(blocks, agg_hbm, state_hbm, up_hbm, w_in_ref, w_bias_ref, w_out_ref,
                 next_hbm, grad_agg, grad_hbm, sums_hbm, wx, wu, wb, acc_in, acc_out, sums_ref,
                 agg_buf, state_buf, up_buf, next_buf, sems, out_sems, sums_sem):
    rows = agg_hbm.shape[0] // blocks

    def copies(step):
        part = pl.ds(pl.multiple_of(step * rows, rows), rows)
        pairs = ((agg_hbm, agg_buf), (state_hbm, state_buf), (up_hbm, up_buf))
        return [pltpu.make_async_copy(a.at[part], b.at[part], sems.at[step, i]) for i, (a, b) in enumerate(pairs)]

    def results(step):
        part = pl.ds(pl.multiple_of(step * rows, rows), rows)
        pairs = ((next_buf, next_hbm), (grad_agg, grad_hbm))
        return [pltpu.make_async_copy(a.at[part], b.at[part], out_sems.at[step, i]) for i, (a, b) in enumerate(pairs)]

    for step in range(blocks):
        for copy in copies(step):
            copy.start()
    build_weights(1, w_in_ref, w_bias_ref, w_out_ref, wx, wu, wb)
    clear(acc_in, acc_out)

    @pl.loop(0, blocks)
    def _(step):
        for copy in copies(step):
            copy.wait()
        part = pl.ds(pl.multiple_of(step * rows, rows), rows)
        up_low = up_buf[part, :]
        dense_step(step, agg_buf.at[part], state_buf.at[part], up_low.astype(F32), up_low, wx, wu, wb,
                   acc_in, acc_out, grad_agg, next_buf.at[part])
        for copy in results(step):
            copy.start()

    store_sums(acc_in, acc_out, sums_ref)
    last = pltpu.make_async_copy(sums_ref, sums_hbm, sums_sem)
    last.start()
    for step in range(blocks):
        for copy in results(step):
            copy.wait()
    last.wait()


def first_pass(agg, state, up, w_in, w_bias, w_out):
    rows, feat = agg.shape
    blocks = rows // 512
    return pl.pallas_call(
        functools.partial(first_kernel, blocks),
        in_specs=[HBM, HBM, HBM, VMEM, VMEM, VMEM],
        out_specs=[HBM, VMEM, HBM, HBM],
        out_shape=[
            pltpu.HBM((rows, feat), F32),
            jax.ShapeDtypeStruct((rows, feat), BF16),
            pltpu.HBM((rows, feat), BF16),
            pltpu.HBM((SUM_ROWS, WIDE), F32),
        ],
        scratch_shapes=scratch(WEIGHT_SHAPES + SUM_SHAPES)
        + [pltpu.VMEM((SUM_ROWS, WIDE), F32)]
        + [pltpu.VMEM((rows, feat), BF16)] * 3
        + [pltpu.VMEM((rows, feat), F32), pltpu.SemaphoreType.DMA((blocks, 3))]
        + [pltpu.SemaphoreType.DMA((blocks, 2)), pltpu.SemaphoreType.DMA],
        compiler_params=params(),
        cost_estimate=cost(5.4e9, 4 << 20, 2 << 20),
        name="first",
    )(in_hbm(agg), in_hbm(state), in_hbm(up), w_in, w_bias, w_out)


def pick_kernel(capacity, skip, base, asked_ref, grad_agg, picked_ref, two_ref, any_ref):
    two, one = jnp.max(asked_ref[:, 0, 31:32]), jnp.max(asked_ref[:, 0, 95:96])
    two_ref[0] = (two > capacity).astype(jnp.int32)
    any_ref[0] = (jnp.maximum(two, one) > capacity).astype(jnp.int32)
    asked = slot_columns(asked_ref[:, 0, :], capacity, (base,), skip)[0]
    pick_rows(asked, grad_agg, picked_ref)


def pick(capacity, skip, base, asked, grad_agg):
    slots, feat = asked.shape[0] * capacity, grad_agg.shape[1]
    return pl.pallas_call(
        functools.partial(pick_kernel, capacity, skip, base),
        in_specs=[VMEM, VMEM],
        out_specs=[VMEM, SMEM, SMEM],
        out_shape=[
            jax.ShapeDtypeStruct((slots, feat), BF16),
            jax.ShapeDtypeStruct((1,), jnp.int32),
            jax.ShapeDtypeStruct((1,), jnp.int32),
        ],
        compiler_params=params(12 << 20),
        cost_estimate=cost(8e8, 1 << 20),
        name="pick",
    )(asked, grad_agg)


def rest_kernel(capacity, tiles_ref, count_ref, agg_ref, state_ref, up_ref, w_in_ref, w_bias_ref, w_out_ref,
                asked_ref, next_ref, picked_ref, sums_ref, live_ref, grad_agg, wx, wu, wb,
                acc_in, acc_out):
    step = pl.program_id(0)
    rows = agg_ref.shape[0]
    count = count_ref[0, 1]

    @pl.when(step == 0)
    def _():
        build_weights(0, w_in_ref, w_bias_ref, w_out_ref, wx, wu, wb)
        clear(acc_in, acc_out)

    up = up_ref[...]
    tile = lax.shift_right_logical(iota((rows, 1), 0) + step * rows, 7)
    dead = (tile == tiles_ref[1, 0]) | ((tile == tiles_ref[1, 1]) & (count > 1))
    up_low = jnp.where(dead, 0.0, up).astype(BF16)
    dense_step(step, agg_ref, state_ref, up, up_low, wx, wu, wb, acc_in, acc_out, grad_agg, next_ref)

    @pl.when(step == pl.num_programs(0) - 1)
    def _():
        store_sums(acc_in, acc_out, sums_ref)
        asked = slot_columns(asked_ref[:, 0, :], capacity, (64,))[0]
        live_ref[...] = onehot(compact_column(asked, (tiles_ref[1, 0], tiles_ref[1, 1]), count), 2 * TILE)
        pick_rows(asked, grad_agg, picked_ref)


def rest_pass(capacity, tiles, count, agg, state, up, w_in, w_bias, w_out, asked):
    rows, feat = agg.shape
    slots = asked.shape[0] * capacity
    block = 512
    row_spec = pl.BlockSpec((block, feat), lambda i: (i, 0))
    return pl.pallas_call(
        functools.partial(rest_kernel, capacity),
        grid=(rows // block,),
        in_specs=[SMEM, SMEM, row_spec, row_spec, row_spec, whole(w_in.shape), whole(w_bias.shape),
                  whole(w_out.shape), whole(asked.shape)],
        out_specs=[row_spec, whole((slots, feat)), whole((SUM_ROWS, WIDE)), whole((slots, 2 * TILE)),
                   whole((rows, feat))],
        out_shape=[
            pltpu.HBM((rows, feat), F32),
            pltpu.HBM((slots, feat), BF16),
            pltpu.HBM((SUM_ROWS, WIDE), F32),
            pltpu.HBM((slots, 2 * TILE), BF16),
            pltpu.HBM((rows, feat), BF16),
        ],
        scratch_shapes=scratch(WEIGHT_SHAPES + SUM_SHAPES),
        compiler_params=params(),
        cost_estimate=cost(5.4e9, 4 << 20, 2 << 20),
        name="rest",
    )(tiles, count, in_hbm(agg), in_hbm(state), in_hbm(up), w_in, w_bias, w_out, asked)


def as_row(column):
    return column.astype(F32).T[0:8].astype(jnp.int32)


def onehot_rows(row, width):
    return (iota((width, row.shape[1]), 0) == row).astype(F32).astype(BF16)


def relation_rows(relation, table_ref):
    width = -(-table_ref.shape[0] // TILE) * TILE
    pad = width - table_ref.shape[0]
    table = jnp.concatenate([table_ref[...], jnp.zeros((pad, table_ref.shape[1]), BF16)], axis=0)
    return dot_nn(onehot(relation, width), table).astype(BF16)


def tables_two_kernel(capacity, tiles_ref, count_ref, ids_ref, table_ref, t_ref, rows_ref):
    for hop in range(2):
        source, relation = slot_columns(ids_ref[hop], capacity, (0, 64))
        if hop == 1:
            t_ref[...] = relation_rows(relation - 1, table_ref)
        rows_ref[hop] = as_row(relation - 1)
        column = compact_column(source - 1, (tiles_ref[hop, 0], tiles_ref[hop, 1]), count_ref[0, hop])
        rows_ref[2 + hop] = as_row(column)


def tables_two(capacity, tiles, count, ids, table):
    feat = table.shape[1]
    slots = ids.shape[1] * capacity
    return pl.pallas_call(
        functools.partial(tables_two_kernel, capacity),
        in_specs=[SMEM, SMEM, VMEM, VMEM],
        out_specs=[VMEM, VMEM],
        out_shape=[
            jax.ShapeDtypeStruct((slots, feat), BF16),
            jax.ShapeDtypeStruct((4, 8, slots), jnp.int32),
        ],
        compiler_params=params(),
        cost_estimate=cost(1e9, 2 << 20),
        name="tables_two",
    )(tiles, count, ids, table)


def tables_one_kernel(capacity, tiles_ref, count_ref, ids_ref, rows_ref, table_ref, answer_ref,
                      one_a, one_b, zero_a, zero_b, t_ref, h_ref, total_ref):
    states = []
    for hop, a, b in ((0, zero_a, zero_b), (1, one_a, one_b)):
        source, relation = slot_columns(ids_ref[hop], capacity, (0, 64))
        column = compact_column(source - 1, (tiles_ref[hop, 0], tiles_ref[hop, 1]), count_ref[0, hop])
        states.append(dot_nn(onehot(column, 2 * TILE), jnp.concatenate([a[...], b[...]], axis=0)).astype(BF16))
        if hop == 0:
            t_ref[...] = relation_rows(relation - 1, table_ref)
    h_ref[...] = states[0]
    total_ref[...] = dot_nn(onehot_rows(rows_ref[1, 0:1, :], total_ref.shape[0]), answer_ref[...] * states[1])


def tables_one(capacity, tiles, count, ids, rows, table, answer, state_one, state_zero):
    slots, feat = answer.shape
    width = -(-table.shape[0] // TILE) * TILE

    def tile(hop, k):
        return pl.BlockSpec((TILE, feat), lambda i, tiles, count: (tiles[hop, k], 0))

    return pl.pallas_call(
        functools.partial(tables_one_kernel, capacity),
        grid_spec=pltpu.PrefetchScalarGridSpec(
            num_scalar_prefetch=2,
            grid=(1,),
            in_specs=[whole(ids.shape), whole(rows.shape), whole(table.shape), whole(answer.shape), tile(1, 0),
                      tile(1, 1), tile(0, 0), tile(0, 1)],
            out_specs=[whole((slots, feat)), whole((slots, feat)), whole((width, feat))],
        ),
        out_shape=[
            jax.ShapeDtypeStruct((slots, feat), BF16),
            jax.ShapeDtypeStruct((slots, feat), BF16),
            jax.ShapeDtypeStruct((width, feat), F32),
        ],
        compiler_params=params(),
        cost_estimate=cost(2e9, 4 << 20),
        name="tables_one",
    )(tiles, count, ids, rows, table, answer, state_one, state_one, state_zero, state_zero)


def extra_kernel(hop, capacity, skip, tiles_ref, count_ref, ids_ref, table_ref, answer_ref, state_a, state_b,
                 part_ref, out_ref, total_ref):
    source, relation = slot_columns(ids_ref[hop], capacity, (0, 64), skip)
    column = compact_column(source - 1, (tiles_ref[hop, 0], tiles_ref[hop, 1]), count_ref[0, hop])
    select = onehot(column, 2 * TILE)
    answer = answer_ref[...]
    more = dot_nn(onehot_rows(as_row(column)[0:1], 2 * TILE), answer * relation_rows(relation - 1, table_ref))
    out_ref[...] = (part_ref[...].astype(F32) + more).astype(BF16)
    states = dot_nn(select, jnp.concatenate([state_a[...], state_b[...]], axis=0)).astype(BF16)
    total_ref[...] = dot_nn(onehot_rows(as_row(relation - 1)[0:1], total_ref.shape[0]), answer * states)


def extra(hop, capacity, skip, tiles, count, ids, table, answer, state, part):
    feat = answer.shape[1]
    width = -(-table.shape[0] // TILE) * TILE

    def tile(k):
        return pl.BlockSpec((TILE, feat), lambda i, tiles, count: (tiles[hop, k], 0))

    return pl.pallas_call(
        functools.partial(extra_kernel, hop, capacity, skip),
        grid_spec=pltpu.PrefetchScalarGridSpec(
            num_scalar_prefetch=2,
            grid=(1,),
            in_specs=[whole(ids.shape), whole(table.shape), whole(answer.shape), tile(0), tile(1), whole(part.shape)],
            out_specs=[whole(part.shape), whole((width, feat))],
        ),
        out_shape=[jax.ShapeDtypeStruct(part.shape, BF16), jax.ShapeDtypeStruct((width, feat), F32)],
        compiler_params=params(),
        cost_estimate=cost(1e9, 2 << 20),
        name="extra",
    )(tiles, count, ids, table, answer, state, state, part)


def contribution_kernel(answer_ref, t_ref, rows_ref, out_ref):
    select = onehot_rows(rows_ref[3, 0:1, :], 2 * TILE)
    out_ref[...] = dot_nn(select, answer_ref[...] * t_ref[...]).astype(BF16)


def contribution(answer, table, rows):
    return pl.pallas_call(
        contribution_kernel,
        in_specs=[VMEM] * 3,
        out_specs=VMEM,
        out_shape=jax.ShapeDtypeStruct((2 * TILE, answer.shape[1]), BF16),
        compiler_params=params(8 << 20),
        cost_estimate=cost(2e8, 3 << 20),
        name="contribution",
    )(answer, table, rows)


def live_kernel(tiles_ref, count_ref, agg_a, agg_b, state_a, state_b, up_a, up_b, c0, c1, c2, c3,
                w_in_ref, w_bias_ref, w_out_ref, live_ref, rest_ref, picked_ref, next_ref, sums_ref, grad_ref,
                wx, wu, wb, acc_in, acc_out):
    build_weights(0, w_in_ref, w_bias_ref, w_out_ref, wx, wu, wb)
    clear(acc_in, acc_out)
    source = (c0[...].astype(F32) + c1[...].astype(F32)) + (c2[...].astype(F32) + c3[...].astype(F32))
    up = jnp.concatenate([up_a[...], up_b[...]], axis=0) + source
    keep = (iota((2 * TILE, 1), 0) < TILE) | (count_ref[0, 1] > 1)
    up_low = jnp.where(keep, up, 0.0).astype(BF16)
    agg = jnp.concatenate([agg_a[...], agg_b[...]], axis=0)
    state = jnp.concatenate([state_a[...], state_b[...]], axis=0)
    aggs, states = [], []
    for s in range(2):
        grad_x = mlp_half(s, agg, state, up_low, wx, wu, wb, acc_in, acc_out)
        aggs.append(grad_x[:, :TILE])
        states.append(grad_x[:, TILE:])
    grad_agg = jnp.concatenate(aggs, axis=1).astype(BF16)
    next_ref[...] = up + jnp.concatenate(states, axis=1)
    store_sums(acc_in, acc_out, sums_ref)
    grad_ref[...] = grad_agg
    picked_ref[...] = (dot_nn(live_ref[...], grad_agg) + rest_ref[...].astype(F32)).astype(BF16)


def live_pass(tiles, count, agg, state, up, parts, weights, live, rest):
    feat = agg.shape[1]

    def tile(k):
        return pl.BlockSpec((TILE, feat), lambda i, tiles, count: (tiles[1, k], 0))

    return pl.pallas_call(
        live_kernel,
        grid_spec=pltpu.PrefetchScalarGridSpec(
            num_scalar_prefetch=2,
            grid=(1,),
            in_specs=[tile(0), tile(1)] * 3 + [whole(parts[0].shape)] * 4
            + [whole(w.shape) for w in weights] + [whole(live.shape), whole(rest.shape)],
            out_specs=[whole(rest.shape), whole((2 * TILE, feat)), whole((SUM_ROWS, WIDE)), whole((2 * TILE, feat))],
            scratch_shapes=scratch(WEIGHT_SHAPES + SUM_SHAPES),
        ),
        out_shape=[
            jax.ShapeDtypeStruct(rest.shape, BF16),
            jax.ShapeDtypeStruct((2 * TILE, feat), F32),
            jax.ShapeDtypeStruct((SUM_ROWS, WIDE), F32),
            pltpu.HBM((2 * TILE, feat), BF16),
        ],
        compiler_params=params(),
        cost_estimate=cost(1.6e9, 4 << 20, 1 << 19),
        name="live",
    )(tiles, count, agg, agg, state, state, up, up, *parts, *weights, live, rest)


def late_kernel(capacity, skip, tiles_ref, count_ref, asked_ref, rest_ref, live_ref, picked_ref):
    asked = slot_columns(asked_ref[:, 0, :], capacity, (64,), skip)[0]
    column = compact_column(asked, (tiles_ref[1, 0], tiles_ref[1, 1]), count_ref[0, 1])
    rest = dot_nn(onehot(asked, rest_ref.shape[0]), rest_ref[...])
    picked_ref[...] = (dot_nn(onehot(column, 2 * TILE), live_ref[...]) + rest).astype(BF16)


def late_pick(capacity, skip, tiles, count, asked, rest, live):
    slots, feat = asked.shape[0] * capacity, rest.shape[1]
    return pl.pallas_call(
        functools.partial(late_kernel, capacity, skip),
        in_specs=[SMEM, SMEM, VMEM, VMEM, VMEM],
        out_specs=VMEM,
        out_shape=jax.ShapeDtypeStruct((slots, feat), BF16),
        compiler_params=params(),
        cost_estimate=cost(8e8, 1 << 20),
        name="late_pick",
    )(tiles, count, asked, rest, live)


GAP = SUM_ROWS


def pack_kernel(answer_ref, t_ref, h_ref, rows_ref, before_ref, w2_ref, w1a_ref, w1b_ref, part_ref, out_ref):
    answer = answer_ref[...]
    part_ref[...] = dot_nn(onehot_rows(rows_ref[2, 0:1, :], 2 * TILE), answer * t_ref[...]).astype(BF16)
    select = onehot_rows(rows_ref[0, 0:1, :], before_ref.shape[0])
    total = before_ref[...] + dot_nn(select, answer * h_ref[...])
    used, feat = total.shape
    out_ref[used:, 0:feat] = jnp.zeros((out_ref.shape[0] - used, feat), BF16)
    out_ref[4 * GAP:, feat:feat + TILE] = jnp.zeros((out_ref.shape[0] - 4 * GAP, TILE), BF16)
    out_ref[0:used, 0:feat] = total.astype(BF16)
    layers = (w1a_ref[...] + w1b_ref[...], w2_ref[...])
    parts = []
    for layer in layers:
        parts += [layer[:, :TILE], layer[:, TILE:]]
    out_ref[0:4 * GAP, feat:feat + TILE] = jnp.concatenate(parts, axis=0).astype(BF16)


def pack_sums(answer, table, states, ids, before, w2, w1a, w1b, rows):
    feat = answer.shape[1]
    return pl.pallas_call(
        pack_kernel,
        in_specs=[VMEM] * 8,
        out_specs=[VMEM, VMEM],
        out_shape=[
            jax.ShapeDtypeStruct((2 * TILE, feat), BF16),
            jax.ShapeDtypeStruct((rows, feat + TILE), BF16),
        ],
        compiler_params=params(),
        cost_estimate=cost(4e8, 4 << 20),
        name="pack_sums",
    )(answer, table, states, ids, before, w2, w1a, w1b)


def combine_kernel(feat, scale_relations, scale_weights, in_ref, out_ref):
    total = jnp.sum(in_ref[...].astype(F32), axis=0)
    lane = iota(total.shape, 1)
    total = total * jnp.where(lane < feat, scale_relations, scale_weights)
    out_ref[...] = jnp.broadcast_to(total.astype(BF16)[None], out_ref.shape)


def combine(chunks, feat, scale_relations, scale_weights):
    return pl.pallas_call(
        functools.partial(combine_kernel, feat, scale_relations, scale_weights),
        in_specs=[VMEM],
        out_specs=VMEM,
        out_shape=jax.ShapeDtypeStruct(chunks.shape, BF16),
        compiler_params=params(),
        cost_estimate=cost(1e6, 1 << 20),
        name="combine",
    )(chunks)


def unpack_kernel(feat, in_ref, relation_ref, w_in_ref, w_bias_ref, w_out_ref):
    groups = relation_ref.shape[0]
    relation_ref[...] = in_ref[0:groups, 0:feat].astype(F32)
    for layer in range(2):
        at = 2 * layer * GAP
        left = in_ref[at:at + GAP, feat:feat + TILE].astype(F32)
        right = in_ref[at + GAP:at + 2 * GAP, feat:feat + TILE].astype(F32)
        both = jnp.concatenate([left, right], axis=1)
        w_in_ref[layer] = both[0:2 * DIM]
        w_out_ref[layer] = both[2 * DIM:3 * DIM]
        w_bias_ref[layer:layer + 1, :] = both[3 * DIM:3 * DIM + 1]


def unpack(gathered, groups, feat):
    return pl.pallas_call(
        functools.partial(unpack_kernel, feat),
        in_specs=[VMEM],
        out_specs=[VMEM] * 4,
        out_shape=[
            jax.ShapeDtypeStruct((groups, feat), F32),
            jax.ShapeDtypeStruct((2, 2 * DIM, WIDE), F32),
            jax.ShapeDtypeStruct((2, WIDE), F32),
            jax.ShapeDtypeStruct((2, DIM, WIDE), F32),
        ],
        compiler_params=params(),
        cost_estimate=cost(1e6, 2 << 20),
        name="unpack",
    )(gathered)


def final_kernel(tiles_ref, count_ref, quarter_ref, next_ref, live_ref, c0, c1, c2, c3, out_ref):
    tile = 2 * quarter_ref[0] + pl.program_id(0)
    value = next_ref[...]
    for k in range(2):
        rows = slice(k * TILE, (k + 1) * TILE)
        is_live = (tile == tiles_ref[1, k]) & (count_ref[0, 1] > k)
        value = jnp.where(is_live, live_ref[rows, :], value)
    for k in range(2):
        rows = slice(k * TILE, (k + 1) * TILE)
        is_live = (tile == tiles_ref[0, k]) & (count_ref[0, 0] > k)
        source = (c0[rows, :].astype(F32) + c1[rows, :].astype(F32)) + (
            c2[rows, :].astype(F32) + c3[rows, :].astype(F32)
        )
        value = jnp.where(is_live, value + source, value)
    out_ref[...] = value.astype(BF16)


def final_pass(tiles, count, quarter_id, after, live, parts, quarter):
    feat = after.shape[1]
    blocks = quarter // TILE
    return pl.pallas_call(
        final_kernel,
        grid_spec=pltpu.PrefetchScalarGridSpec(
            num_scalar_prefetch=3,
            grid=(blocks,),
            in_specs=[pl.BlockSpec((TILE, feat), lambda i, t, c, q: (q[0] * blocks + i, 0)), whole(live.shape)]
            + [whole(parts[0].shape)] * 4,
            out_specs=pl.BlockSpec((TILE, feat), lambda i, *_: (i, 0)),
        ),
        out_shape=jax.ShapeDtypeStruct((quarter, feat), BF16),
        compiler_params=params(),
        cost_estimate=cost(1e6, 1 << 20),
        name="final",
    )(tiles, count, quarter_id, after, live, *parts)


def shards(state_zero, state_one, aggregate_one, aggregate_two, cotangent, relation_table, update_in, update_bias,
           update_out, frontier_tiles, frontier_count, edge_source, edge_relation, edge_target, edge_owner):
    block_rows, feat = state_zero.shape
    groups = relation_table.shape[0]
    group_size = lax.axis_size("rel")
    peers = lax.axis_size("ent")
    quarter = block_rows // group_size
    edges = edge_source.shape[0]
    capacity = 3 * edges // (2 * peers)
    regular = 2 * capacity // 3
    over = capacity - regular
    slots = peers * regular
    sum_rows = 8 * peers

    def exchange(chunks):
        return lax.all_to_all(chunks, "ent", split_axis=0, concat_axis=0, tiled=True)

    def over_rel(part):
        turned = [
            lax.ppermute(part, "rel", [(i, (i + k) % group_size) for i in range(group_size)])
            for k in range(1, group_size)
        ]
        return [part] + turned

    row = lambda values: values.reshape(1, edges)
    count = jnp.swapaxes(frontier_count, 0, 1)
    weights = (update_in, update_bias, jnp.swapaxes(update_out, 1, 2))
    request, ids = pl.pallas_call(
        functools.partial(slots_kernel, peers),
        in_specs=[HBM] * 6,
        out_specs=[VMEM] * 2,
        out_shape=[
            jax.ShapeDtypeStruct((peers, 1, 128), F32),
            jax.ShapeDtypeStruct((2, peers, 128), F32),
        ],
        scratch_shapes=[pltpu.VMEM(frontier_tiles.shape, jnp.int32), pltpu.VMEM(count.shape, jnp.int32)]
        + [pltpu.VMEM((1, edges), jnp.int32)] * 4
        + [pltpu.SemaphoreType.DMA((6,))],
        compiler_params=params(8 << 20),
        cost_estimate=cost(1e8, 1 << 20),
        name="slots",
    )(in_hbm(frontier_tiles), in_hbm(count), *(in_hbm(row(values)) for values in (edge_owner, edge_target, edge_source, edge_relation)))
    asked = exchange(request)

    upstream_one, grad_agg, grad_kept, sums_two = first_pass(aggregate_two, state_one, cotangent, *weights)
    picked_two, more_two, more_any = pick(regular, 0, 0, asked, grad_agg)
    more_two, more_any = more_two[0], more_any[0]
    answered_two = exchange(picked_two.reshape(peers, regular, feat)).reshape(slots, feat)
    after, rest, sums_rest, live, grad_rest = rest_pass(
        regular, frontier_tiles, count, aggregate_one, state_zero, upstream_one, *weights, asked
    )
    edge_table, rows = tables_two(regular, frontier_tiles, count, ids, relation_table)
    answered_two, rest, edge_table, rows, more_two, more_any = lax.optimization_barrier(
        (answered_two, rest, edge_table, rows, more_two, more_any)
    )

    def over_two(part):
        picked = pick(over, regular, 0, asked, in_hbm(grad_kept))[0]
        answer = exchange(picked.reshape(peers, over, feat)).reshape(peers * over, feat)
        return extra(
            1, over, regular, frontier_tiles, count, in_hbm(ids), in_hbm(relation_table), answer, in_hbm(state_one), part
        )

    part = contribution(answered_two, edge_table, rows)
    part = lax.switch(more_two, (lambda part: part, lambda part: over_two(part)[0]), part)
    parts = over_rel(part)
    table_one, states_one, relation_two = tables_one(
        regular, frontier_tiles, count, ids, rows, relation_table, answered_two, state_one, state_zero
    )
    parts[0], rest, table_one, states_one, relation_two = lax.optimization_barrier(
        (parts[0], rest, table_one, states_one, relation_two)
    )
    picked_one, after_live, sums_live, grad_live = live_pass(
        frontier_tiles, count, aggregate_one, state_zero, upstream_one, parts, weights, live, rest
    )
    answered_one = exchange(picked_one.reshape(peers, regular, feat)).reshape(slots, feat)
    answered_one, more_any = lax.optimization_barrier((answered_one, more_any))
    part, packed = pack_sums(
        answered_one, table_one, states_one, rows, relation_two, sums_two, sums_rest, sums_live, sum_rows
    )

    def over_any(part, packed):
        first = over_two(part)[1]
        picked = late_pick(over, regular, frontier_tiles, count, asked, in_hbm(grad_rest), in_hbm(grad_live))
        answer = exchange(picked.reshape(peers, over, feat)).reshape(peers * over, feat)
        part, second = extra(
            0, over, regular, frontier_tiles, count, in_hbm(ids), in_hbm(relation_table), answer, in_hbm(state_zero), part
        )
        used = first.shape[0]
        total = packed[:used, :feat].astype(F32) + (first + second)
        return part, packed.at[:used, :feat].set(total.astype(BF16))

    part, packed = lax.switch(more_any, (lambda part, packed: (part, packed), over_any), part, packed)
    parts = over_rel(part)
    scale_weights = 1.0 / math.sqrt(block_rows * peers * QUERIES)
    scale_relations = math.sqrt(groups * group_size / (edges * peers * group_size))
    chunks = exchange(packed.reshape(peers, 8, feat + TILE))
    gathered = exchange(combine(chunks, feat, scale_relations, scale_weights)).reshape(sum_rows, feat + TILE)
    quarter_id = lax.axis_index("rel").astype(jnp.int32).reshape(1)
    grad_zero = final_pass(frontier_tiles, count, quarter_id, after, after_live, parts, quarter)
    relation, grad_in, grad_bias, grad_out = unpack(gathered, groups, feat)
    return grad_zero, relation, grad_in, grad_bias, jnp.swapaxes(grad_out, 1, 2)


def solution(mesh):
    in_specs = (
        P("ent", None),
        P("ent", None),
        P("ent", None),
        P("ent", None),
        P("ent", None),
        P("rel", None),
        P(),
        P(),
        P(),
        P(None, "ent"),
        P(None, "ent"),
        P(("ent", "rel")),
        P(("ent", "rel")),
        P(("ent", "rel")),
        P(("ent", "rel"), None),
    )
    out_specs = (P(("ent", "rel"), None), P("rel", None), P(), P(), P())
    return jax.shard_map(shards, mesh=mesh, in_specs=in_specs, out_specs=out_specs, check_vma=False)
```

```python
import functools
import math

import jax
import jax.numpy as jnp
from jax import lax
from jax.experimental import pallas as pl
from jax.experimental.pallas import tpu as pltpu
from jax.sharding import PartitionSpec as P

QUERIES = 8
DIM = 32
TILE = 128
WIDE = 256
HALF_Q = 4
F32 = jnp.float32
BF16 = jnp.bfloat16
VMEM = pl.BlockSpec(memory_space=pltpu.VMEM)
SMEM = pl.BlockSpec(memory_space=pltpu.SMEM)
HBM = pl.BlockSpec(memory_space=pltpu.HBM)


def in_hbm(array):
    return pltpu.with_memory_space_constraint(array, pltpu.HBM)


def iota(shape, dim):
    return lax.broadcasted_iota(jnp.int32, shape, dim)


def dot_nn(a, b):
    return lax.dot_general(a, b, (((1,), (0,)), ((), ())), preferred_element_type=F32)


def dot_nt(a, b):
    return lax.dot_general(a, b, (((1,), (1,)), ((), ())), preferred_element_type=F32)


def dot_tn(a, b):
    return lax.dot_general(a, b, (((0,), (0,)), ((), ())), preferred_element_type=F32)


def params(vmem=20 << 20):
    return pltpu.CompilerParams(vmem_limit_bytes=vmem)


def cost(flops, nbytes, trans=0):
    return pl.CostEstimate(flops=int(flops), bytes_accessed=int(nbytes), transcendentals=int(trans))


def slots_kernel(peers, tiles_hbm, count_hbm, owner_hbm, target_hbm, source_hbm, relation_hbm, request_ref, ids_ref,
                 tiles_ref, count_ref, owner_ref, target_ref, source_ref, relation_ref, sems):
    pairs = (
        (owner_hbm, owner_ref), (source_hbm, source_ref), (tiles_hbm, tiles_ref), (count_hbm, count_ref),
        (target_hbm, target_ref), (relation_hbm, relation_ref),
    )
    copies = [pltpu.make_async_copy(a, b, sems.at[i]) for i, (a, b) in enumerate(pairs)]
    for copy in copies:
        copy.start()
    for copy in copies:
        copy.wait()
    edges = owner_ref.shape[1]
    hit = (iota((peers, edges), 0) == owner_ref[...]).astype(F32)
    below = (iota((TILE, TILE), 0) < iota((TILE, TILE), 1)).astype(BF16)
    tile = lax.shift_right_logical(source_ref[...], 7)
    request, tops = [], []
    for hop in (1, 0):
        first, second = tiles_ref[hop:hop + 1, 0:1], tiles_ref[hop:hop + 1, 1:2]
        live = (tile == first) | ((tile == second) & (count_ref[0:1, hop:hop + 1] > 1))
        own = jnp.where(live, hit, 0.0)
        own_low = own.astype(BF16)
        offset = jnp.zeros((peers, 1), F32)
        pieces = []
        for b in range(edges // TILE):
            block = slice(b * TILE, (b + 1) * TILE)
            pieces.append(dot_nn(own_low[:, block], below) + offset)
            offset = offset + jnp.sum(own[:, block], axis=1, keepdims=True)
        earlier = jnp.sum(jnp.concatenate(pieces, axis=1) * own, axis=0, keepdims=True).astype(jnp.int32)
        place = jnp.where((iota((32, edges), 0) == earlier) & live, 1.0, 0.0)

        def spread(values):
            high = lax.shift_right_logical(values, 5)
            low = values & 31
            return [place * high.astype(F32), place * low.astype(F32)]

        request += spread(target_ref[...])
        tops.append(jnp.max(offset, axis=0, keepdims=True))
        second = jnp.concatenate(
            spread(source_ref[...] + 1) + spread(relation_ref[...] + 1), axis=0
        ).astype(BF16)
        ids_ref[hop] = dot_nt(own_low, second)
    lane = iota((peers, 128), 1)
    sent = dot_nt(hit.astype(BF16), jnp.concatenate(request, axis=0).astype(BF16))
    sent = jnp.where(lane == 31, tops[0], sent)
    request_ref[:, 0, :] = jnp.where(lane == 95, tops[1], sent)


def slot_columns(table, capacity, bases, skip=0):
    peers = table.shape[0]
    slots = peers * capacity
    row = iota((slots, peers), 0)
    start = iota((slots, peers), 1) * capacity
    expand = ((row >= start) & (row < start + capacity)).astype(BF16)
    spread = dot_nn(expand, table.astype(BF16))
    row = iota((slots, 128), 0)
    group = ((row.astype(F32) + 0.5) * (1.0 / capacity)).astype(jnp.int32)
    place = row - group * capacity + skip
    lane = iota((slots, 128), 1)
    columns = []
    for base in bases:
        weight = jnp.where(lane == place + base, 32.0, 0.0) + jnp.where(
            lane == place + (base + 32), 1.0, 0.0
        )
        columns.append(dot_nn((spread * weight).astype(BF16), jnp.ones((128, 128), BF16)).astype(jnp.int32))
    return columns


def compact_column(column, tiles, count):
    tile = lax.shift_right_arithmetic(column, 7)
    inner = column & 127
    result = jnp.full(column.shape, -1, jnp.int32)
    for k in range(len(tiles)):
        live = (tile == tiles[k]) & (count > k)
        result = jnp.where(live, inner + k * TILE, result)
    return result


def onehot(column, width):
    column = column.astype(jnp.int16)
    lane = lax.broadcasted_iota(jnp.int16, column.shape, 1)
    one, zero = jnp.ones((), BF16), jnp.zeros((), BF16)
    parts = [jnp.where(lane == column - t, one, zero) for t in range(0, width, TILE)]
    return jnp.concatenate(parts, axis=1)


def build_weights(layer, w_in_ref, w_bias_ref, w_out_ref, wx_ref, wu_ref, wb_ref):
    wx_ref[...] = jnp.zeros_like(wx_ref)
    wu_ref[...] = jnp.zeros_like(wu_ref)
    for q in range(HALF_Q):
        rows, cols = slice(q * DIM, (q + 1) * DIM), slice(q * WIDE, (q + 1) * WIDE)
        low = slice(TILE + q * DIM, TILE + (q + 1) * DIM)
        wx_ref[rows, cols] = 0.5 * w_in_ref[layer, 0:DIM, :]
        wx_ref[low, cols] = 0.5 * w_in_ref[layer, DIM:2 * DIM, :]
        wu_ref[rows, cols] = w_out_ref[layer]
        wb_ref[:, cols] = 0.5 * w_bias_ref[layer:layer + 1, :]


def mlp_half(s, agg, state, up_low, wx, wu, bias, acc_in, acc_out):
    lanes = slice(s * TILE, (s + 1) * TILE)
    x = jnp.concatenate([agg[:, lanes], state[:, lanes]], axis=1)
    up = up_low[:, lanes]
    x_turned, up_turned = x.T, up.T
    half = dot_nn(x, wx[...]) + bias[...]
    bend = jnp.tanh(half)
    above = 1.0 + bend
    act_low = (half * above).astype(BF16)
    slope = above * (1.0 + half * (1.0 - bend))
    low = (dot_nn(up, wu[...]) * slope).astype(BF16)
    ones = jnp.ones((16, x.shape[0]), BF16)
    for q in range(HALF_Q):
        cols = slice(q * WIDE, (q + 1) * WIDE)
        rows = slice(q * DIM, (q + 1) * DIM)
        low_rows = slice(TILE + q * DIM, TILE + (q + 1) * DIM)
        own = jnp.concatenate([x_turned[rows], x_turned[low_rows], ones], axis=0)
        acc_in[...] += dot_nn(own, low[:, cols])
        acc_out[...] += dot_nn(up_turned[rows], act_low[:, cols])
    return dot_nt(low, wx[...])


def store_sums(acc_in, acc_out, sums_ref):
    sums_ref[0:2 * DIM, :] = 0.5 * acc_in[0:2 * DIM, :]
    sums_ref[2 * DIM:3 * DIM, :] = acc_out[...]
    sums_ref[3 * DIM:3 * DIM + 8, :] = 0.5 * acc_in[2 * DIM:2 * DIM + 8, :]


def clear(acc_in, acc_out):
    acc_in[...] = jnp.zeros_like(acc_in)
    acc_out[...] = jnp.zeros_like(acc_out)


WEIGHT_SHAPES = [
    ((2 * TILE, HALF_Q * WIDE), BF16),
    ((TILE, HALF_Q * WIDE), BF16),
    ((1, HALF_Q * WIDE), F32),
]
SUM_SHAPES = [((2 * DIM + 16, WIDE), F32), ((DIM, WIDE), F32)]
SUM_ROWS = 3 * DIM + 8


def scratch(shapes):
    return [pltpu.VMEM(shape, dtype) for shape, dtype in shapes]


def whole(shape):
    return pl.BlockSpec(shape, lambda i, *_: (0,) * len(shape))


def pick_rows(asked, grad_agg, picked_ref, chunks=4):
    rows, slots = grad_agg.shape[0], asked.shape[0]
    step = slots // chunks
    for c in range(chunks):
        part = slice(c * step, (c + 1) * step)
        picked_ref[part, :] = dot_nn(onehot(asked[part], rows), grad_agg[...]).astype(BF16)


def dense_step(step, agg_ref, state_ref, up, up_low, wx, wu, wb, acc_in, acc_out, grad_agg, next_ref):
    rows = agg_ref.shape[0]
    aggs, states = [], []
    for s in range(2):
        grad_x = mlp_half(s, agg_ref[...], state_ref[...], up_low, wx, wu, wb, acc_in, acc_out)
        aggs.append(grad_x[:, :TILE])
        states.append(grad_x[:, TILE:])
    grad_agg[pl.ds(pl.multiple_of(step * rows, rows), rows), :] = jnp.concatenate(aggs, axis=1).astype(BF16)
    next_ref[...] = up + jnp.concatenate(states, axis=1)


def first_kernel(blocks, agg_hbm, state_hbm, up_hbm, w_in_ref, w_bias_ref, w_out_ref,
                 next_hbm, grad_agg, grad_hbm, sums_hbm, wx, wu, wb, acc_in, acc_out, sums_ref,
                 agg_buf, state_buf, up_buf, next_buf, sems, out_sems, sums_sem):
    rows = agg_hbm.shape[0] // blocks

    def copies(step):
        part = pl.ds(pl.multiple_of(step * rows, rows), rows)
        pairs = ((agg_hbm, agg_buf), (state_hbm, state_buf), (up_hbm, up_buf))
        return [pltpu.make_async_copy(a.at[part], b.at[part], sems.at[step, i]) for i, (a, b) in enumerate(pairs)]

    def results(step):
        part = pl.ds(pl.multiple_of(step * rows, rows), rows)
        pairs = ((next_buf, next_hbm), (grad_agg, grad_hbm))
        return [pltpu.make_async_copy(a.at[part], b.at[part], out_sems.at[step, i]) for i, (a, b) in enumerate(pairs)]

    for step in range(blocks):
        for copy in copies(step):
            copy.start()
    build_weights(1, w_in_ref, w_bias_ref, w_out_ref, wx, wu, wb)
    clear(acc_in, acc_out)

    @pl.loop(0, blocks)
    def _(step):
        for copy in copies(step):
            copy.wait()
        part = pl.ds(pl.multiple_of(step * rows, rows), rows)
        up_low = up_buf[part, :]
        dense_step(step, agg_buf.at[part], state_buf.at[part], up_low.astype(F32), up_low, wx, wu, wb,
                   acc_in, acc_out, grad_agg, next_buf.at[part])
        for copy in results(step):
            copy.start()

    store_sums(acc_in, acc_out, sums_ref)
    last = pltpu.make_async_copy(sums_ref, sums_hbm, sums_sem)
    last.start()
    for step in range(blocks):
        for copy in results(step):
            copy.wait()
    last.wait()


def first_pass(agg, state, up, w_in, w_bias, w_out):
    rows, feat = agg.shape
    blocks = rows // 512
    return pl.pallas_call(
        functools.partial(first_kernel, blocks),
        in_specs=[HBM, HBM, HBM, VMEM, VMEM, VMEM],
        out_specs=[HBM, VMEM, HBM, HBM],
        out_shape=[
            pltpu.HBM((rows, feat), F32),
            jax.ShapeDtypeStruct((rows, feat), BF16),
            pltpu.HBM((rows, feat), BF16),
            pltpu.HBM((SUM_ROWS, WIDE), F32),
        ],
        scratch_shapes=scratch(WEIGHT_SHAPES + SUM_SHAPES)
        + [pltpu.VMEM((SUM_ROWS, WIDE), F32)]
        + [pltpu.VMEM((rows, feat), BF16)] * 3
        + [pltpu.VMEM((rows, feat), F32), pltpu.SemaphoreType.DMA((blocks, 3))]
        + [pltpu.SemaphoreType.DMA((blocks, 2)), pltpu.SemaphoreType.DMA],
        compiler_params=params(),
        cost_estimate=cost(5.4e9, 4 << 20, 2 << 20),
        name="first",
    )(in_hbm(agg), in_hbm(state), in_hbm(up), w_in, w_bias, w_out)


def pick_kernel(capacity, skip, base, asked_ref, grad_agg, picked_hbm, two_ref, any_ref, picked_ref, sems):
    two, one = jnp.max(asked_ref[:, 0, 31:32]), jnp.max(asked_ref[:, 0, 95:96])
    two_ref[0] = (two > capacity).astype(jnp.int32)
    any_ref[0] = (jnp.maximum(two, one) > capacity).astype(jnp.int32)
    asked = slot_columns(asked_ref[:, 0, :], capacity, (base,), skip)[0]
    chunks = sems.shape[0]
    step = picked_ref.shape[0] // chunks
    copies = []
    for c in range(chunks):
        part = pl.ds(c * step, step)
        select = onehot(asked[c * step:(c + 1) * step], grad_agg.shape[0])
        picked_ref[part, :] = dot_nn(select, grad_agg[...]).astype(BF16)
        copies.append(pltpu.make_async_copy(picked_ref.at[part], picked_hbm.at[part], sems.at[c]))
        copies[-1].start()
    for copy in copies:
        copy.wait()


def pick(capacity, skip, base, asked, grad_agg):
    slots, feat = asked.shape[0] * capacity, grad_agg.shape[1]
    return pl.pallas_call(
        functools.partial(pick_kernel, capacity, skip, base),
        in_specs=[VMEM, VMEM],
        out_specs=[HBM, SMEM, SMEM],
        out_shape=[
            pltpu.HBM((slots, feat), BF16),
            jax.ShapeDtypeStruct((1,), jnp.int32),
            jax.ShapeDtypeStruct((1,), jnp.int32),
        ],
        scratch_shapes=[pltpu.VMEM((slots, feat), BF16), pltpu.SemaphoreType.DMA((4,))],
        compiler_params=params(12 << 20),
        cost_estimate=cost(8e8, 1 << 20),
        name="pick",
    )(asked, grad_agg)


def rest_kernel(capacity, tiles_ref, count_ref, agg_ref, state_ref, up_ref, w_in_ref, w_bias_ref, w_out_ref,
                asked_ref, next_ref, picked_ref, sums_ref, live_ref, grad_agg, wx, wu, wb,
                acc_in, acc_out):
    step = pl.program_id(0)
    rows = agg_ref.shape[0]
    count = count_ref[0, 1]

    @pl.when(step == 0)
    def _():
        build_weights(0, w_in_ref, w_bias_ref, w_out_ref, wx, wu, wb)
        clear(acc_in, acc_out)

    up = up_ref[...]
    tile = lax.shift_right_logical(iota((rows, 1), 0) + step * rows, 7)
    dead = (tile == tiles_ref[1, 0]) | ((tile == tiles_ref[1, 1]) & (count > 1))
    up_low = jnp.where(dead, 0.0, up).astype(BF16)
    dense_step(step, agg_ref, state_ref, up, up_low, wx, wu, wb, acc_in, acc_out, grad_agg, next_ref)

    @pl.when(step == pl.num_programs(0) - 1)
    def _():
        store_sums(acc_in, acc_out, sums_ref)
        asked = slot_columns(asked_ref[:, 0, :], capacity, (64,))[0]
        live_ref[...] = onehot(compact_column(asked, (tiles_ref[1, 0], tiles_ref[1, 1]), count), 2 * TILE)
        pick_rows(asked, grad_agg, picked_ref)


def rest_pass(capacity, tiles, count, agg, state, up, w_in, w_bias, w_out, asked):
    rows, feat = agg.shape
    slots = asked.shape[0] * capacity
    block = 512
    row_spec = pl.BlockSpec((block, feat), lambda i: (i, 0))
    return pl.pallas_call(
        functools.partial(rest_kernel, capacity),
        grid=(rows // block,),
        in_specs=[SMEM, SMEM, row_spec, row_spec, row_spec, whole(w_in.shape), whole(w_bias.shape),
                  whole(w_out.shape), whole(asked.shape)],
        out_specs=[row_spec, whole((slots, feat)), whole((SUM_ROWS, WIDE)), whole((slots, 2 * TILE)),
                   whole((rows, feat))],
        out_shape=[
            pltpu.HBM((rows, feat), F32),
            pltpu.HBM((slots, feat), BF16),
            pltpu.HBM((SUM_ROWS, WIDE), F32),
            pltpu.HBM((slots, 2 * TILE), BF16),
            pltpu.HBM((rows, feat), BF16),
        ],
        scratch_shapes=scratch(WEIGHT_SHAPES + SUM_SHAPES),
        compiler_params=params(),
        cost_estimate=cost(5.4e9, 4 << 20, 2 << 20),
        name="rest",
    )(in_hbm(tiles), in_hbm(count), in_hbm(agg), in_hbm(state), in_hbm(up), w_in, w_bias, w_out, asked)


def as_row(column):
    return column.astype(F32).T[0:8].astype(jnp.int32)


def onehot_rows(row, width):
    return (iota((width, row.shape[1]), 0) == row).astype(F32).astype(BF16)


def relation_rows(relation, table_ref):
    width = -(-table_ref.shape[0] // TILE) * TILE
    pad = width - table_ref.shape[0]
    table = jnp.concatenate([table_ref[...], jnp.zeros((pad, table_ref.shape[1]), BF16)], axis=0)
    return dot_nn(onehot(relation, width), table).astype(BF16)


def tables_two_kernel(capacity, tiles_ref, count_ref, ids_ref, table_ref, t_ref, rows_ref):
    for hop in range(2):
        source, relation = slot_columns(ids_ref[hop], capacity, (0, 64))
        if hop == 1:
            t_ref[...] = relation_rows(relation - 1, table_ref)
        rows_ref[hop] = as_row(relation - 1)
        column = compact_column(source - 1, (tiles_ref[hop, 0], tiles_ref[hop, 1]), count_ref[0, hop])
        rows_ref[2 + hop] = as_row(column)


def tables_two(capacity, tiles, count, ids, table):
    feat = table.shape[1]
    slots = ids.shape[1] * capacity
    return pl.pallas_call(
        functools.partial(tables_two_kernel, capacity),
        in_specs=[SMEM, SMEM, VMEM, VMEM],
        out_specs=[VMEM, VMEM],
        out_shape=[
            jax.ShapeDtypeStruct((slots, feat), BF16),
            jax.ShapeDtypeStruct((4, 8, slots), jnp.int32),
        ],
        compiler_params=params(),
        cost_estimate=cost(1e9, 2 << 20),
        name="tables_two",
    )(in_hbm(tiles), in_hbm(count), ids, table)


def tables_one_kernel(capacity, tiles_ref, count_ref, ids_ref, rows_ref, table_ref, answer_ref,
                      one_a, one_b, zero_a, zero_b, t_ref, h_ref, total_ref):
    states = []
    for hop, a, b in ((0, zero_a, zero_b), (1, one_a, one_b)):
        source, relation = slot_columns(ids_ref[hop], capacity, (0, 64))
        column = compact_column(source - 1, (tiles_ref[hop, 0], tiles_ref[hop, 1]), count_ref[0, hop])
        states.append(dot_nn(onehot(column, 2 * TILE), jnp.concatenate([a[...], b[...]], axis=0)).astype(BF16))
        if hop == 0:
            t_ref[...] = relation_rows(relation - 1, table_ref)
    h_ref[...] = states[0]
    total_ref[...] = dot_nn(onehot_rows(rows_ref[1, 0:1, :], total_ref.shape[0]), answer_ref[...] * states[1])


def tables_one(capacity, tiles, count, ids, rows, table, answer, state_one, state_zero):
    slots, feat = answer.shape
    width = -(-table.shape[0] // TILE) * TILE

    def tile(hop, k):
        return pl.BlockSpec((TILE, feat), lambda i, tiles, count: (tiles[hop, k], 0))

    return pl.pallas_call(
        functools.partial(tables_one_kernel, capacity),
        grid_spec=pltpu.PrefetchScalarGridSpec(
            num_scalar_prefetch=2,
            grid=(1,),
            in_specs=[whole(ids.shape), whole(rows.shape), whole(table.shape), whole(answer.shape), tile(1, 0),
                      tile(1, 1), tile(0, 0), tile(0, 1)],
            out_specs=[whole((slots, feat)), whole((slots, feat)), whole((width, feat))],
        ),
        out_shape=[
            jax.ShapeDtypeStruct((slots, feat), BF16),
            jax.ShapeDtypeStruct((slots, feat), BF16),
            jax.ShapeDtypeStruct((width, feat), F32),
        ],
        compiler_params=params(),
        cost_estimate=cost(2e9, 4 << 20),
        name="tables_one",
    )(in_hbm(tiles), in_hbm(count), ids, rows, table, answer, state_one, state_one, state_zero, state_zero)


def extra_kernel(hop, capacity, skip, tiles_ref, count_ref, ids_ref, table_ref, answer_ref, state_a, state_b,
                 part_ref, out_ref, total_ref):
    source, relation = slot_columns(ids_ref[hop], capacity, (0, 64), skip)
    column = compact_column(source - 1, (tiles_ref[hop, 0], tiles_ref[hop, 1]), count_ref[0, hop])
    select = onehot(column, 2 * TILE)
    answer = answer_ref[...]
    more = dot_nn(onehot_rows(as_row(column)[0:1], 2 * TILE), answer * relation_rows(relation - 1, table_ref))
    out_ref[...] = (part_ref[...].astype(F32) + more).astype(BF16)
    states = dot_nn(select, jnp.concatenate([state_a[...], state_b[...]], axis=0)).astype(BF16)
    total_ref[...] = dot_nn(onehot_rows(as_row(relation - 1)[0:1], total_ref.shape[0]), answer * states)


def extra(hop, capacity, skip, tiles, count, ids, table, answer, state, part):
    feat = answer.shape[1]
    width = -(-table.shape[0] // TILE) * TILE

    def tile(k):
        return pl.BlockSpec((TILE, feat), lambda i, tiles, count: (tiles[hop, k], 0))

    return pl.pallas_call(
        functools.partial(extra_kernel, hop, capacity, skip),
        grid_spec=pltpu.PrefetchScalarGridSpec(
            num_scalar_prefetch=2,
            grid=(1,),
            in_specs=[whole(ids.shape), whole(table.shape), whole(answer.shape), tile(0), tile(1), whole(part.shape)],
            out_specs=[whole(part.shape), whole((width, feat))],
        ),
        out_shape=[jax.ShapeDtypeStruct(part.shape, BF16), jax.ShapeDtypeStruct((width, feat), F32)],
        compiler_params=params(),
        cost_estimate=cost(1e9, 2 << 20),
        name="extra",
    )(in_hbm(tiles), in_hbm(count), ids, table, answer, state, state, part)


def contribution_kernel(answer_ref, t_ref, rows_ref, out_ref):
    select = onehot_rows(rows_ref[3, 0:1, :], 2 * TILE)
    out_ref[...] = dot_nn(select, answer_ref[...] * t_ref[...]).astype(BF16)


def contribution(answer, table, rows):
    return pl.pallas_call(
        contribution_kernel,
        in_specs=[VMEM] * 3,
        out_specs=VMEM,
        out_shape=jax.ShapeDtypeStruct((2 * TILE, answer.shape[1]), BF16),
        compiler_params=params(8 << 20),
        cost_estimate=cost(2e8, 3 << 20),
        name="contribution",
    )(answer, table, rows)


def live_kernel(tiles_ref, count_ref, agg_a, agg_b, state_a, state_b, up_a, up_b, c0, c1, c2, c3,
                w_in_ref, w_bias_ref, w_out_ref, live_ref, rest_ref, picked_ref, next_ref, sums_ref, grad_ref,
                wx, wu, wb, acc_in, acc_out):
    build_weights(0, w_in_ref, w_bias_ref, w_out_ref, wx, wu, wb)
    clear(acc_in, acc_out)
    source = (c0[...].astype(F32) + c1[...].astype(F32)) + (c2[...].astype(F32) + c3[...].astype(F32))
    up = jnp.concatenate([up_a[...], up_b[...]], axis=0) + source
    keep = (iota((2 * TILE, 1), 0) < TILE) | (count_ref[0, 1] > 1)
    up_low = jnp.where(keep, up, 0.0).astype(BF16)
    agg = jnp.concatenate([agg_a[...], agg_b[...]], axis=0)
    state = jnp.concatenate([state_a[...], state_b[...]], axis=0)
    aggs, states = [], []
    for s in range(2):
        grad_x = mlp_half(s, agg, state, up_low, wx, wu, wb, acc_in, acc_out)
        aggs.append(grad_x[:, :TILE])
        states.append(grad_x[:, TILE:])
    grad_agg = jnp.concatenate(aggs, axis=1).astype(BF16)
    next_ref[...] = up + jnp.concatenate(states, axis=1)
    store_sums(acc_in, acc_out, sums_ref)
    grad_ref[...] = grad_agg
    picked_ref[...] = (dot_nn(live_ref[...], grad_agg) + rest_ref[...].astype(F32)).astype(BF16)


def live_pass(tiles, count, agg, state, up, parts, weights, live, rest):
    feat = agg.shape[1]

    def tile(k):
        return pl.BlockSpec((TILE, feat), lambda i, tiles, count: (tiles[1, k], 0))

    return pl.pallas_call(
        live_kernel,
        grid_spec=pltpu.PrefetchScalarGridSpec(
            num_scalar_prefetch=2,
            grid=(1,),
            in_specs=[tile(0), tile(1)] * 3 + [whole(parts[0].shape)] * 4
            + [whole(w.shape) for w in weights] + [whole(live.shape), whole(rest.shape)],
            out_specs=[whole(rest.shape), whole((2 * TILE, feat)), whole((SUM_ROWS, WIDE)), whole((2 * TILE, feat))],
            scratch_shapes=scratch(WEIGHT_SHAPES + SUM_SHAPES),
        ),
        out_shape=[
            jax.ShapeDtypeStruct(rest.shape, BF16),
            jax.ShapeDtypeStruct((2 * TILE, feat), F32),
            jax.ShapeDtypeStruct((SUM_ROWS, WIDE), F32),
            pltpu.HBM((2 * TILE, feat), BF16),
        ],
        compiler_params=params(),
        cost_estimate=cost(1.6e9, 4 << 20, 1 << 19),
        name="live",
    )(in_hbm(tiles), in_hbm(count), agg, agg, state, state, up, up, *parts, *weights, live, rest)


def late_kernel(capacity, skip, tiles_ref, count_ref, asked_ref, rest_ref, live_ref, picked_ref):
    asked = slot_columns(asked_ref[:, 0, :], capacity, (64,), skip)[0]
    column = compact_column(asked, (tiles_ref[1, 0], tiles_ref[1, 1]), count_ref[0, 1])
    rest = dot_nn(onehot(asked, rest_ref.shape[0]), rest_ref[...])
    picked_ref[...] = (dot_nn(onehot(column, 2 * TILE), live_ref[...]) + rest).astype(BF16)


def late_pick(capacity, skip, tiles, count, asked, rest, live):
    slots, feat = asked.shape[0] * capacity, rest.shape[1]
    return pl.pallas_call(
        functools.partial(late_kernel, capacity, skip),
        in_specs=[SMEM, SMEM, VMEM, VMEM, VMEM],
        out_specs=VMEM,
        out_shape=jax.ShapeDtypeStruct((slots, feat), BF16),
        compiler_params=params(),
        cost_estimate=cost(8e8, 1 << 20),
        name="late_pick",
    )(in_hbm(tiles), in_hbm(count), asked, rest, live)


GAP = SUM_ROWS


def pack_kernel(answer_ref, t_ref, h_ref, rows_ref, before_ref, w2_ref, w1a_ref, w1b_ref, part_ref, out_ref):
    answer = answer_ref[...]
    part_ref[...] = dot_nn(onehot_rows(rows_ref[2, 0:1, :], 2 * TILE), answer * t_ref[...]).astype(BF16)
    select = onehot_rows(rows_ref[0, 0:1, :], before_ref.shape[0])
    total = before_ref[...] + dot_nn(select, answer * h_ref[...])
    used, feat = total.shape
    out_ref[used:, 0:feat] = jnp.zeros((out_ref.shape[0] - used, feat), BF16)
    out_ref[4 * GAP:, feat:feat + TILE] = jnp.zeros((out_ref.shape[0] - 4 * GAP, TILE), BF16)
    out_ref[0:used, 0:feat] = total.astype(BF16)
    layers = (w1a_ref[...] + w1b_ref[...], w2_ref[...])
    parts = []
    for layer in layers:
        parts += [layer[:, :TILE], layer[:, TILE:]]
    out_ref[0:4 * GAP, feat:feat + TILE] = jnp.concatenate(parts, axis=0).astype(BF16)


def pack_sums(answer, table, states, ids, before, w2, w1a, w1b, rows):
    feat = answer.shape[1]
    return pl.pallas_call(
        pack_kernel,
        in_specs=[VMEM] * 8,
        out_specs=[VMEM, VMEM],
        out_shape=[
            jax.ShapeDtypeStruct((2 * TILE, feat), BF16),
            jax.ShapeDtypeStruct((rows, feat + TILE), BF16),
        ],
        compiler_params=params(),
        cost_estimate=cost(4e8, 4 << 20),
        name="pack_sums",
    )(answer, table, states, ids, before, w2, w1a, w1b)


def combine_kernel(feat, scale_relations, scale_weights, in_ref, out_ref):
    total = jnp.sum(in_ref[...].astype(F32), axis=0)
    lane = iota(total.shape, 1)
    total = total * jnp.where(lane < feat, scale_relations, scale_weights)
    out_ref[...] = jnp.broadcast_to(total.astype(BF16)[None], out_ref.shape)


def combine(chunks, feat, scale_relations, scale_weights):
    return pl.pallas_call(
        functools.partial(combine_kernel, feat, scale_relations, scale_weights),
        in_specs=[VMEM],
        out_specs=VMEM,
        out_shape=jax.ShapeDtypeStruct(chunks.shape, BF16),
        compiler_params=params(),
        cost_estimate=cost(1e6, 1 << 20),
        name="combine",
    )(chunks)


def unpack_kernel(feat, in_ref, relation_ref, w_in_ref, w_bias_ref, w_out_ref):
    groups = relation_ref.shape[0]
    relation_ref[...] = in_ref[0:groups, 0:feat].astype(F32)
    for layer in range(2):
        at = 2 * layer * GAP
        left = in_ref[at:at + GAP, feat:feat + TILE].astype(F32)
        right = in_ref[at + GAP:at + 2 * GAP, feat:feat + TILE].astype(F32)
        both = jnp.concatenate([left, right], axis=1)
        w_in_ref[layer] = both[0:2 * DIM]
        w_out_ref[layer] = both[2 * DIM:3 * DIM]
        w_bias_ref[layer:layer + 1, :] = both[3 * DIM:3 * DIM + 1]


def unpack(gathered, groups, feat):
    return pl.pallas_call(
        functools.partial(unpack_kernel, feat),
        in_specs=[VMEM],
        out_specs=[VMEM] * 4,
        out_shape=[
            jax.ShapeDtypeStruct((groups, feat), F32),
            jax.ShapeDtypeStruct((2, 2 * DIM, WIDE), F32),
            jax.ShapeDtypeStruct((2, WIDE), F32),
            jax.ShapeDtypeStruct((2, DIM, WIDE), F32),
        ],
        compiler_params=params(),
        cost_estimate=cost(1e6, 2 << 20),
        name="unpack",
    )(gathered)


def final_kernel(tiles_ref, count_ref, quarter_ref, next_ref, live_ref, c0, c1, c2, c3, out_ref):
    tile = 2 * quarter_ref[0] + pl.program_id(0)
    value = next_ref[...]
    for k in range(2):
        rows = slice(k * TILE, (k + 1) * TILE)
        is_live = (tile == tiles_ref[1, k]) & (count_ref[0, 1] > k)
        value = jnp.where(is_live, live_ref[rows, :], value)
    for k in range(2):
        rows = slice(k * TILE, (k + 1) * TILE)
        is_live = (tile == tiles_ref[0, k]) & (count_ref[0, 0] > k)
        source = (c0[rows, :].astype(F32) + c1[rows, :].astype(F32)) + (
            c2[rows, :].astype(F32) + c3[rows, :].astype(F32)
        )
        value = jnp.where(is_live, value + source, value)
    out_ref[...] = value.astype(BF16)


def final_pass(tiles, count, quarter_id, after, live, parts, quarter):
    feat = after.shape[1]
    blocks = quarter // TILE
    return pl.pallas_call(
        final_kernel,
        grid_spec=pltpu.PrefetchScalarGridSpec(
            num_scalar_prefetch=3,
            grid=(blocks,),
            in_specs=[pl.BlockSpec((TILE, feat), lambda i, t, c, q: (q[0] * blocks + i, 0)), whole(live.shape)]
            + [whole(parts[0].shape)] * 4,
            out_specs=pl.BlockSpec((TILE, feat), lambda i, *_: (i, 0)),
        ),
        out_shape=jax.ShapeDtypeStruct((quarter, feat), BF16),
        compiler_params=params(),
        cost_estimate=cost(1e6, 1 << 20),
        name="final",
    )(in_hbm(tiles), in_hbm(count), quarter_id, after, live, *parts)


def shards(state_zero, state_one, aggregate_one, aggregate_two, cotangent, relation_table, update_in, update_bias,
           update_out, frontier_tiles, frontier_count, edge_source, edge_relation, edge_target, edge_owner):
    block_rows, feat = state_zero.shape
    groups = relation_table.shape[0]
    group_size = lax.axis_size("rel")
    peers = lax.axis_size("ent")
    quarter = block_rows // group_size
    edges = edge_source.shape[0]
    capacity = 3 * edges // (2 * peers)
    regular = 2 * capacity // 3
    over = capacity - regular
    slots = peers * regular
    sum_rows = 8 * peers

    def exchange(chunks):
        return lax.all_to_all(chunks, "ent", split_axis=0, concat_axis=0, tiled=True)

    def over_rel(part):
        turned = [
            lax.ppermute(part, "rel", [(i, (i + k) % group_size) for i in range(group_size)])
            for k in range(1, group_size)
        ]
        return [part] + turned

    row = lambda values: values.reshape(1, edges)
    count = jnp.swapaxes(frontier_count, 0, 1)
    weights = (update_in, update_bias, jnp.swapaxes(update_out, 1, 2))
    request, ids = pl.pallas_call(
        functools.partial(slots_kernel, peers),
        in_specs=[HBM] * 6,
        out_specs=[VMEM] * 2,
        out_shape=[
            jax.ShapeDtypeStruct((peers, 1, 128), F32),
            jax.ShapeDtypeStruct((2, peers, 128), F32),
        ],
        scratch_shapes=[pltpu.VMEM(frontier_tiles.shape, jnp.int32), pltpu.VMEM(count.shape, jnp.int32)]
        + [pltpu.VMEM((1, edges), jnp.int32)] * 4
        + [pltpu.SemaphoreType.DMA((6,))],
        compiler_params=params(8 << 20),
        cost_estimate=cost(1e8, 1 << 20),
        name="slots",
    )(in_hbm(frontier_tiles), in_hbm(count), *(in_hbm(row(values)) for values in (edge_owner, edge_target, edge_source, edge_relation)))
    asked = exchange(request)

    upstream_one, grad_agg, grad_kept, sums_two = first_pass(aggregate_two, state_one, cotangent, *weights)
    picked_two, more_two, more_any = pick(regular, 0, 0, asked, grad_agg)
    more_two, more_any = lax.optimization_barrier((more_two[0], more_any[0]))
    more_two, more_any = more_two > 0, more_any > 0
    answered_two = exchange(picked_two.reshape(peers, regular, feat)).reshape(slots, feat)
    after, rest, sums_rest, live, grad_rest = rest_pass(
        regular, frontier_tiles, count, aggregate_one, state_zero, upstream_one, *weights, asked
    )
    edge_table, rows = tables_two(regular, frontier_tiles, count, ids, relation_table)
    answered_two, rest, edge_table, rows, more_two, more_any = lax.optimization_barrier(
        (answered_two, rest, edge_table, rows, more_two, more_any)
    )

    def over_two(part):
        picked = pick(over, regular, 0, asked, in_hbm(grad_kept))[0]
        answer = exchange(picked.reshape(peers, over, feat)).reshape(peers * over, feat)
        return extra(
            1, over, regular, frontier_tiles, count, in_hbm(ids), in_hbm(relation_table), answer, in_hbm(state_one), part
        )

    part = contribution(answered_two, edge_table, rows)
    part = lax.cond(more_two, lambda part: over_two(part)[0], lambda part: part, part)
    parts = over_rel(part)
    table_one, states_one, relation_two = tables_one(
        regular, frontier_tiles, count, ids, rows, relation_table, answered_two, state_one, state_zero
    )
    parts[0], rest, table_one, states_one, relation_two = lax.optimization_barrier(
        (parts[0], rest, table_one, states_one, relation_two)
    )
    picked_one, after_live, sums_live, grad_live = live_pass(
        frontier_tiles, count, aggregate_one, state_zero, upstream_one, parts, weights, live, rest
    )
    answered_one = exchange(picked_one.reshape(peers, regular, feat)).reshape(slots, feat)
    answered_one, more_any = lax.optimization_barrier((answered_one, more_any))
    part, packed = pack_sums(
        answered_one, table_one, states_one, rows, relation_two, sums_two, sums_rest, sums_live, sum_rows
    )

    def over_any(part, packed):
        first = over_two(part)[1]
        picked = late_pick(over, regular, frontier_tiles, count, asked, in_hbm(grad_rest), in_hbm(grad_live))
        answer = exchange(picked.reshape(peers, over, feat)).reshape(peers * over, feat)
        part, second = extra(
            0, over, regular, frontier_tiles, count, in_hbm(ids), in_hbm(relation_table), answer, in_hbm(state_zero), part
        )
        used = first.shape[0]
        total = packed[:used, :feat].astype(F32) + (first + second)
        return part, packed.at[:used, :feat].set(total.astype(BF16))

    part, packed = lax.cond(more_any, over_any, lambda part, packed: (part, packed), part, packed)
    parts = over_rel(part)
    scale_weights = 1.0 / math.sqrt(block_rows * peers * QUERIES)
    scale_relations = math.sqrt(groups * group_size / (edges * peers * group_size))
    chunks = exchange(packed.reshape(peers, 8, feat + TILE))
    gathered = exchange(combine(chunks, feat, scale_relations, scale_weights)).reshape(sum_rows, feat + TILE)
    quarter_id = lax.axis_index("rel").astype(jnp.int32).reshape(1)
    grad_zero = final_pass(frontier_tiles, count, quarter_id, after, after_live, parts, quarter)
    relation, grad_in, grad_bias, grad_out = unpack(gathered, groups, feat)
    return grad_zero, relation, grad_in, grad_bias, jnp.swapaxes(grad_out, 1, 2)


def solution(mesh):
    in_specs = (
        P("ent", None),
        P("ent", None),
        P("ent", None),
        P("ent", None),
        P("ent", None),
        P("rel", None),
        P(),
        P(),
        P(),
        P(None, "ent"),
        P(None, "ent"),
        P(("ent", "rel")),
        P(("ent", "rel")),
        P(("ent", "rel")),
        P(("ent", "rel"), None),
    )
    out_specs = (P(("ent", "rel"), None), P("rel", None), P(), P(), P())
    return jax.shard_map(shards, mesh=mesh, in_specs=in_specs, out_specs=out_specs, check_vma=False)
```

```python
import functools
import math

import jax
import jax.numpy as jnp
from jax import lax
from jax.experimental import pallas as pl
from jax.experimental.pallas import tpu as pltpu
from jax.sharding import PartitionSpec as P

QUERIES = 8
DIM = 32
TILE = 128
WIDE = 256
HALF_Q = 4
F32 = jnp.float32
BF16 = jnp.bfloat16
VMEM = pl.BlockSpec(memory_space=pltpu.VMEM)
SMEM = pl.BlockSpec(memory_space=pltpu.SMEM)
HBM = pl.BlockSpec(memory_space=pltpu.HBM)


def in_hbm(array):
    return pltpu.with_memory_space_constraint(array, pltpu.HBM)


def iota(shape, dim):
    return lax.broadcasted_iota(jnp.int32, shape, dim)


def dot_nn(a, b):
    return lax.dot_general(a, b, (((1,), (0,)), ((), ())), preferred_element_type=F32)


def dot_nt(a, b):
    return lax.dot_general(a, b, (((1,), (1,)), ((), ())), preferred_element_type=F32)


def dot_tn(a, b):
    return lax.dot_general(a, b, (((0,), (0,)), ((), ())), preferred_element_type=F32)


def params(vmem=20 << 20):
    return pltpu.CompilerParams(vmem_limit_bytes=vmem)


def cost(flops, nbytes, trans=0):
    return pl.CostEstimate(flops=int(flops), bytes_accessed=int(nbytes), transcendentals=int(trans))


def slots_kernel(peers, tiles_hbm, count_hbm, owner_hbm, target_hbm, source_hbm, relation_hbm, request_ref, ids_ref,
                 tiles_ref, count_ref, owner_ref, target_ref, source_ref, relation_ref, sems):
    pairs = (
        (owner_hbm, owner_ref), (source_hbm, source_ref), (tiles_hbm, tiles_ref), (count_hbm, count_ref),
        (target_hbm, target_ref), (relation_hbm, relation_ref),
    )
    copies = [pltpu.make_async_copy(a, b, sems.at[i]) for i, (a, b) in enumerate(pairs)]
    for copy in copies:
        copy.start()
    for copy in copies:
        copy.wait()
    edges = owner_ref.shape[1]
    hit = (iota((peers, edges), 0) == owner_ref[...]).astype(F32)
    below = (iota((TILE, TILE), 0) < iota((TILE, TILE), 1)).astype(BF16)
    tile = lax.shift_right_logical(source_ref[...], 7)
    request, tops = [], []
    for hop in (1, 0):
        first, second = tiles_ref[hop:hop + 1, 0:1], tiles_ref[hop:hop + 1, 1:2]
        live = (tile == first) | ((tile == second) & (count_ref[0:1, hop:hop + 1] > 1))
        own = jnp.where(live, hit, 0.0)
        own_low = own.astype(BF16)
        offset = jnp.zeros((peers, 1), F32)
        pieces = []
        for b in range(edges // TILE):
            block = slice(b * TILE, (b + 1) * TILE)
            pieces.append(dot_nn(own_low[:, block], below) + offset)
            offset = offset + jnp.sum(own[:, block], axis=1, keepdims=True)
        earlier = jnp.sum(jnp.concatenate(pieces, axis=1) * own, axis=0, keepdims=True).astype(jnp.int32)
        place = jnp.where((iota((32, edges), 0) == earlier) & live, 1.0, 0.0)

        def spread(values):
            high = lax.shift_right_logical(values, 5)
            low = values & 31
            return [place * high.astype(F32), place * low.astype(F32)]

        request += spread(target_ref[...])
        tops.append(jnp.max(offset, axis=0, keepdims=True))
        second = jnp.concatenate(
            spread(source_ref[...] + 1) + spread(relation_ref[...] + 1), axis=0
        ).astype(BF16)
        ids_ref[hop] = dot_nt(own_low, second)
    lane = iota((peers, 128), 1)
    sent = dot_nt(hit.astype(BF16), jnp.concatenate(request, axis=0).astype(BF16))
    sent = jnp.where(lane == 31, tops[0], sent)
    request_ref[:, 0, :] = jnp.where(lane == 95, tops[1], sent)


def slot_columns(table, capacity, bases, skip=0):
    peers = table.shape[0]
    slots = peers * capacity
    row = iota((slots, peers), 0)
    start = iota((slots, peers), 1) * capacity
    expand = ((row >= start) & (row < start + capacity)).astype(BF16)
    spread = dot_nn(expand, table.astype(BF16))
    row = iota((slots, 128), 0)
    group = ((row.astype(F32) + 0.5) * (1.0 / capacity)).astype(jnp.int32)
    place = row - group * capacity + skip
    lane = iota((slots, 128), 1)
    columns = []
    for base in bases:
        weight = jnp.where(lane == place + base, 32.0, 0.0) + jnp.where(
            lane == place + (base + 32), 1.0, 0.0
        )
        columns.append(dot_nn((spread * weight).astype(BF16), jnp.ones((128, 128), BF16)).astype(jnp.int32))
    return columns


def compact_column(column, tiles, count):
    tile = lax.shift_right_arithmetic(column, 7)
    inner = column & 127
    result = jnp.full(column.shape, -1, jnp.int32)
    for k in range(len(tiles)):
        live = (tile == tiles[k]) & (count > k)
        result = jnp.where(live, inner + k * TILE, result)
    return result


def onehot(column, width):
    column = column.astype(jnp.int16)
    lane = lax.broadcasted_iota(jnp.int16, column.shape, 1)
    one, zero = jnp.ones((), BF16), jnp.zeros((), BF16)
    parts = [jnp.where(lane == column - t, one, zero) for t in range(0, width, TILE)]
    return jnp.concatenate(parts, axis=1)


def build_weights(layer, w_in_ref, w_bias_ref, w_out_ref, wx_ref, wu_ref, wb_ref):
    wx_ref[...] = jnp.zeros_like(wx_ref)
    wu_ref[...] = jnp.zeros_like(wu_ref)
    for q in range(HALF_Q):
        rows, cols = slice(q * DIM, (q + 1) * DIM), slice(q * WIDE, (q + 1) * WIDE)
        low = slice(TILE + q * DIM, TILE + (q + 1) * DIM)
        wx_ref[rows, cols] = 0.5 * w_in_ref[layer, 0:DIM, :]
        wx_ref[low, cols] = 0.5 * w_in_ref[layer, DIM:2 * DIM, :]
        wu_ref[rows, cols] = w_out_ref[layer]
        wb_ref[:, cols] = 0.5 * w_bias_ref[layer:layer + 1, :]


def mlp_half(s, agg, state, up_low, wx, wu, bias, acc_in, acc_out):
    lanes = slice(s * TILE, (s + 1) * TILE)
    x = jnp.concatenate([agg[:, lanes], state[:, lanes]], axis=1)
    up = up_low[:, lanes]
    x_turned, up_turned = x.T, up.T
    half = dot_nn(x, wx[...]) + bias[...]
    bend = jnp.tanh(half)
    above = 1.0 + bend
    act_low = (half * above).astype(BF16)
    slope = above * (1.0 + half * (1.0 - bend))
    low = (dot_nn(up, wu[...]) * slope).astype(BF16)
    ones = jnp.ones((16, x.shape[0]), BF16)
    for q in range(HALF_Q):
        cols = slice(q * WIDE, (q + 1) * WIDE)
        rows = slice(q * DIM, (q + 1) * DIM)
        low_rows = slice(TILE + q * DIM, TILE + (q + 1) * DIM)
        own = jnp.concatenate([x_turned[rows], x_turned[low_rows], ones], axis=0)
        acc_in[...] += dot_nn(own, low[:, cols])
        acc_out[...] += dot_nn(up_turned[rows], act_low[:, cols])
    return dot_nt(low, wx[...])


def store_sums(acc_in, acc_out, sums_ref):
    sums_ref[0:2 * DIM, :] = 0.5 * acc_in[0:2 * DIM, :]
    sums_ref[2 * DIM:3 * DIM, :] = acc_out[...]
    sums_ref[3 * DIM:3 * DIM + 8, :] = 0.5 * acc_in[2 * DIM:2 * DIM + 8, :]


def clear(acc_in, acc_out):
    acc_in[...] = jnp.zeros_like(acc_in)
    acc_out[...] = jnp.zeros_like(acc_out)


WEIGHT_SHAPES = [
    ((2 * TILE, HALF_Q * WIDE), BF16),
    ((TILE, HALF_Q * WIDE), BF16),
    ((1, HALF_Q * WIDE), F32),
]
SUM_SHAPES = [((2 * DIM + 16, WIDE), F32), ((DIM, WIDE), F32)]
SUM_ROWS = 3 * DIM + 8


def scratch(shapes):
    return [pltpu.VMEM(shape, dtype) for shape, dtype in shapes]


def whole(shape):
    return pl.BlockSpec(shape, lambda i, *_: (0,) * len(shape))


def pick_rows(asked, grad_agg, picked_ref, chunks=4):
    rows, slots = grad_agg.shape[0], asked.shape[0]
    step = slots // chunks
    for c in range(chunks):
        part = slice(c * step, (c + 1) * step)
        picked_ref[part, :] = dot_nn(onehot(asked[part], rows), grad_agg[...]).astype(BF16)


def dense_step(step, agg_ref, state_ref, up, up_low, wx, wu, wb, acc_in, acc_out, grad_agg, next_ref):
    rows = agg_ref.shape[0]
    aggs, states = [], []
    for s in range(2):
        grad_x = mlp_half(s, agg_ref[...], state_ref[...], up_low, wx, wu, wb, acc_in, acc_out)
        aggs.append(grad_x[:, :TILE])
        states.append(grad_x[:, TILE:])
    grad_agg[pl.ds(pl.multiple_of(step * rows, rows), rows), :] = jnp.concatenate(aggs, axis=1).astype(BF16)
    next_ref[...] = up + jnp.concatenate(states, axis=1)


def first_kernel(blocks, agg_hbm, state_hbm, up_hbm, w_in_ref, w_bias_ref, w_out_ref,
                 next_hbm, grad_agg, grad_hbm, sums_hbm, wx, wu, wb, acc_in, acc_out, sums_ref,
                 agg_buf, state_buf, up_buf, next_buf, sems, out_sems, sums_sem):
    rows = agg_hbm.shape[0] // blocks

    def copies(step):
        part = pl.ds(pl.multiple_of(step * rows, rows), rows)
        pairs = ((agg_hbm, agg_buf), (state_hbm, state_buf), (up_hbm, up_buf))
        return [pltpu.make_async_copy(a.at[part], b.at[part], sems.at[step, i]) for i, (a, b) in enumerate(pairs)]

    def results(step):
        part = pl.ds(pl.multiple_of(step * rows, rows), rows)
        pairs = ((next_buf, next_hbm), (grad_agg, grad_hbm))
        return [pltpu.make_async_copy(a.at[part], b.at[part], out_sems.at[step, i]) for i, (a, b) in enumerate(pairs)]

    for step in range(blocks):
        for copy in copies(step):
            copy.start()
    build_weights(1, w_in_ref, w_bias_ref, w_out_ref, wx, wu, wb)
    clear(acc_in, acc_out)

    @pl.loop(0, blocks)
    def _(step):
        for copy in copies(step):
            copy.wait()
        part = pl.ds(pl.multiple_of(step * rows, rows), rows)
        up_low = up_buf[part, :]
        dense_step(step, agg_buf.at[part], state_buf.at[part], up_low.astype(F32), up_low, wx, wu, wb,
                   acc_in, acc_out, grad_agg, next_buf.at[part])
        for copy in results(step):
            copy.start()

    store_sums(acc_in, acc_out, sums_ref)
    last = pltpu.make_async_copy(sums_ref, sums_hbm, sums_sem)
    last.start()
    for step in range(blocks):
        for copy in results(step):
            copy.wait()
    last.wait()


def first_pass(agg, state, up, w_in, w_bias, w_out):
    rows, feat = agg.shape
    blocks = rows // 512
    return pl.pallas_call(
        functools.partial(first_kernel, blocks),
        in_specs=[HBM, HBM, HBM, VMEM, VMEM, VMEM],
        out_specs=[HBM, VMEM, HBM, HBM],
        out_shape=[
            pltpu.HBM((rows, feat), F32),
            jax.ShapeDtypeStruct((rows, feat), BF16),
            pltpu.HBM((rows, feat), BF16),
            pltpu.HBM((SUM_ROWS, WIDE), F32),
        ],
        scratch_shapes=scratch(WEIGHT_SHAPES + SUM_SHAPES)
        + [pltpu.VMEM((SUM_ROWS, WIDE), F32)]
        + [pltpu.VMEM((rows, feat), BF16)] * 3
        + [pltpu.VMEM((rows, feat), F32), pltpu.SemaphoreType.DMA((blocks, 3))]
        + [pltpu.SemaphoreType.DMA((blocks, 2)), pltpu.SemaphoreType.DMA],
        compiler_params=params(),
        cost_estimate=cost(5.4e9, 4 << 20, 2 << 20),
        name="first",
    )(in_hbm(agg), in_hbm(state), in_hbm(up), w_in, w_bias, w_out)


def pick_kernel(capacity, skip, base, asked_ref, grad_agg, picked_ref, over_ref):
    two, one = jnp.max(asked_ref[:, 0, 31:32]), jnp.max(asked_ref[:, 0, 95:96])
    over_ref[0] = (two > capacity).astype(jnp.int32) + (jnp.maximum(two, one) > capacity).astype(jnp.int32)
    asked = slot_columns(asked_ref[:, 0, :], capacity, (base,), skip)[0]
    pick_rows(asked, grad_agg, picked_ref)


def pick(capacity, skip, base, asked, grad_agg):
    slots, feat = asked.shape[0] * capacity, grad_agg.shape[1]
    return pl.pallas_call(
        functools.partial(pick_kernel, capacity, skip, base),
        in_specs=[VMEM, VMEM],
        out_specs=[VMEM, SMEM],
        out_shape=[
            jax.ShapeDtypeStruct((slots, feat), BF16),
            jax.ShapeDtypeStruct((1,), jnp.int32),
        ],
        compiler_params=params(12 << 20),
        cost_estimate=cost(8e8, 1 << 20),
        name="pick",
    )(asked, grad_agg)


def rest_kernel(capacity, tiles_ref, count_ref, agg_ref, state_ref, up_ref, w_in_ref, w_bias_ref, w_out_ref,
                asked_ref, next_ref, picked_ref, sums_ref, live_ref, grad_agg, wx, wu, wb,
                acc_in, acc_out):
    step = pl.program_id(0)
    rows = agg_ref.shape[0]
    count = count_ref[0, 1]

    @pl.when(step == 0)
    def _():
        build_weights(0, w_in_ref, w_bias_ref, w_out_ref, wx, wu, wb)
        clear(acc_in, acc_out)

    up = up_ref[...]
    tile = lax.shift_right_logical(iota((rows, 1), 0) + step * rows, 7)
    dead = (tile == tiles_ref[1, 0]) | ((tile == tiles_ref[1, 1]) & (count > 1))
    up_low = jnp.where(dead, 0.0, up).astype(BF16)
    dense_step(step, agg_ref, state_ref, up, up_low, wx, wu, wb, acc_in, acc_out, grad_agg, next_ref)

    @pl.when(step == pl.num_programs(0) - 1)
    def _():
        store_sums(acc_in, acc_out, sums_ref)
        asked = slot_columns(asked_ref[:, 0, :], capacity, (64,))[0]
        live_ref[...] = onehot(compact_column(asked, (tiles_ref[1, 0], tiles_ref[1, 1]), count), 2 * TILE)
        pick_rows(asked, grad_agg, picked_ref)


def rest_pass(capacity, tiles, count, agg, state, up, w_in, w_bias, w_out, asked):
    rows, feat = agg.shape
    slots = asked.shape[0] * capacity
    block = 512
    row_spec = pl.BlockSpec((block, feat), lambda i: (i, 0))
    return pl.pallas_call(
        functools.partial(rest_kernel, capacity),
        grid=(rows // block,),
        in_specs=[SMEM, SMEM, row_spec, row_spec, row_spec, whole(w_in.shape), whole(w_bias.shape),
                  whole(w_out.shape), whole(asked.shape)],
        out_specs=[row_spec, whole((slots, feat)), whole((SUM_ROWS, WIDE)), whole((slots, 2 * TILE)),
                   whole((rows, feat))],
        out_shape=[
            pltpu.HBM((rows, feat), F32),
            pltpu.HBM((slots, feat), BF16),
            pltpu.HBM((SUM_ROWS, WIDE), F32),
            pltpu.HBM((slots, 2 * TILE), BF16),
            pltpu.HBM((rows, feat), BF16),
        ],
        scratch_shapes=scratch(WEIGHT_SHAPES + SUM_SHAPES),
        compiler_params=params(),
        cost_estimate=cost(5.4e9, 4 << 20, 2 << 20),
        name="rest",
    )(tiles, count, in_hbm(agg), in_hbm(state), in_hbm(up), w_in, w_bias, w_out, asked)


def as_row(column):
    return column.astype(F32).T[0:8].astype(jnp.int32)


def onehot_rows(row, width):
    return (iota((width, row.shape[1]), 0) == row).astype(F32).astype(BF16)


def relation_rows(relation, table_ref):
    width = -(-table_ref.shape[0] // TILE) * TILE
    pad = width - table_ref.shape[0]
    table = jnp.concatenate([table_ref[...], jnp.zeros((pad, table_ref.shape[1]), BF16)], axis=0)
    return dot_nn(onehot(relation, width), table).astype(BF16)


def tables_two_kernel(capacity, tiles_ref, count_ref, ids_ref, table_ref, t_ref, rows_ref):
    for hop in range(2):
        source, relation = slot_columns(ids_ref[hop], capacity, (0, 64))
        if hop == 1:
            t_ref[...] = relation_rows(relation - 1, table_ref)
        rows_ref[hop] = as_row(relation - 1)
        column = compact_column(source - 1, (tiles_ref[hop, 0], tiles_ref[hop, 1]), count_ref[0, hop])
        rows_ref[2 + hop] = as_row(column)


def tables_two(capacity, tiles, count, ids, table):
    feat = table.shape[1]
    slots = ids.shape[1] * capacity
    return pl.pallas_call(
        functools.partial(tables_two_kernel, capacity),
        in_specs=[SMEM, SMEM, VMEM, VMEM],
        out_specs=[VMEM, VMEM],
        out_shape=[
            jax.ShapeDtypeStruct((slots, feat), BF16),
            jax.ShapeDtypeStruct((4, 8, slots), jnp.int32),
        ],
        compiler_params=params(),
        cost_estimate=cost(1e9, 2 << 20),
        name="tables_two",
    )(tiles, count, ids, table)


def tables_one_kernel(capacity, tiles_ref, count_ref, ids_ref, rows_ref, table_ref, answer_ref,
                      one_a, one_b, zero_a, zero_b, t_ref, h_ref, total_ref):
    states = []
    for hop, a, b in ((0, zero_a, zero_b), (1, one_a, one_b)):
        source, relation = slot_columns(ids_ref[hop], capacity, (0, 64))
        column = compact_column(source - 1, (tiles_ref[hop, 0], tiles_ref[hop, 1]), count_ref[0, hop])
        states.append(dot_nn(onehot(column, 2 * TILE), jnp.concatenate([a[...], b[...]], axis=0)).astype(BF16))
        if hop == 0:
            t_ref[...] = relation_rows(relation - 1, table_ref)
    h_ref[...] = states[0]
    total_ref[...] = dot_nn(onehot_rows(rows_ref[1, 0:1, :], total_ref.shape[0]), answer_ref[...] * states[1])


def tables_one(capacity, tiles, count, ids, rows, table, answer, state_one, state_zero):
    slots, feat = answer.shape
    width = -(-table.shape[0] // TILE) * TILE

    def tile(hop, k):
        return pl.BlockSpec((TILE, feat), lambda i, tiles, count: (tiles[hop, k], 0))

    return pl.pallas_call(
        functools.partial(tables_one_kernel, capacity),
        grid_spec=pltpu.PrefetchScalarGridSpec(
            num_scalar_prefetch=2,
            grid=(1,),
            in_specs=[whole(ids.shape), whole(rows.shape), whole(table.shape), whole(answer.shape), tile(1, 0),
                      tile(1, 1), tile(0, 0), tile(0, 1)],
            out_specs=[whole((slots, feat)), whole((slots, feat)), whole((width, feat))],
        ),
        out_shape=[
            jax.ShapeDtypeStruct((slots, feat), BF16),
            jax.ShapeDtypeStruct((slots, feat), BF16),
            jax.ShapeDtypeStruct((width, feat), F32),
        ],
        compiler_params=params(),
        cost_estimate=cost(2e9, 4 << 20),
        name="tables_one",
    )(tiles, count, ids, rows, table, answer, state_one, state_one, state_zero, state_zero)


def extra_kernel(hop, capacity, skip, tiles_ref, count_ref, ids_ref, table_ref, answer_ref, state_a, state_b,
                 part_ref, out_ref, total_ref):
    source, relation = slot_columns(ids_ref[hop], capacity, (0, 64), skip)
    column = compact_column(source - 1, (tiles_ref[hop, 0], tiles_ref[hop, 1]), count_ref[0, hop])
    select = onehot(column, 2 * TILE)
    answer = answer_ref[...]
    more = dot_nn(onehot_rows(as_row(column)[0:1], 2 * TILE), answer * relation_rows(relation - 1, table_ref))
    out_ref[...] = (part_ref[...].astype(F32) + more).astype(BF16)
    states = dot_nn(select, jnp.concatenate([state_a[...], state_b[...]], axis=0)).astype(BF16)
    total_ref[...] = dot_nn(onehot_rows(as_row(relation - 1)[0:1], total_ref.shape[0]), answer * states)


def extra(hop, capacity, skip, tiles, count, ids, table, answer, state, part):
    feat = answer.shape[1]
    width = -(-table.shape[0] // TILE) * TILE

    def tile(k):
        return pl.BlockSpec((TILE, feat), lambda i, tiles, count: (tiles[hop, k], 0))

    return pl.pallas_call(
        functools.partial(extra_kernel, hop, capacity, skip),
        grid_spec=pltpu.PrefetchScalarGridSpec(
            num_scalar_prefetch=2,
            grid=(1,),
            in_specs=[whole(ids.shape), whole(table.shape), whole(answer.shape), tile(0), tile(1), whole(part.shape)],
            out_specs=[whole(part.shape), whole((width, feat))],
        ),
        out_shape=[jax.ShapeDtypeStruct(part.shape, BF16), jax.ShapeDtypeStruct((width, feat), F32)],
        compiler_params=params(),
        cost_estimate=cost(1e9, 2 << 20),
        name="extra",
    )(tiles, count, ids, table, answer, state, state, part)


def contribution_kernel(answer_ref, t_ref, rows_ref, out_ref):
    select = onehot_rows(rows_ref[3, 0:1, :], 2 * TILE)
    out_ref[...] = dot_nn(select, answer_ref[...] * t_ref[...]).astype(BF16)


def contribution(answer, table, rows):
    return pl.pallas_call(
        contribution_kernel,
        in_specs=[VMEM] * 3,
        out_specs=VMEM,
        out_shape=jax.ShapeDtypeStruct((2 * TILE, answer.shape[1]), BF16),
        compiler_params=params(8 << 20),
        cost_estimate=cost(2e8, 3 << 20),
        name="contribution",
    )(answer, table, rows)


def live_kernel(tiles_ref, count_ref, agg_a, agg_b, state_a, state_b, up_a, up_b, c0, c1, c2, c3,
                w_in_ref, w_bias_ref, w_out_ref, live_ref, rest_ref, picked_ref, next_ref, sums_ref, grad_ref,
                wx, wu, wb, acc_in, acc_out):
    build_weights(0, w_in_ref, w_bias_ref, w_out_ref, wx, wu, wb)
    clear(acc_in, acc_out)
    source = (c0[...].astype(F32) + c1[...].astype(F32)) + (c2[...].astype(F32) + c3[...].astype(F32))
    up = jnp.concatenate([up_a[...], up_b[...]], axis=0) + source
    keep = (iota((2 * TILE, 1), 0) < TILE) | (count_ref[0, 1] > 1)
    up_low = jnp.where(keep, up, 0.0).astype(BF16)
    agg = jnp.concatenate([agg_a[...], agg_b[...]], axis=0)
    state = jnp.concatenate([state_a[...], state_b[...]], axis=0)
    aggs, states = [], []
    for s in range(2):
        grad_x = mlp_half(s, agg, state, up_low, wx, wu, wb, acc_in, acc_out)
        aggs.append(grad_x[:, :TILE])
        states.append(grad_x[:, TILE:])
    grad_agg = jnp.concatenate(aggs, axis=1).astype(BF16)
    next_ref[...] = up + jnp.concatenate(states, axis=1)
    store_sums(acc_in, acc_out, sums_ref)
    grad_ref[...] = grad_agg
    picked_ref[...] = (dot_nn(live_ref[...], grad_agg) + rest_ref[...].astype(F32)).astype(BF16)


def live_pass(tiles, count, agg, state, up, parts, weights, live, rest):
    feat = agg.shape[1]

    def tile(k):
        return pl.BlockSpec((TILE, feat), lambda i, tiles, count: (tiles[1, k], 0))

    return pl.pallas_call(
        live_kernel,
        grid_spec=pltpu.PrefetchScalarGridSpec(
            num_scalar_prefetch=2,
            grid=(1,),
            in_specs=[tile(0), tile(1)] * 3 + [whole(parts[0].shape)] * 4
            + [whole(w.shape) for w in weights] + [whole(live.shape), whole(rest.shape)],
            out_specs=[whole(rest.shape), whole((2 * TILE, feat)), whole((SUM_ROWS, WIDE)), whole((2 * TILE, feat))],
            scratch_shapes=scratch(WEIGHT_SHAPES + SUM_SHAPES),
        ),
        out_shape=[
            jax.ShapeDtypeStruct(rest.shape, BF16),
            jax.ShapeDtypeStruct((2 * TILE, feat), F32),
            jax.ShapeDtypeStruct((SUM_ROWS, WIDE), F32),
            pltpu.HBM((2 * TILE, feat), BF16),
        ],
        compiler_params=params(),
        cost_estimate=cost(1.6e9, 4 << 20, 1 << 19),
        name="live",
    )(tiles, count, agg, agg, state, state, up, up, *parts, *weights, live, rest)


def late_kernel(capacity, skip, tiles_ref, count_ref, asked_ref, rest_ref, live_ref, picked_ref):
    asked = slot_columns(asked_ref[:, 0, :], capacity, (64,), skip)[0]
    column = compact_column(asked, (tiles_ref[1, 0], tiles_ref[1, 1]), count_ref[0, 1])
    rest = dot_nn(onehot(asked, rest_ref.shape[0]), rest_ref[...])
    picked_ref[...] = (dot_nn(onehot(column, 2 * TILE), live_ref[...]) + rest).astype(BF16)


def late_pick(capacity, skip, tiles, count, asked, rest, live):
    slots, feat = asked.shape[0] * capacity, rest.shape[1]
    return pl.pallas_call(
        functools.partial(late_kernel, capacity, skip),
        in_specs=[SMEM, SMEM, VMEM, VMEM, VMEM],
        out_specs=VMEM,
        out_shape=jax.ShapeDtypeStruct((slots, feat), BF16),
        compiler_params=params(),
        cost_estimate=cost(8e8, 1 << 20),
        name="late_pick",
    )(tiles, count, asked, rest, live)


GAP = SUM_ROWS


def pack_kernel(answer_ref, t_ref, h_ref, rows_ref, before_ref, w2_ref, w1a_ref, w1b_ref, part_ref, out_ref):
    answer = answer_ref[...]
    part_ref[...] = dot_nn(onehot_rows(rows_ref[2, 0:1, :], 2 * TILE), answer * t_ref[...]).astype(BF16)
    select = onehot_rows(rows_ref[0, 0:1, :], before_ref.shape[0])
    total = before_ref[...] + dot_nn(select, answer * h_ref[...])
    used, feat = total.shape
    out_ref[used:, 0:feat] = jnp.zeros((out_ref.shape[0] - used, feat), BF16)
    out_ref[4 * GAP:, feat:feat + TILE] = jnp.zeros((out_ref.shape[0] - 4 * GAP, TILE), BF16)
    out_ref[0:used, 0:feat] = total.astype(BF16)
    layers = (w1a_ref[...] + w1b_ref[...], w2_ref[...])
    parts = []
    for layer in layers:
        parts += [layer[:, :TILE], layer[:, TILE:]]
    out_ref[0:4 * GAP, feat:feat + TILE] = jnp.concatenate(parts, axis=0).astype(BF16)


def pack_sums(answer, table, states, ids, before, w2, w1a, w1b, rows):
    feat = answer.shape[1]
    return pl.pallas_call(
        pack_kernel,
        in_specs=[VMEM] * 8,
        out_specs=[VMEM, VMEM],
        out_shape=[
            jax.ShapeDtypeStruct((2 * TILE, feat), BF16),
            jax.ShapeDtypeStruct((rows, feat + TILE), BF16),
        ],
        compiler_params=params(),
        cost_estimate=cost(4e8, 4 << 20),
        name="pack_sums",
    )(answer, table, states, ids, before, w2, w1a, w1b)


def combine_kernel(feat, scale_relations, scale_weights, in_ref, out_ref):
    total = jnp.sum(in_ref[...].astype(F32), axis=0)
    lane = iota(total.shape, 1)
    total = total * jnp.where(lane < feat, scale_relations, scale_weights)
    out_ref[...] = jnp.broadcast_to(total.astype(BF16)[None], out_ref.shape)


def combine(chunks, feat, scale_relations, scale_weights):
    return pl.pallas_call(
        functools.partial(combine_kernel, feat, scale_relations, scale_weights),
        in_specs=[VMEM],
        out_specs=VMEM,
        out_shape=jax.ShapeDtypeStruct(chunks.shape, BF16),
        compiler_params=params(),
        cost_estimate=cost(1e6, 1 << 20),
        name="combine",
    )(chunks)


def unpack_kernel(feat, in_ref, relation_ref, w_in_ref, w_bias_ref, w_out_ref):
    groups = relation_ref.shape[0]
    relation_ref[...] = in_ref[0:groups, 0:feat].astype(F32)
    for layer in range(2):
        at = 2 * layer * GAP
        left = in_ref[at:at + GAP, feat:feat + TILE].astype(F32)
        right = in_ref[at + GAP:at + 2 * GAP, feat:feat + TILE].astype(F32)
        both = jnp.concatenate([left, right], axis=1)
        w_in_ref[layer] = both[0:2 * DIM]
        w_out_ref[layer] = both[2 * DIM:3 * DIM]
        w_bias_ref[layer:layer + 1, :] = both[3 * DIM:3 * DIM + 1]


def unpack(gathered, groups, feat):
    return pl.pallas_call(
        functools.partial(unpack_kernel, feat),
        in_specs=[VMEM],
        out_specs=[VMEM] * 4,
        out_shape=[
            jax.ShapeDtypeStruct((groups, feat), F32),
            jax.ShapeDtypeStruct((2, 2 * DIM, WIDE), F32),
            jax.ShapeDtypeStruct((2, WIDE), F32),
            jax.ShapeDtypeStruct((2, DIM, WIDE), F32),
        ],
        compiler_params=params(),
        cost_estimate=cost(1e6, 2 << 20),
        name="unpack",
    )(gathered)


def final_kernel(tiles_ref, count_ref, quarter_ref, next_ref, live_ref, c0, c1, c2, c3, out_ref):
    tile = 2 * quarter_ref[0] + pl.program_id(0)
    value = next_ref[...]
    for k in range(2):
        rows = slice(k * TILE, (k + 1) * TILE)
        is_live = (tile == tiles_ref[1, k]) & (count_ref[0, 1] > k)
        value = jnp.where(is_live, live_ref[rows, :], value)
    for k in range(2):
        rows = slice(k * TILE, (k + 1) * TILE)
        is_live = (tile == tiles_ref[0, k]) & (count_ref[0, 0] > k)
        source = (c0[rows, :].astype(F32) + c1[rows, :].astype(F32)) + (
            c2[rows, :].astype(F32) + c3[rows, :].astype(F32)
        )
        value = jnp.where(is_live, value + source, value)
    out_ref[...] = value.astype(BF16)


def final_pass(tiles, count, quarter_id, after, live, parts, quarter):
    feat = after.shape[1]
    blocks = quarter // TILE
    return pl.pallas_call(
        final_kernel,
        grid_spec=pltpu.PrefetchScalarGridSpec(
            num_scalar_prefetch=3,
            grid=(blocks,),
            in_specs=[pl.BlockSpec((TILE, feat), lambda i, t, c, q: (q[0] * blocks + i, 0)), whole(live.shape)]
            + [whole(parts[0].shape)] * 4,
            out_specs=pl.BlockSpec((TILE, feat), lambda i, *_: (i, 0)),
        ),
        out_shape=jax.ShapeDtypeStruct((quarter, feat), BF16),
        compiler_params=params(),
        cost_estimate=cost(1e6, 1 << 20),
        name="final",
    )(tiles, count, quarter_id, after, live, *parts)


def shards(state_zero, state_one, aggregate_one, aggregate_two, cotangent, relation_table, update_in, update_bias,
           update_out, frontier_tiles, frontier_count, edge_source, edge_relation, edge_target, edge_owner):
    block_rows, feat = state_zero.shape
    groups = relation_table.shape[0]
    group_size = lax.axis_size("rel")
    peers = lax.axis_size("ent")
    quarter = block_rows // group_size
    edges = edge_source.shape[0]
    capacity = 3 * edges // (2 * peers)
    regular = 2 * capacity // 3
    over = capacity - regular
    slots = peers * regular
    sum_rows = 8 * peers

    def exchange(chunks):
        return lax.all_to_all(chunks, "ent", split_axis=0, concat_axis=0, tiled=True)

    def over_rel(part):
        turned = [
            lax.ppermute(part, "rel", [(i, (i + k) % group_size) for i in range(group_size)])
            for k in range(1, group_size)
        ]
        return [part] + turned

    row = lambda values: values.reshape(1, edges)
    count = jnp.swapaxes(frontier_count, 0, 1)
    weights = (update_in, update_bias, jnp.swapaxes(update_out, 1, 2))
    request, ids = pl.pallas_call(
        functools.partial(slots_kernel, peers),
        in_specs=[HBM] * 6,
        out_specs=[VMEM] * 2,
        out_shape=[
            jax.ShapeDtypeStruct((peers, 1, 128), F32),
            jax.ShapeDtypeStruct((2, peers, 128), F32),
        ],
        scratch_shapes=[pltpu.VMEM(frontier_tiles.shape, jnp.int32), pltpu.VMEM(count.shape, jnp.int32)]
        + [pltpu.VMEM((1, edges), jnp.int32)] * 4
        + [pltpu.SemaphoreType.DMA((6,))],
        compiler_params=params(8 << 20),
        cost_estimate=cost(1e8, 1 << 20),
        name="slots",
    )(in_hbm(frontier_tiles), in_hbm(count), *(in_hbm(row(values)) for values in (edge_owner, edge_target, edge_source, edge_relation)))
    asked = exchange(request)

    upstream_one, grad_agg, grad_kept, sums_two = first_pass(aggregate_two, state_one, cotangent, *weights)
    picked_two, code = pick(regular, 0, 0, asked, grad_agg)
    code = lax.optimization_barrier(lax.optimization_barrier(code[0]) + 1)
    more_two, more_any = code > 2, code > 1
    answered_two = exchange(picked_two.reshape(peers, regular, feat)).reshape(slots, feat)
    after, rest, sums_rest, live, grad_rest = rest_pass(
        regular, frontier_tiles, count, aggregate_one, state_zero, upstream_one, *weights, asked
    )
    edge_table, rows = tables_two(regular, frontier_tiles, count, ids, relation_table)
    answered_two, rest, edge_table, rows, more_two, more_any = lax.optimization_barrier(
        (answered_two, rest, edge_table, rows, more_two, more_any)
    )

    def over_two(part):
        picked = pick(over, regular, 0, asked, in_hbm(grad_kept))[0]
        answer = exchange(picked.reshape(peers, over, feat)).reshape(peers * over, feat)
        return extra(
            1, over, regular, frontier_tiles, count, in_hbm(ids), in_hbm(relation_table), answer, in_hbm(state_one), part
        )

    part = contribution(answered_two, edge_table, rows)
    part = lax.cond(more_two, lambda part: over_two(part)[0], lambda part: part, part)
    parts = over_rel(part)
    table_one, states_one, relation_two = tables_one(
        regular, frontier_tiles, count, ids, rows, relation_table, answered_two, state_one, state_zero
    )
    parts[0], rest, table_one, states_one, relation_two = lax.optimization_barrier(
        (parts[0], rest, table_one, states_one, relation_two)
    )
    picked_one, after_live, sums_live, grad_live = live_pass(
        frontier_tiles, count, aggregate_one, state_zero, upstream_one, parts, weights, live, rest
    )
    answered_one = exchange(picked_one.reshape(peers, regular, feat)).reshape(slots, feat)
    answered_one, more_any = lax.optimization_barrier((answered_one, more_any))
    part, packed = pack_sums(
        answered_one, table_one, states_one, rows, relation_two, sums_two, sums_rest, sums_live, sum_rows
    )

    def over_any(part, packed):
        first = over_two(part)[1]
        picked = late_pick(over, regular, frontier_tiles, count, asked, in_hbm(grad_rest), in_hbm(grad_live))
        answer = exchange(picked.reshape(peers, over, feat)).reshape(peers * over, feat)
        part, second = extra(
            0, over, regular, frontier_tiles, count, in_hbm(ids), in_hbm(relation_table), answer, in_hbm(state_zero), part
        )
        used = first.shape[0]
        total = packed[:used, :feat].astype(F32) + (first + second)
        return part, packed.at[:used, :feat].set(total.astype(BF16))

    part, packed = lax.cond(more_any, over_any, lambda part, packed: (part, packed), part, packed)
    parts = over_rel(part)
    scale_weights = 1.0 / math.sqrt(block_rows * peers * QUERIES)
    scale_relations = math.sqrt(groups * group_size / (edges * peers * group_size))
    chunks = exchange(packed.reshape(peers, 8, feat + TILE))
    gathered = exchange(combine(chunks, feat, scale_relations, scale_weights)).reshape(sum_rows, feat + TILE)
    quarter_id = lax.axis_index("rel").astype(jnp.int32).reshape(1)
    grad_zero = final_pass(frontier_tiles, count, quarter_id, after, after_live, parts, quarter)
    relation, grad_in, grad_bias, grad_out = unpack(gathered, groups, feat)
    return grad_zero, relation, grad_in, grad_bias, jnp.swapaxes(grad_out, 1, 2)


def solution(mesh):
    in_specs = (
        P("ent", None),
        P("ent", None),
        P("ent", None),
        P("ent", None),
        P("ent", None),
        P("rel", None),
        P(),
        P(),
        P(),
        P(None, "ent"),
        P(None, "ent"),
        P(("ent", "rel")),
        P(("ent", "rel")),
        P(("ent", "rel")),
        P(("ent", "rel"), None),
    )
    out_specs = (P(("ent", "rel"), None), P("rel", None), P(), P(), P())
    return jax.shard_map(shards, mesh=mesh, in_specs=in_specs, out_specs=out_specs, check_vma=False)
```
